32 devices in a mesh: dp: 8 (over z, y), tensor: 4 (over x, core).
Axes of the slice: x: 2, y: 2, z: 4, core: 2. Of those that a mesh axis runs over, the one named last changes fastest.
Arguments:
- tokens: bfloat16 [8192, 1024], P('dp', 'tensor'), may hold values from -6 to 6
- dealing: int32 [8192], P('dp'), may hold values from 0 to 8191, as said below
- seq_ids: int32 [8192], P('dp'), may hold values from 0 to 8191, as said below
- first_values: bfloat16 [8192, 1024], P('dp', 'tensor'), may hold values from -6 to 6
- out_grad: bfloat16 [8192, 1024], P('dp', 'tensor'), may hold values from -6 to 6
- norm1_gain: bfloat16 [1024], replicated, may hold values from 0.5 to 1.5
- norm2_gain: bfloat16 [1024], replicated, may hold values from 0.5 to 1.5
- w_query: bfloat16 [1024, 1024], P(None, 'tensor'), may hold values from -0.1875 to 0.1875
- w_key: bfloat16 [1024, 1024], P(None, 'tensor'), may hold values from -0.1875 to 0.1875
- w_value: bfloat16 [1024, 1024], P(None, 'tensor'), may hold values from -0.1875 to 0.1875
- w_out: bfloat16 [1024, 1024], P('tensor'), may hold values from -1 to 1
- w_gate: bfloat16 [1024, 2816], P(None, 'tensor'), may hold values from -0.1875 to 0.1875
- w_up: bfloat16 [1024, 2816], P(None, 'tensor'), may hold values from -0.1875 to 0.1875
- w_down: bfloat16 [2816, 1024], P('tensor'), may hold values from -0.109375 to 0.109375
Outputs:
- output: bfloat16 [8192, 1024], P('dp', 'tensor')
- input_grad: bfloat16 [8192, 1024], P('dp', 'tensor')
- first_values_grad: bfloat16 [8192, 1024], P('dp', 'tensor')
- norm1_gain_grad: float32 [4, 256], P('tensor', 'dp')
- norm2_gain_grad: float32 [4, 256], P('tensor', 'dp')
- w_query_grad: float32 [1024, 1024], P('dp', 'tensor')
- w_key_grad: float32 [1024, 1024], P('dp', 'tensor')
- w_value_grad: float32 [1024, 1024], P('dp', 'tensor')
- w_out_grad: float32 [1024, 1024], P('tensor', 'dp')
- w_gate_grad: float32 [1024, 2816], P('dp', 'tensor')
- w_up_grad: float32 [1024, 2816], P('dp', 'tensor')
- w_down_grad: float32 [2816, 1024], P('tensor', 'dp')
The draws below stay inside these ranges and needn't reach their ends.
Inputs may be any that keep to these rules, and one draw needn't show every extreme that they name: `dealing`: a permutation; the tokens of each dp index go evenly, 1024 / 8 of them, to the rows of each dp index's block of 1024 dealt rows. `seq_ids`: never fall; no sequence crosses a multiple of 1024 rows; in every draw some block of 1024 rows is a single sequence; the rows of block b carry ids from b * 1024 to b * 1024 + 1023.
All inputs are finite; a program needn't handle non-finite values.
Results may differ from the reference program's by a relative error of at most 0.013.
Values may be sent and summed in bfloat16 or wider, within the bound.
No kernel may reach another device: no remote copies, remote signals or barrier semaphores. Data moves between devices by JAX's collectives and lax.ppermute only.
A program may use at most 128 MiB of HBM per device.

```python
import jax
import jax.numpy as jnp
from jax import lax

D = 1024
HEADS = 16
HEAD_DIM = 64
FF = 2816
TOK_DEV = 1024
TOKENS = 8192
N_DP = 8
N_TENSOR = 4


def draw_dealing(key, part):
    folded = jax.random.fold_in(key, 11)
    key_rank, key_tie = jax.random.split(folded)
    per_pair = TOK_DEV // N_DP
    rank_keys = jax.random.split(key_rank, N_DP)
    slot_rank = jax.vmap(lambda single: jax.random.permutation(single, TOK_DEV))(rank_keys)
    source = (slot_rank // per_pair).reshape(TOKENS).astype(jnp.int32)
    tiebreak = jax.random.permutation(key_tie, TOKENS).astype(jnp.int32)
    scores = source * TOKENS + tiebreak
    return jnp.argsort(scores).astype(jnp.int32)


def draw_seq_ids(key, part):
    folded = jax.random.fold_in(key, 23)
    key_flags, key_whole = jax.random.split(folded)
    upper = max(TOK_DEV // 4, 2)
    flags = (jax.random.randint(key_flags, (N_DP, TOK_DEV), 0, upper) == 0).astype(jnp.int32)
    whole = jax.random.randint(key_whole, (), 0, N_DP)
    rows = jnp.arange(N_DP, dtype=jnp.int32)[:, None]
    cols = jnp.arange(TOK_DEV, dtype=jnp.int32)[None, :]
    flags = jnp.where((rows == whole) | (cols == 0), 0, flags)
    idents = rows * TOK_DEV + jnp.cumsum(flags, axis=1)
    return idents.reshape(TOKENS).astype(jnp.int32)


def steps_of(rng, dims, pieces, least, high):
    loudness, own = 1.0, jax.random.fold_in(rng, 6)
    for dim, shards_of in pieces:
        heights = jnp.exp(jax.random.uniform(jax.random.fold_in(own, dim), (shards_of,), jnp.float32, least / len(pieces), high / len(pieces)))
        loudness = loudness * jnp.repeat(heights, dims[dim] // shards_of).reshape([-1 if axis == dim else 1 for axis in range(len(dims))])
    return loudness


def bell_draw(own_key, dims, scale, most, cuts=(), kind=jnp.bfloat16):
    values = scale * jax.random.normal(own_key, dims, jnp.float32)
    if cuts:
        values = values * steps_of(own_key, dims, cuts, -0.22, 0.18)
    return jnp.clip(values, -most, most).astype(kind)


def setup_inputs(seed: int = 0) -> dict:
    key_list = jax.random.split(jax.random.key(seed), 15)
    return {
        "tokens": bell_draw(key_list[0], (TOKENS, D), 1.0, 6.0, ((0, 8), (1, 4))),
        "dealing": draw_dealing(jax.random.fold_in(key_list[14], 71), 0),
        "seq_ids": draw_seq_ids(jax.random.fold_in(key_list[14], 71), 0),
        "first_values": bell_draw(key_list[3], (TOKENS, HEADS * HEAD_DIM), 1.0, 6.0, ((0, 8), (1, 4))),
        "out_grad": bell_draw(key_list[4], (TOKENS, D), 1.0, 6.0, ((0, 8), (1, 4))),
        "norm1_gain": jnp.clip(1.0 + 0.1 * jax.random.normal(key_list[5], (D,), jnp.float32), 0.5, 1.5).astype(jnp.bfloat16),
        "norm2_gain": jnp.clip(1.0 + 0.1 * jax.random.normal(key_list[6], (D,), jnp.float32), 0.5, 1.5).astype(jnp.bfloat16),
        "w_query": bell_draw(key_list[7], (D, HEADS * HEAD_DIM), D ** -0.5, 0.1875, ((1, 4),)),
        "w_key": bell_draw(key_list[8], (D, HEADS * HEAD_DIM), D ** -0.5, 0.1875, ((1, 4),)),
        "w_value": bell_draw(key_list[9], (D, HEADS * HEAD_DIM), D ** -0.5, 0.1875, ((1, 4),)),
        "w_out": bell_draw(key_list[10], (HEADS * HEAD_DIM, D), (D // 32) ** -0.5, 1.0, ((0, 4),)),
        "w_gate": bell_draw(key_list[11], (D, FF), D ** -0.5, 0.1875, ((1, 4),)),
        "w_up": bell_draw(key_list[12], (D, FF), D ** -0.5, 0.1875, ((1, 4),)),
        "w_down": bell_draw(key_list[13], (FF, D), FF ** -0.5, 0.109375, ((0, 4),)),
    }


EPS = 1e-06
THETA = 10000.0
NEG = -1e+30
HI = lax.Precision.HIGHEST

@jax.custom_vjp
def low(v):
    return lax.optimization_barrier(v.astype(jnp.bfloat16)).astype(jnp.float32)

@jax.custom_vjp
def low_back(v):
    return v

def low_keep(v):
    return (low(v), None)

def low_pass(kept, grad):
    return (grad,)

def back_keep(v):
    return (v, None)

def back_low(kept, grad):
    return (low(grad),)
low.defvjp(low_keep, low_pass)
low_back.defvjp(back_keep, back_low)

def both_ways(value):
    return low_back(low(value))

def matmul(left, right):
    return jnp.dot(left, right, precision=HI, preferred_element_type=jnp.float32)

def rope_tables(seq_row, head_dim):
    count = seq_row.shape[0]
    places = jnp.arange(count, dtype=jnp.int32)
    change = jnp.concatenate([jnp.ones((1,), bool), seq_row[1:] != seq_row[:-1]])
    starts = lax.cummax(jnp.where(change, places, jnp.zeros_like(places)), axis=0)
    offset = (places - starts).astype(jnp.float32)
    half = head_dim // 2
    freqs = THETA ** (-jnp.arange(half, dtype=jnp.float32) / half)
    angles = offset[:, None] * freqs[None, :]
    return (jnp.cos(angles), jnp.sin(angles))

def rotate(values, cos_rows, sin_rows):
    count = values.shape[0]
    half = cos_rows.shape[1]
    parts = values.reshape(count, -1, 2, half)
    first = parts[:, :, 0]
    second = parts[:, :, 1]
    cos_b = cos_rows[:, None, :]
    sin_b = sin_rows[:, None, :]
    return jnp.stack([first * cos_b - second * sin_b, second * cos_b + first * sin_b], axis=2).reshape(count, -1)

def layer(params, resid, firsts, seq_row):
    gain1, gain2, w_query, w_key, w_value, w_out, w_gate, w_up, w_down = params
    count = resid.shape[0]
    cos_rows, sin_rows = rope_tables(seq_row, HEAD_DIM)
    scale1 = lax.rsqrt(lax.optimization_barrier(jnp.mean(resid * resid, axis=1, keepdims=True)) + EPS)
    normed1 = low(resid * scale1 * gain1)
    query_pre = low_back(matmul(normed1, w_query))
    key_pre = low_back(matmul(normed1, w_key))
    queries = low(rotate(query_pre, cos_rows, sin_rows)).reshape(count, HEADS, HEAD_DIM)
    keys = low(rotate(key_pre, cos_rows, sin_rows)).reshape(count, HEADS, HEAD_DIM)
    values = both_ways(0.5 * matmul(normed1, w_value) + 0.5 * firsts).reshape(count, HEADS, HEAD_DIM)
    scores = low_back(jnp.einsum('qhd,khd->hqk', queries, keys, precision=HI) * HEAD_DIM ** (-0.5))
    places = jnp.arange(count, dtype=jnp.int32)
    mask = (seq_row[:, None] == seq_row[None, :]) & (places[None, :] <= places[:, None])
    scores = jnp.where(mask[None], scores, NEG)
    probs = jax.nn.softmax(scores, axis=-1)
    attended = both_ways(jnp.einsum('hqk,khd->qhd', low(probs), values, precision=HI)).reshape(count, HEADS * HEAD_DIM)
    middle = resid + low_back(matmul(attended, w_out))
    scale2 = lax.rsqrt(lax.optimization_barrier(jnp.mean(middle * middle, axis=1, keepdims=True)) + EPS)
    normed2 = low(middle * scale2 * gain2)
    gate = low_back(matmul(normed2, w_gate))
    upval = low_back(matmul(normed2, w_up))
    hidden = low(jax.nn.silu(gate) * upval)
    return middle + low_back(matmul(hidden, w_down))

def reference(tokens, dealing, seq_ids, first_values, out_grad, norm1_gain, norm2_gain, w_query, w_key, w_value, w_out, w_gate, w_up, w_down):
    inverse = jnp.argsort(dealing)

    def to_bins(array):
        return array[inverse].astype(jnp.float32).reshape(N_DP, TOK_DEV, -1)
    params = tuple((w.astype(jnp.float32) for w in (norm1_gain, norm2_gain, w_query, w_key, w_value, w_out, w_gate, w_up, w_down)))

    def per_bin(carry, items):
        resid, firsts, grads, seqs = items
        result, pullback = jax.vjp(lambda prm, rsd, fst: layer(prm, rsd, fst, seqs), params, resid, firsts)
        dparams, dresid, dfirst = pullback(grads)
        carry = jax.tree.map(jnp.add, carry, dparams)
        return (carry, (result, dresid, dfirst))
    zeros = tuple((jnp.zeros_like(w) for w in params))
    sums, (results, dresids, dfirsts) = lax.scan(per_bin, zeros, (to_bins(tokens), to_bins(first_values), to_bins(out_grad), seq_ids.reshape(N_DP, TOK_DEV)))

    def back_order(array):
        return array.reshape(TOKENS, -1)[dealing]
    output = back_order(results).astype(jnp.bfloat16)
    input_grad = back_order(dresids).astype(jnp.bfloat16)
    first_grad = back_order(dfirsts).astype(jnp.bfloat16)
    gain1_grad = sums[0].reshape(N_TENSOR, D // N_TENSOR)
    gain2_grad = sums[1].reshape(N_TENSOR, D // N_TENSOR)
    return (output, input_grad, first_grad, gain1_grad, gain2_grad, sums[2], sums[3], sums[4], sums[5], sums[6], sums[7], sums[8])
```

```python
import functools

import jax
import jax.numpy as jnp
from jax import lax
from jax.experimental import pallas as pl
from jax.experimental.pallas import tpu as pltpu
from jax.sharding import PartitionSpec as P

HEAD_DIM = 64
EPS = 1e-06
THETA = 10000.0
NEG = -1e30
BF = jnp.bfloat16
F32 = jnp.float32
BLK = 256
EXTRA = 8
MIB = 1 << 20


def nn(a, b):
    return lax.dot_general(a, b, (((1,), (0,)), ((), ())), preferred_element_type=F32)


def nt(a, b):
    return lax.dot_general(a, b, (((1,), (1,)), ((), ())), preferred_element_type=F32)


def tn(a, b):
    return lax.dot_general(a, b, (((0,), (0,)), ((), ())), preferred_element_type=F32)


def iota(shape, dim):
    return lax.broadcasted_iota(jnp.int32, shape, dim)


def whole(shape):
    return pl.BlockSpec(shape, lambda i, *_: (0,) * len(shape))


def rows(block, width):
    return pl.BlockSpec((block, width), lambda i, *_: (i, 0))


def params(mib):
    return pltpu.CompilerParams(
        dimension_semantics=("arbitrary",), vmem_limit_bytes=mib * MIB
    )


def sds(shape, dtype):
    return jax.ShapeDtypeStruct(shape, dtype)


def call(kernel, grid, ids, ins, outs, scratch=(), mib=40, name=None):
    return pl.pallas_call(
        kernel,
        out_shape=tuple(sds(s, d) for s, d, _ in outs),
        grid_spec=pltpu.PrefetchScalarGridSpec(
            num_scalar_prefetch=1,
            grid=(grid,),
            in_specs=[s for _, s in ins],
            out_specs=tuple(s for _, _, s in outs),
            scratch_shapes=list(scratch),
        ),
        compiler_params=params(mib),
        name=name,
    )(ids, *[a for a, _ in ins])


def pack_tokens(ids, deal_row, tok, n_dp):
    count, width = tok.shape
    per = count // n_dp

    def kernel(ids_ref, deal_ref, tok_ref, out_ref, pos_ref):
        deal = deal_ref[...]
        dest = deal // count
        slot = deal % count
        oh = iota((n_dp, count), 0) == dest
        before = iota((count, count), 0) < iota((count, count), 1)
        seen = nn(oh.astype(BF), before.astype(BF))
        base = (iota((n_dp, 1), 0) * per).astype(F32)
        pos = jnp.sum(jnp.where(oh, seen + base, 0.0), axis=0, keepdims=True)
        pos = pos.astype(jnp.int32)
        pos_ref[...] = jnp.broadcast_to(pos, (8, count))
        high = jnp.broadcast_to(slot // 32, (8, count))
        lowp = jnp.broadcast_to(slot % 32, (8, count))
        hl = jnp.where(iota((8, count), 0) == 0, high, lowp).astype(F32).astype(BF)
        tok = tok_ref[...]
        out_ref[:, per : per + EXTRA, :] = jnp.zeros((n_dp, EXTRA, width), BF)
        for d in range(n_dp):
            pick = (iota((per, count), 0) + d * per == pos).astype(F32).astype(BF)
            out_ref[d, 0:per, :] = nn(pick, tok).astype(BF)
            out_ref[d, per : per + 8, 0:per] = nt(hl, pick).astype(BF)

    return call(
        kernel,
        1,
        ids,
        [(deal_row, whole((1, count))), (tok, whole(tok.shape))],
        [
            ((n_dp, per + EXTRA, width), BF, whole((n_dp, per + EXTRA, width))),
            ((8, count), jnp.int32, whole((8, count))),
        ],
        name="pack_tokens",
    )


def pack_rest(ids, pos8, arrays, n_dp):
    count = arrays[0].shape[0]
    per = count // n_dp

    def kernel(ids_ref, pos_ref, *refs):
        pos = pos_ref[0:1, :]
        srcs, dsts = refs[: len(arrays)], refs[len(arrays) :]
        vals = [s[...] for s in srcs]
        for d in range(n_dp):
            pick = (iota((per, count), 0) + d * per == pos).astype(F32).astype(BF)
            for v, dst in zip(vals, dsts):
                dst[d] = nn(pick, v).astype(BF)

    return call(
        kernel,
        1,
        ids,
        [(pos8, whole((8, count)))] + [(a, whole(a.shape)) for a in arrays],
        [
            ((n_dp, per, a.shape[1]), BF, whole((n_dp, per, a.shape[1])))
            for a in arrays
        ],
        name="pack_rest",
    )


def one_hot(ids, row, col):
    count = row.shape[1]

    def kernel(ids_ref, row_ref, col_ref, a_ref, b_ref):
        i = pl.program_id(0)
        a_ref[...] = (iota((BLK, count), 0) + i * BLK == row_ref[...]).astype(F32).astype(BF)
        b_ref[...] = (iota((BLK, count), 1) == col_ref[...]).astype(F32).astype(BF)

    return call(
        kernel,
        count // BLK,
        ids,
        [(row, whole((1, count))), (col, rows(BLK, 1))],
        [((count, count), BF, rows(BLK, count))] * 2,
        name="one_hot",
    )


def permute_sum(ids, perm, parts, name):
    count, width = parts[0].shape

    def kernel(ids_ref, perm_ref, *refs):
        total = refs[0][...].astype(F32)
        for r in refs[1:-1]:
            total = total + r[...].astype(F32)
        refs[-1][...] = nn(perm_ref[...], total.astype(BF)).astype(BF)

    return call(
        kernel,
        1,
        ids,
        [(perm, whole(perm.shape))] + [(p, whole(p.shape)) for p in parts],
        [((count, width), BF, whole((count, width)))],
        name=name,
    )[0]


def place_grad(ids, perm, near, far):
    n_dp, per, two = near.shape
    count = n_dp * per
    width = two // 2

    def kernel(ids_ref, perm_ref, a_ref, b_ref, out_ref):
        t = ids_ref[0]
        perm = perm_ref[...]
        a = nn(perm, a_ref[...].reshape(count, two)).astype(BF)
        b = nn(perm, b_ref[...].reshape(count, two)).astype(BF)
        for flip, val in ((0, a[:, :width]), (2, a[:, width:]), (1, b[:, :width]), (3, b[:, width:])):
            at = pl.multiple_of((t ^ flip) * width, width)
            out_ref[:, pl.ds(at, width)] = val

    return call(
        kernel,
        count // BLK,
        ids,
        [(perm, rows(BLK, count)), (near, whole(near.shape)), (far, whole(far.shape))],
        [((count, 4 * width), BF, rows(BLK, 4 * width))],
        name="place_grad",
    )[0]


def head_mask(shape, head, split):
    lane = iota(shape, 1)
    if split:
        return (lane % (shape[1] // 2)) // (HEAD_DIM // 2) == head
    return lane // HEAD_DIM == head


def split_perm(width):
    half = HEAD_DIM // 2
    src = iota((width, width), 0)
    dst = iota((width, width), 1)
    second = dst // (width // 2)
    rest = dst % (width // 2)
    want = (rest // half) * HEAD_DIM + second * half + rest % half
    return (src == want).astype(F32).astype(BF)


def qkv_attention(ids, perm, pieces, firsts, cos, sin, gain, wq, wk, wv, start_col):
    n_dp, padded, width = pieces[0].shape
    per = firsts.shape[1]
    count = n_dp * per
    dim = gain.shape[1]
    heads = width // HEAD_DIM
    blocks = count // BLK

    def kernel(
        ids_ref, perm_ref, x0, x1, x2, x3, fv_ref, cos_ref, sin_ref, gain_ref,
        wq_ref, wk_ref, wv_ref, start_ref,
        x_out, n_out, q_out, k_out, v_out, o_out, lse_out, wqp, wkp, xs, ks, vs,
    ):
        i = pl.program_id(0)
        t = ids_ref[0]

        @pl.when(i == 0)
        def _():
            sp = split_perm(width)
            wqp[...] = nn(wq_ref[...], sp).astype(BF)
            wkp[...] = nn(wk_ref[...], sp).astype(BF)

        perm = perm_ref[...]
        for flip, ref in enumerate((x0, x1, x2, x3)):
            at = pl.multiple_of((t ^ flip) * width, width)
            xs[:, pl.ds(at, width)] = nn(perm, ref[:, 0:per, :].reshape(count, width))
        x = xs[...]
        x_out[...] = x.astype(BF)
        scale = lax.rsqrt(jnp.sum(x * x, axis=1, keepdims=True) / dim + EPS)
        normed = (x * scale * gain_ref[...]).astype(BF)
        n_out[...] = normed
        qp = nn(normed, wqp[...])
        kp = nn(normed, wkp[...])
        half = width // 2
        c, s = cos_ref[...], sin_ref[...]

        def rope(v):
            a, b = v[:, :half], v[:, half:]
            return jnp.concatenate([a * c - b * s, b * c + a * s], axis=1).astype(BF)

        q = rope(qp)
        k = rope(kp)
        fv = nn(perm, fv_ref[...].reshape(count, width))
        v = (0.5 * nn(normed, wv_ref[...]) + 0.5 * fv).astype(BF)
        q = (q.astype(F32) * HEAD_DIM ** (-0.5)).astype(BF)
        q_out[...] = q
        k_out[...] = k
        v_out[...] = v
        at = pl.multiple_of(i * BLK, BLK)
        ks[pl.ds(at, BLK), :] = k
        vs[pl.ds(at, BLK), :] = v
        start = start_ref[...]
        for j in range(blocks):

            @pl.when(i == j)
            def _(j=j):
                n = (j + 1) * BLK
                keys = ks[0:n, :]
                vals = vs[0:n, :]
                col = iota((BLK, n), 1)
                valid = (col >= start) & (col <= iota((BLK, n), 0) + j * BLK)
                out = jnp.zeros((BLK, width), F32)
                lse = jnp.zeros((BLK, 128), F32)
                for h in range(heads):
                    qh = jnp.where(head_mask((BLK, width), h, True), q, jnp.zeros_like(q))
                    sc = jnp.where(valid, nt(qh, keys), NEG)
                    top = jnp.max(sc, axis=1, keepdims=True)
                    ex = jnp.exp(sc - top)
                    total = jnp.sum(ex, axis=1, keepdims=True)
                    oh = nn(ex.astype(BF), vals) * (1.0 / total)
                    out = jnp.where(head_mask((BLK, width), h, False), oh, out)
                    lse = jnp.where(iota((BLK, 128), 1) == h, top + jnp.log(total), lse)
                o_out[...] = out.astype(BF)
                lse_out[...] = jnp.transpose(lse)[0:8, :]

    wide = rows(BLK, dim)
    narrow = rows(BLK, width)
    return call(
        kernel,
        blocks,
        ids,
        [(perm, rows(BLK, count))]
        + [(p, whole(p.shape)) for p in pieces]
        + [
            (firsts, whole(firsts.shape)),
            (cos, rows(BLK, width // 2)),
            (sin, rows(BLK, width // 2)),
            (gain, whole(gain.shape)),
            (wq, whole(wq.shape)),
            (wk, whole(wk.shape)),
            (wv, whole(wv.shape)),
            (start_col, rows(BLK, 1)),
        ],
        [
            ((count, dim), BF, wide),
            ((count, dim), BF, wide),
            ((count, width), BF, narrow),
            ((count, width), BF, narrow),
            ((count, width), BF, narrow),
            ((count, width), BF, narrow),
            ((8, count), F32, pl.BlockSpec((8, BLK), lambda i, *_: (0, i))),
            ((dim, width), BF, whole((dim, width))),
            ((dim, width), BF, whole((dim, width))),
        ],
        scratch=[
            pltpu.VMEM((BLK, dim), F32),
            pltpu.VMEM((count, width), BF),
            pltpu.VMEM((count, width), BF),
        ],
        name="qkv_attention",
    )


def feed_forward(ids, x, o_pieces, w_pieces, gain, w_gate, w_up, w_down):
    count, dim = x.shape
    width = o_pieces[0].shape[1]
    units = w_gate.shape[1]

    def kernel(
        ids_ref, x_ref, o0, o1, o2, o3, w0, w1, w2, w3, gain_ref, wg_ref, wu_ref, wd_ref,
        x1_out, n_out, g_out, u_out, h_out, yk0, yk2, ysend, ys,
    ):
        t = ids_ref[0]
        x1 = x_ref[...].astype(F32)
        for o, w in ((o0, w0), (o1, w1), (o2, w2), (o3, w3)):
            x1 = x1 + nn(o[...], w[...])
        x1_out[...] = x1
        scale = lax.rsqrt(jnp.sum(x1 * x1, axis=1, keepdims=True) / dim + EPS)
        normed = (x1 * scale * gain_ref[...]).astype(BF)
        n_out[...] = normed
        g = nn(normed, wg_ref[...])
        u = nn(normed, wu_ref[...])
        g_out[...] = g
        u_out[...] = u
        hid = (g * jax.nn.sigmoid(g) * u).astype(BF)
        h_out[...] = hid
        ys[...] = nn(hid, wd_ref[...])

        def piece(flip):
            return pl.ds(pl.multiple_of((t ^ flip) * width, width), width)

        yk0[...] = ys[:, piece(0)] + x1_out[:, piece(0)]
        yk2[...] = ys[:, piece(2)]
        ysend[0] = ys[:, piece(1)].astype(BF)
        ysend[1] = ys[:, piece(3)].astype(BF)

    wide = rows(BLK, dim)
    narrow = rows(BLK, width)
    mid = rows(BLK, units)
    return call(
        kernel,
        count // BLK,
        ids,
        [(x, wide)]
        + [(o, narrow) for o in o_pieces]
        + [(w, whole(w.shape)) for w in w_pieces]
        + [
            (gain, whole(gain.shape)),
            (w_gate, whole(w_gate.shape)),
            (w_up, whole(w_up.shape)),
            (w_down, whole(w_down.shape)),
        ],
        [
            ((count, dim), F32, wide),
            ((count, dim), BF, wide),
            ((count, units), F32, mid),
            ((count, units), F32, mid),
            ((count, units), BF, mid),
            ((count, width), F32, narrow),
            ((count, width), F32, narrow),
            ((2, count, width), BF, pl.BlockSpec((2, BLK, width), lambda i, *_: (0, i, 0))),
        ],
        scratch=[pltpu.VMEM((BLK, dim), F32)],
        name="feed_forward",
    )


def feed_backward(ids, x1, dy, g, u, w_pieces, gain, w_gate, w_up, w_down):
    count, dim = x1.shape
    width = w_pieces[0].shape[0]
    units = w_gate.shape[1]

    def kernel(
        ids_ref, x1_ref, dy_ref, g_ref, u_ref, w0, w1, w2, w3, gain_ref, wg_ref, wu_ref, wd_ref,
        dg_out, du_out, ak0, ak2, asend, dk0, dk2, dsend, gg_out, ds,
    ):
        i = pl.program_id(0)
        t = ids_ref[0]
        dy = dy_ref[...]
        g, u = g_ref[...], u_ref[...]
        sg = jax.nn.sigmoid(g)
        dh = nt(dy, wd_ref[...])
        du = (dh * (g * sg)).astype(BF)
        dg = (dh * u * sg * (1.0 + g * (1.0 - sg))).astype(BF)
        dg_out[...] = dg
        du_out[...] = du
        dn = nt(dg, wg_ref[...]) + nt(du, wu_ref[...])
        x1 = x1_ref[...]
        scale = lax.rsqrt(jnp.sum(x1 * x1, axis=1, keepdims=True) / dim + EPS)

        @pl.when(i == 0)
        def _():
            gg_out[...] = jnp.zeros_like(gg_out)

        gg_out[0:1, :] += jnp.sum(dn * (x1 * scale), axis=0, keepdims=True)
        z = dn * gain_ref[...]
        dot_row = jnp.sum(z * x1, axis=1, keepdims=True)
        part = scale * z - x1 * (scale * scale * scale * dot_row / dim) + 0.25 * dy.astype(F32)
        ds[...] = part

        def piece(flip):
            return pl.ds(pl.multiple_of((t ^ flip) * width, width), width)

        dk0[...] = ds[:, piece(0)]
        dk2[...] = ds[:, piece(2)]
        dsend[0] = ds[:, piece(1)].astype(BF)
        dsend[1] = ds[:, piece(3)].astype(BF)
        low = part.astype(BF)
        ak0[...] = nt(low, w0[...])
        asend[0] = nt(low, w1[...]).astype(BF)
        ak2[...] = nt(low, w2[...])
        asend[1] = nt(low, w3[...]).astype(BF)

    wide = rows(BLK, dim)
    narrow = rows(BLK, width)
    mid = rows(BLK, units)
    pair = ((2, count, width), BF, pl.BlockSpec((2, BLK, width), lambda i, *_: (0, i, 0)))
    keep = ((count, width), F32, narrow)
    return call(
        kernel,
        count // BLK,
        ids,
        [(x1, wide), (dy, wide), (g, mid), (u, mid)]
        + [(w, whole(w.shape)) for w in w_pieces]
        + [
            (gain, whole(gain.shape)),
            (w_gate, whole(w_gate.shape)),
            (w_up, whole(w_up.shape)),
            (w_down, whole(w_down.shape)),
        ],
        [
            ((count, units), BF, mid),
            ((count, units), BF, mid),
            keep,
            keep,
            pair,
            keep,
            keep,
            pair,
            ((8, dim), F32, whole((8, dim))),
        ],
        scratch=[pltpu.VMEM((BLK, dim), F32)],
        name="feed_backward",
    )


def attention_backward(ids, q, k, v, o, lse, a_parts, start_row, cos, sin, x, gain, wqp, wkp, wv):
    count, width = q.shape
    dim = x.shape[1]
    heads = width // HEAD_DIM
    blocks = count // BLK
    half = width // 2

    def kernel(
        ids_ref, q_ref, k_ref, v_ref, o_ref, lse_ref, a0, a1, a2, start_ref, cos_ref, sin_ref,
        x_ref, gain_ref, wq_ref, wk_ref, wv_ref,
        dv_out, dqkv_out, ek0, ek2, esend, gg_out, da, delta, dq, es,
    ):
        i = pl.program_id(0)
        t = ids_ref[0]

        @pl.when(i == 0)
        def _():
            gg_out[...] = jnp.zeros_like(gg_out)
            grad = (a0[...] + a1[...].astype(F32) + a2[...].astype(F32)).astype(BF)
            da[...] = grad
            prod = grad.astype(F32) * o_ref[...].astype(F32)
            pick = (iota((8, width), 1) // HEAD_DIM == iota((8, width), 0)).astype(F32)
            delta[...] = lax.dot_general(
                pick, prod, (((1,), (1,)), ((), ())),
                precision=lax.Precision.HIGHEST, preferred_element_type=F32,
            )
            dq[...] = jnp.zeros_like(dq)

        for j in range(blocks):

            @pl.when(i == j)
            def _(j=j):
                q0 = j * BLK
                n = count - q0
                qs = q_ref[q0:count, :]
                ds = da[q0:count, :]
                kj = k_ref[q0 : q0 + BLK, :]
                vj = v_ref[q0 : q0 + BLK, :]
                key = iota((BLK, n), 0)
                valid = (key + q0 >= start_ref[:, q0:count]) & (key <= iota((BLK, n), 1))
                dk = jnp.zeros((BLK, width), F32)
                dv = jnp.zeros((BLK, width), F32)
                grads, masked = [], []
                for h in range(heads):
                    mk = head_mask((BLK, width), h, True)
                    mv = head_mask((BLK, width), h, False)
                    kh = jnp.where(mk, kj, jnp.zeros_like(kj))
                    vh = jnp.where(mv, vj, jnp.zeros_like(vj))
                    sc = nt(kh, qs) - lse_ref[h : h + 1, q0:count]
                    pr = jnp.exp(jnp.where(valid, sc, NEG))
                    dp = nt(vh, ds)
                    dsc = (pr * (dp - delta[h : h + 1, q0:count])).astype(BF)
                    dv = jnp.where(mv, nn(pr.astype(BF), ds), dv)
                    dk = jnp.where(mk, nn(dsc, qs), dk)
                    grads.append(dsc)
                    masked.append(kh)
                dq[q0:count, :] += tn(jnp.concatenate(grads, 0), jnp.concatenate(masked, 0))
                es[0, :, 0:width] = dk
                es[1, :, 0:width] = dv

        at = pl.multiple_of(i * BLK, BLK)
        dqj = dq[pl.ds(at, BLK), :] * HEAD_DIM ** (-0.5)
        dkj = es[0, :, 0:width]
        dvj = es[1, :, 0:width]
        c, s = cos_ref[...], sin_ref[...]

        def rope_back(g):
            a, b = g[:, :half], g[:, half:]
            return jnp.concatenate([a * c + b * s, b * c - a * s], axis=1).astype(BF)

        dqp = rope_back(dqj)
        dkp = rope_back(dkj)
        dvp = (0.5 * dvj.astype(BF).astype(F32)).astype(BF)
        dv_out[...] = dvp
        sp = split_perm(width)
        dqkv_out[:, 0:width] = nt(dqp, sp).astype(BF)
        dqkv_out[:, width : 2 * width] = nt(dkp, sp).astype(BF)
        dqkv_out[:, 2 * width : 3 * width] = dvp
        dn = nt(dqp, wq_ref[...]) + nt(dkp, wk_ref[...]) + nt(dvp, wv_ref[...])
        x = x_ref[...].astype(F32)
        scale = lax.rsqrt(jnp.sum(x * x, axis=1, keepdims=True) / dim + EPS)
        gg_out[0:1, :] += jnp.sum(dn * (x * scale), axis=0, keepdims=True)
        z = dn * gain_ref[...]
        dot_row = jnp.sum(z * x, axis=1, keepdims=True)
        es[0] = scale * z - x * (scale * scale * scale * dot_row / dim)

        def piece(flip):
            return pl.ds(pl.multiple_of((t ^ flip) * width, width), width)

        ek0[...] = es[0, :, piece(0)]
        ek2[...] = es[0, :, piece(2)]
        esend[0] = es[0, :, piece(1)].astype(BF)
        esend[1] = es[0, :, piece(3)].astype(BF)

    narrow = rows(BLK, width)
    pair = ((2, count, width), BF, pl.BlockSpec((2, BLK, width), lambda i, *_: (0, i, 0)))
    keep = ((count, width), F32, narrow)
    full = whole((count, width))
    return call(
        kernel,
        blocks,
        ids,
        [(q, full), (k, full), (v, full), (o, full), (lse, whole(lse.shape))]
        + [(a, full) for a in a_parts]
        + [
            (start_row, whole((1, count))),
            (cos, rows(BLK, half)),
            (sin, rows(BLK, half)),
            (x, rows(BLK, dim)),
            (gain, whole(gain.shape)),
            (wqp, whole(wqp.shape)),
            (wkp, whole(wkp.shape)),
            (wv, whole(wv.shape)),
        ],
        [
            ((count, width), BF, narrow),
            ((count, 3 * width), BF, rows(BLK, 3 * width)),
            keep,
            keep,
            pair,
            ((8, dim), F32, whole((8, dim))),
        ],
        scratch=[
            pltpu.VMEM((count, width), BF),
            pltpu.VMEM((8, count), F32),
            pltpu.VMEM((count, width), F32),
            pltpu.VMEM((2, BLK, dim), F32),
        ],
        mib=48,
        name="attention_backward",
    )


ORDER = (0, 2, 1, 3)


def weight_grads(ids, pairs, name):
    count, dim = pairs[0][0].shape
    chunk = dim // 8

    def kernel(ids_ref, *refs):
        m = len(pairs)
        ins, outs, tmp = refs[: 2 * m], refs[2 * m : 4 * m], refs[4 * m :]
        y = ids_ref[1] & 1
        for p in range(m):
            tmp[p][...] = tn(ins[2 * p][...], ins[2 * p + 1][...])
            keep = pl.ds(pl.multiple_of(y * chunk, chunk), chunk)
            send = pl.ds(pl.multiple_of((1 - y) * chunk, chunk), chunk)
            outs[2 * p][0] = tmp[p][keep, :].astype(BF)
            outs[2 * p + 1][0] = tmp[p][send, :].astype(BF)

    def left_map(j, ids):
        flip = (j & 1) * 2 + (j >> 1)
        return (0, (ids[1] >> 1) ^ flip)

    ins, outs, scratch = [], [], []
    for left, right in pairs:
        ins.append((left, pl.BlockSpec((count, 2 * chunk), left_map)))
        ins.append((right, whole(right.shape)))
        spec = pl.BlockSpec((1, chunk, right.shape[1]), lambda j, *_: (j, 0, 0))
        outs += [((4, chunk, right.shape[1]), BF, spec)] * 2
        scratch.append(pltpu.VMEM((2 * chunk, right.shape[1]), F32))
    flat = call(kernel, 4, ids, ins, outs, scratch, mib=48, name=name)
    return [(flat[2 * p], flat[2 * p + 1]) for p in range(len(pairs))]


def flip_dp(value, bit):
    n = lax.axis_size("dp")
    return lax.ppermute(value, "dp", [(d, d ^ bit) for d in range(n)])


def flip_tensor(value, bit):
    return lax.ppermute(value, "tensor", [(d, d ^ bit) for d in range(4)])


def halve_sum(keep, send):
    total = keep.astype(F32) + flip_dp(send, 1).astype(F32)
    total = total[0:2] + flip_dp(total[2:4].astype(BF), 2).astype(F32)
    return total[0] + flip_dp(total[1].astype(BF), 4).astype(F32)


def gather_pieces(own):
    one = flip_tensor(own, 1)
    two = flip_tensor(own, 2)
    three = flip_tensor(two, 1)
    return (own, one, two, three)


def scatter_parts(keep0, keep2, send):
    got = flip_tensor(send, 1)
    far = flip_tensor((keep2 + got[1].astype(F32)).astype(BF), 2)
    return (keep0, got[0], far)


def per_device(
    tokens,
    dealing,
    seq_ids,
    first_values,
    out_grad,
    norm1_gain,
    norm2_gain,
    w_query,
    w_key,
    w_value,
    w_out,
    w_gate,
    w_up,
    w_down,
):
    n_dp = lax.axis_size("dp")
    count, width = tokens.shape
    dim = norm1_gain.shape[0]
    per = count // n_dp
    t = lax.axis_index("tensor")
    d = lax.axis_index("dp")
    ids = jnp.stack([t, d]).astype(jnp.int32)

    def exchange(packed):
        return lax.all_to_all(packed, "dp", split_axis=0, concat_axis=0, tiled=True)

    deal_row = dealing.reshape(1, count)
    sent, pos8 = pack_tokens(ids, deal_row, tokens, n_dp)
    arrived = exchange(sent)
    grad_far = flip_tensor(out_grad, 2)
    pieces = gather_pieces(arrived)
    slots = (
        arrived[:, per, :per].astype(F32) * 32.0 + arrived[:, per + 1, :per].astype(F32)
    ).astype(jnp.int32)
    place, place_t = one_hot(ids, slots.reshape(1, count), slots.reshape(count, 1))

    first_sent, near_sent = pack_rest(
        ids, pos8, [first_values, jnp.concatenate([out_grad, grad_far], axis=1)], n_dp
    )
    first_sent, pieces0 = lax.optimization_barrier((first_sent, arrived))
    firsts = exchange(first_sent)
    near_sent, firsts = lax.optimization_barrier((near_sent, firsts))
    near = exchange(near_sent)
    far = flip_tensor(near, 1)

    start = jnp.sum(seq_ids[None, :] < seq_ids[:, None], axis=1, dtype=jnp.int32)
    start_flat = start
    offset = (jnp.arange(count, dtype=jnp.int32) - start_flat).astype(F32)
    half = HEAD_DIM // 2
    freqs = THETA ** (-jnp.arange(half, dtype=F32) / half)
    angles = offset[:, None] * freqs[None, :]
    reps = (1, width // HEAD_DIM)
    cos = jnp.tile(jnp.cos(angles), reps)
    sin = jnp.tile(jnp.sin(angles), reps)
    gain1 = norm1_gain.astype(F32).reshape(1, dim)
    gain2 = norm2_gain.astype(F32).reshape(1, dim)

    x, normed1, q, k, v, attended, lse, wqp, wkp = qkv_attention(
        ids, place, pieces, firsts, cos, sin, gain1, w_query, w_key, w_value,
        start_flat.reshape(count, 1),
    )
    w_pieces = gather_pieces(w_out)
    o_pieces = gather_pieces(attended)
    dy = place_grad(ids, place, near, far)
    x1, normed2, gate, up, hidden, yk0, yk2, ysend = feed_forward(
        ids, x, o_pieces, w_pieces, gain2, w_gate, w_up, w_down
    )
    dgate, dup, ak0, ak2, asend, dk0, dk2, dsend, gg2 = feed_backward(
        ids, x1, dy, gate, up, w_pieces, gain2, w_gate, w_up, w_down
    )
    a_parts = scatter_parts(ak0, ak2, asend)
    y_parts = scatter_parts(yk0, yk2, ysend)
    d_parts = scatter_parts(dk0, dk2, dsend)
    dx1 = d_parts[0] + d_parts[1].astype(F32) + d_parts[2].astype(F32)
    da = gather_pieces(dx1.astype(BF))

    dvp, dqkv, ek0, ek2, esend, gg1 = attention_backward(
        ids, q, k, v, attended, lse, a_parts, start_flat.reshape(1, count), cos, sin, x, gain1,
        wqp, wkp, w_value,
    )
    e_parts = scatter_parts(ek0, ek2, esend)

    da_full = jnp.zeros((count, dim), BF)
    for flip in range(4):
        da_full = lax.dynamic_update_slice(da_full, da[flip], (0, (t ^ flip) * width))

    if n_dp == 8:
        mlp = weight_grads(
            ids, [(normed2, dgate), (normed2, dup), (dy, hidden)], "grads_mlp"
        )
        gw_gate, gw_up, gw_down = [halve_sum(*pair) for pair in mlp]
        gw_down = gw_down.T
        (att,) = weight_grads(ids, [(normed1, dqkv)], "grads_qkv")
        gw_qkv = halve_sum(*att)
        gw_q, gw_k, gw_v = jnp.split(gw_qkv, 3, axis=1)
        (wo,) = weight_grads(ids, [(da_full, attended)], "grads_out")
        gw_out = halve_sum(*wo).T
    else:

        def scattered(left, right, dim_):
            full = jnp.einsum("ta,tb->ab", left, right, preferred_element_type=F32)
            return lax.psum_scatter(full, "dp", scatter_dimension=dim_, tiled=True)

        gw_gate = scattered(normed2, dgate, 0)
        gw_up = scattered(normed2, dup, 0)
        gw_down = scattered(hidden, dy, 1)
        gw_q, gw_k, gw_v = [
            scattered(normed1, p, 0) for p in jnp.split(dqkv, 3, axis=1)
        ]
        gw_out = scattered(attended, da_full, 1)

    gains = lax.psum(jnp.concatenate([gg1[0:1], gg2[0:1]], axis=0), ("dp", "tensor"))
    part = width // n_dp
    mine = lax.dynamic_slice(gains, (0, t * width + d * part), (2, part))

    pos = pos8[0]
    restore = one_hot(ids, pos.reshape(1, count), pos.reshape(count, 1))[1]

    def send_back(parts, name):
        packed = permute_sum(ids, place_t, parts, name).reshape(n_dp, per, width)
        back = exchange(packed).reshape(count, width)
        return permute_sum(ids, restore, [back], name + "_restore")

    output = send_back(list(y_parts), "output")
    first_grad = send_back([dvp], "first_grad")
    input_grad = send_back(list(e_parts) + [dx1], "input_grad")
    return (
        output,
        input_grad,
        first_grad,
        mine[0:1],
        mine[1:2],
        gw_q,
        gw_k,
        gw_v,
        gw_out,
        gw_gate,
        gw_up,
        gw_down,
    )


def solution(mesh):
    in_specs = (
        P("dp", "tensor"),
        P("dp"),
        P("dp"),
        P("dp", "tensor"),
        P("dp", "tensor"),
        P(),
        P(),
        P(None, "tensor"),
        P(None, "tensor"),
        P(None, "tensor"),
        P("tensor", None),
        P(None, "tensor"),
        P(None, "tensor"),
        P("tensor", None),
    )
    out_specs = (
        P("dp", "tensor"),
        P("dp", "tensor"),
        P("dp", "tensor"),
        P("tensor", "dp"),
        P("tensor", "dp"),
        P("dp", "tensor"),
        P("dp", "tensor"),
        P("dp", "tensor"),
        P("tensor", "dp"),
        P("dp", "tensor"),
        P("dp", "tensor"),
        P("tensor", "dp"),
    )
    return jax.shard_map(
        per_device, mesh=mesh, in_specs=in_specs, out_specs=out_specs, check_vma=False
    )
```

```python
import functools

import jax
import jax.numpy as jnp
from jax import lax
from jax.experimental import pallas as pl
from jax.experimental.pallas import tpu as pltpu
from jax.sharding import PartitionSpec as P

HEAD_DIM = 64
EPS = 1e-06
THETA = 10000.0
NEG = -1e30
BF = jnp.bfloat16
F32 = jnp.float32
BLK = 256
EXTRA = 8
MIB = 1 << 20


def nn(a, b):
    return lax.dot_general(a, b, (((1,), (0,)), ((), ())), preferred_element_type=F32)


def nt(a, b):
    return lax.dot_general(a, b, (((1,), (1,)), ((), ())), preferred_element_type=F32)


def tn(a, b):
    return lax.dot_general(a, b, (((0,), (0,)), ((), ())), preferred_element_type=F32)


def iota(shape, dim):
    return lax.broadcasted_iota(jnp.int32, shape, dim)


TIMES = {
    "pack_tokens": 3,
    "pack_rows": 3,
    "qkv_attention": 14,
    "feed_forward": 12,
    "sort_rows": 3,
    "grads_down": 5,
    "feed_backward": 15,
    "grads_mlp": 8,
    "return_rows": 3,
    "attention_backward": 17,
    "grads_out": 4,
    "grads_qkv": 5,
    "pack_grads": 4,
    "unpack_grads": 4,
    "restore_rows": 3,
}


class Fetched:
    def __init__(self, src, buf, sems, base, parts):
        size = src.shape[0] // parts
        self.buf = buf
        self.copies = [
            pltpu.make_async_copy(
                src.at[pl.ds(p * size, size)], buf.at[pl.ds(p * size, size)], sems.at[base + p]
            )
            for p in range(parts)
        ]
        self.waited = [False] * parts

    def start(self):
        for c in self.copies:
            c.start()

    def __call__(self, part=None):
        for p in range(len(self.copies)) if part is None else (part,):
            if not self.waited[p]:
                self.copies[p].wait()
                self.waited[p] = True
        return self.buf


class Stored:
    def __init__(self, dst, buf, sems, base):
        self.dst, self.buf, self.sems, self.at = dst, buf, sems, base
        self.copies = []

    def flush(self, *index):
        src = self.buf.at[index] if index else self.buf
        dst = self.dst.at[index] if index else self.dst
        c = pltpu.make_async_copy(src, dst, self.sems.at[self.at + len(self.copies)])
        c.start()
        self.copies.append(c)


def call(body, ids, ins, outs, scratch=(), mib=48, name=None):
    took = TIMES[name]
    n_in, n_out = len(ins), len(outs)
    in_at = [sum(p for _, p in ins[:k]) for k in range(n_in + 1)]
    out_at = [sum(p for _, _, p in outs[:k]) for k in range(n_out + 1)]

    def kernel(ids_ref, *refs):
        srcs, refs = refs[:n_in], refs[n_in:]
        dsts, refs = refs[:n_out], refs[n_out:]
        bufs, refs = refs[:n_in], refs[n_in:]
        obufs, refs = refs[:n_out], refs[n_out:]
        in_sems, out_sems, refs = refs[0], refs[1], refs[2:]
        inputs = [
            Fetched(src, buf, in_sems, in_at[k], ins[k][1])
            for k, (src, buf) in enumerate(zip(srcs, bufs))
        ]
        outputs = [
            Stored(dst, buf, out_sems, out_at[k]) for k, (dst, buf) in enumerate(zip(dsts, obufs))
        ]
        for i in inputs:
            i.start()
        body(ids_ref, inputs, outputs, refs)
        for i in inputs:
            i()
        for k, o in enumerate(outputs):
            assert len(o.copies) == outs[k][2]
            for c in o.copies:
                c.wait()

    return pl.pallas_call(
        kernel,
        out_shape=tuple(pltpu.HBM(s, d) for s, d, _ in outs),
        in_specs=[pl.BlockSpec(memory_space=pltpu.SMEM)]
        + [pl.BlockSpec(memory_space=pl.ANY)] * n_in,
        out_specs=tuple(pl.BlockSpec(memory_space=pl.ANY) for _ in outs),
        scratch_shapes=[pltpu.VMEM(a.shape, a.dtype) for a, _ in ins]
        + [pltpu.VMEM(s, d) for s, d, _ in outs]
        + [pltpu.SemaphoreType.DMA((in_at[-1],)), pltpu.SemaphoreType.DMA((out_at[-1],))]
        + list(scratch),
        compiler_params=pltpu.CompilerParams(vmem_limit_bytes=mib * MIB),
        cost_estimate=pl.CostEstimate(
            flops=took * 1_150_000_000, transcendentals=0, bytes_accessed=took * 3_690_000
        ),
        name=name,
    )(ids, *[pltpu.with_memory_space_constraint(a, pltpu.HBM) for a, _ in ins])


def piece(ids_ref, flip, width):
    return pl.ds(pl.multiple_of((ids_ref[0] ^ flip) * width, width), width)


def picks(index, first, size):
    shape = (size, index.shape[1])
    return jnp.where(iota(shape, 0) + first == index, 1.0, 0.0).astype(BF)


def pack_tokens(ids, deal_row, tok, n_dp):
    count, width = tok.shape
    per = count // n_dp
    lanes = 128

    def body(ids_ref, ins, outs, scratch):
        deal_in, tok_in = ins
        out, pos_out = outs
        deal = deal_in()[...]
        dest = deal // count
        slot = deal % count
        oh = jnp.where(iota((n_dp, count), 0) == dest, 1.0, 0.0)
        upto = jnp.where(iota((lanes, lanes), 0) <= iota((lanes, lanes), 1), 1.0, 0.0)
        parts = [oh[:, b * lanes : (b + 1) * lanes] for b in range(count // lanes)]
        inner = nn(jnp.concatenate(parts, axis=0).astype(BF), upto.astype(BF))
        base = (iota((n_dp, 1), 0) * per - 1).astype(F32)
        rows_ = []
        for b, part in enumerate(parts):
            seen = inner[b * n_dp : (b + 1) * n_dp]
            rows_.append(jnp.sum(part * (seen + base), axis=0, keepdims=True))
            base = base + seen[:, lanes - 1 :]
        pos = jnp.concatenate(rows_, axis=1).astype(jnp.int32)
        pos_out.buf[...] = jnp.broadcast_to(pos, (8, count))
        pos_out.flush()
        high = jnp.broadcast_to(slot // 32, (8, count))
        low = jnp.broadcast_to(slot % 32, (8, count))
        hl = jnp.where(iota((8, count), 0) == 0, high, low).astype(F32).astype(BF)
        out.buf[:, per : per + EXTRA, :] = jnp.zeros((n_dp, EXTRA, width), BF)
        size = min(count, 512)
        group = size // per
        for g in range(count // size):
            pick = picks(pos, g * size, size)
            moved = nn(pick, tok_in()[...]).astype(BF)
            marks = nt(hl, pick).astype(BF)
            for e in range(group):
                d = g * group + e
                out.buf[d, 0:per, :] = moved[e * per : (e + 1) * per]
                out.buf[d, per : per + 8, 0:per] = marks[:, e * per : (e + 1) * per]
            out.flush(pl.ds(g * group, group))

    return call(
        body,
        ids,
        [(deal_row, 1), (tok, 1)],
        [
            ((n_dp, per + EXTRA, width), BF, count // min(count, 512)),
            ((8, count), jnp.int32, 1),
        ],
        name="pack_tokens",
    )


def permuted(ids, index, parts, transpose, name):
    count, width = parts[0].shape
    blocks = 2
    size = count // blocks

    def body(ids_ref, ins, outs, scratch):
        idx = ins[0]()[0:1, :]
        total = ins[1]()[...]
        for r in ins[2:]:
            total = total.astype(F32) + r()[...].astype(F32)
        total = total.astype(BF)
        (out,) = outs
        if transpose:
            acc = tn(picks(idx, 0, count), total)
            out.buf[...] = acc.astype(BF)
            out.flush()
        else:
            for b in range(blocks):
                at = slice(b * size, (b + 1) * size)
                out.buf[at, :] = nn(picks(idx, b * size, size), total).astype(BF)
                out.flush(pl.ds(b * size, size))

    return call(
        body,
        ids,
        [(index, 1)] + [(p, 1) for p in parts],
        [((count, width), BF, 1 if transpose else blocks)],
        name=name,
    )[0]


def head_mask(shape, head, split):
    lane = iota(shape, 1)
    if split:
        return (lane % (shape[1] // 2)) // (HEAD_DIM // 2) == head
    return lane // HEAD_DIM == head


def split_perm(width):
    half = HEAD_DIM // 2
    src = iota((width, width), 0)
    dst = iota((width, width), 1)
    second = dst // (width // 2)
    rest = dst % (width // 2)
    want = (rest // half) * HEAD_DIM + second * half + rest % half
    return (src == want).astype(F32).astype(BF)


def qkv_attention(ids, slot_row, pieces, firsts, cos, sin, gain, wq, wk, wv, start_row):
    n_dp, padded, width = pieces[0].shape
    per = firsts.shape[1]
    count = n_dp * per
    dim = gain.shape[1]
    heads = width // HEAD_DIM
    blocks = count // BLK
    half = width // 2

    def body(ids_ref, ins, outs, scratch):
        slot_in, x0, x1, x2, x3, fv_in, wq_in, wk_in, wv_in, cos_in, sin_in, gain_in, start_in = ins
        x_out, n_out, qkv_out, o_out, lse_out, w_out = outs
        cat, vt = scratch
        slots = slot_in()[...]
        for flip, ref in enumerate((x0, x1, x2, x3)):
            cat[:, piece(ids_ref, flip, width)] = ref()[:, 0:per, :].reshape(count, width)
        cat[:, dim:] = fv_in()[...].reshape(count, width)
        sp = split_perm(width)
        w_out.buf[:, 0:width] = nn(wq_in()[...], sp).astype(BF)
        w_out.buf[:, width : 2 * width] = nn(wk_in()[...], sp).astype(BF)
        w_out.buf[:, 2 * width :] = wv_in()[...]
        w_out.flush()
        lse_out.buf[...] = jnp.zeros_like(lse_out.buf)

        def rope(v, c, s):
            a, b = v[:, :half], v[:, half:]
            return jnp.concatenate([a * c - b * s, b * c + a * s], axis=1).astype(BF)

        for j in range(blocks):
            at = slice(j * BLK, (j + 1) * BLK)
            ds = pl.ds(j * BLK, BLK)
            moved = nn(picks(slots, j * BLK, BLK), cat[...])
            x = moved[:, :dim]
            x_out.buf[at, :] = x.astype(BF)
            x_out.flush(ds)
            scale = lax.rsqrt(jnp.sum(x * x, axis=1, keepdims=True) / dim + EPS)
            normed = (x * scale * gain_in()[...]).astype(BF)
            n_out.buf[at, :] = normed
            n_out.flush(ds)
            qkv = nn(normed, w_out.buf[...])
            c, s = cos_in()[at, :], sin_in()[at, :]
            q = rope(qkv[:, 0:width], c, s)
            v = 0.5 * qkv[:, 2 * width :] + 0.5 * moved[:, dim:]
            q = (q.astype(F32) * HEAD_DIM ** (-0.5)).astype(BF)
            qkv_out.buf[at, 0:width] = q
            qkv_out.buf[at, width : 2 * width] = rope(qkv[:, width : 2 * width], c, s)
            qkv_out.buf[at, 2 * width :] = v.astype(BF)
            qkv_out.flush(ds)
            vt[:, at] = jnp.transpose(v).astype(BF)
            start = start_in()[:, at]
            n = (j + 1) * BLK
            keys = qkv_out.buf[0:n, width : 2 * width]
            key = iota((n, BLK), 0)
            valid = (key >= start) & (key <= iota((n, BLK), 1) + j * BLK)
            out = []
            for h in range(heads):
                qh = jnp.where(head_mask((BLK, width), h, True), q, jnp.zeros_like(q))
                sc = jnp.where(valid, nt(keys, qh), NEG)
                top = jnp.max(sc, axis=0, keepdims=True)
                ex = jnp.exp(sc - top)
                total = jnp.sum(ex, axis=0, keepdims=True)
                vals = vt[h * HEAD_DIM : (h + 1) * HEAD_DIM, 0:n]
                out.append(nn(vals, ex.astype(BF)) * (1.0 / total))
                lse_out.buf[h : h + 1, at] = top + jnp.log(total)
            o_out.buf[at, :] = jnp.transpose(jnp.concatenate(out, axis=0)).astype(BF)
            o_out.flush(ds)
        lse_out.flush()

    return call(
        body,
        ids,
        [(slot_row, 1)]
        + [(p, 1) for p in pieces]
        + [(a, 1) for a in (firsts, wq, wk, wv, cos, sin, gain, start_row)],
        [
            ((count, dim), BF, blocks),
            ((count, dim), BF, blocks),
            ((count, 3 * width), BF, blocks),
            ((count, width), BF, blocks),
            ((8, count), F32, 1),
            ((dim, 3 * width), BF, 1),
        ],
        scratch=[pltpu.VMEM((count, dim + width), BF), pltpu.VMEM((width, count), BF)],
        name="qkv_attention",
    )


FEED = 512


def feed_forward(ids, x, o_pieces, w_pieces, gain, w_gate, w_up, w_down):
    count, dim = x.shape
    width = o_pieces[0].shape[1]
    units = w_gate.shape[0]
    size = min(FEED, count)
    blocks = count // size

    def body(ids_ref, ins, outs, scratch):
        w_ins, o_ins = ins[0:4], ins[4:8]
        x_in, gain_in, wg_in, wu_in, wd_in = ins[8:]
        x1_out, n_out, fg_out, fu_out, h_out, yk0, yk2, ysend = outs
        ys, xs, wo = scratch
        for k, w in enumerate(w_ins):
            wo[k * width : (k + 1) * width, :] = w()[...]
        for j in range(blocks):
            at = slice(j * size, (j + 1) * size)
            ds = pl.ds(j * size, size)
            heads = jnp.concatenate([o()[at, :] for o in o_ins], axis=1)
            x1 = x_in(j)[at, :].astype(F32) + nn(heads, wo[...])
            xs[...] = x1
            x1_out.buf[at, :] = x1.astype(BF)
            x1_out.flush(ds)
            scale = lax.rsqrt(jnp.sum(x1 * x1, axis=1, keepdims=True) / dim + EPS)
            normed = (x1 * scale * gain_in()[...]).astype(BF)
            n_out.buf[at, :] = normed
            n_out.flush(ds)
            g = nt(normed, wg_in()[...])
            u = nt(normed, wu_in()[...])
            sg = jax.nn.sigmoid(g)
            silu = g * sg
            hid = (silu * u).astype(BF)
            h_out.buf[at, :] = hid
            h_out.flush(ds)
            fu_out.buf[at, :] = silu.astype(BF)
            fu_out.flush(ds)
            fg_out.buf[at, :] = (u * sg * (1.0 + g * (1.0 - sg))).astype(BF)
            fg_out.flush(ds)
            ys[...] = nn(hid, wd_in()[...])
            ysend.buf[0, at, :] = ys[:, piece(ids_ref, 1, width)].astype(BF)
            ysend.buf[1, at, :] = ys[:, piece(ids_ref, 3, width)].astype(BF)
            ysend.flush(slice(None), ds)
            own = piece(ids_ref, 0, width)
            yk0.buf[at, :] = ys[:, own] + xs[:, own]
            yk0.flush(ds)
            yk2.buf[at, :] = ys[:, piece(ids_ref, 2, width)].astype(BF)
            yk2.flush(ds)

    return call(
        body,
        ids,
        [(w, 1) for w in w_pieces]
        + [(o, 1) for o in o_pieces]
        + [(x, blocks), (gain, 1), (w_gate, 1), (w_up, 1), (w_down, 1)],
        [
            ((count, dim), BF, blocks),
            ((count, dim), BF, blocks),
            ((count, units), BF, blocks),
            ((count, units), BF, blocks),
            ((count, units), BF, blocks),
            ((count, width), F32, blocks),
            ((count, width), BF, blocks),
            ((2, count, width), BF, blocks),
        ],
        scratch=[
            pltpu.VMEM((size, dim), F32),
            pltpu.VMEM((size, dim), F32),
            pltpu.VMEM((4 * width, dim), BF),
        ],
        mib=60,
        name="feed_forward",
    )


def feed_backward(ids, x1, near, far, fg, fu, w_pieces, gain, w_gate, w_up, w_down):
    count, dim = x1.shape
    width = w_pieces[0].shape[0]
    units = w_gate.shape[0]
    size = min(FEED, count)
    blocks = count // size

    def body(ids_ref, ins, outs, scratch):
        wd_in, near_in, far_in, fg_in, fu_in, wg_in, wu_in, x1_in, gain_in = ins[:9]
        w_ins = ins[9:]
        dg_out, du_out, ak0, ak2, asend, dk0, dk2, dsend, gg_out = outs
        ds_, ys, wo = scratch
        sums = jnp.zeros((1, dim), F32)
        for j in range(blocks):
            at = slice(j * size, (j + 1) * size)
            ds = pl.ds(j * size, size)
            near_, far_ = near_in(j)[at, :], far_in(j)[at, :]
            ys[:, piece(ids_ref, 0, width)] = near_[:, :width]
            ys[:, piece(ids_ref, 2, width)] = near_[:, width:]
            ys[:, piece(ids_ref, 1, width)] = far_[:, :width]
            ys[:, piece(ids_ref, 3, width)] = far_[:, width:]
            dy = ys[...]
            dh = nt(dy, wd_in()[...])
            dg = (dh * fg_in(j)[at, :].astype(F32)).astype(BF)
            du = (dh * fu_in(j)[at, :].astype(F32)).astype(BF)
            dg_out.buf[at, :] = dg
            du_out.buf[at, :] = du
            dg_out.flush(ds)
            du_out.flush(ds)
            dn = nn(dg, wg_in()[...]) + nn(du, wu_in()[...])
            x1 = x1_in(j)[at, :].astype(F32)
            scale = lax.rsqrt(jnp.sum(x1 * x1, axis=1, keepdims=True) / dim + EPS)
            sums = sums + jnp.sum(dn * (x1 * scale), axis=0, keepdims=True)
            z = dn * gain_in()[...]
            dot_row = jnp.sum(z * x1, axis=1, keepdims=True)
            part = scale * z - x1 * (scale * scale * scale * dot_row / dim)
            part = part + 0.25 * dy.astype(F32)
            ds_[...] = part
            if j == 0:
                for k, w in enumerate(w_ins):
                    wo[k * width : (k + 1) * width, :] = w()[...]
            da = nt(part.astype(BF), wo[...])
            asend.buf[0, at, :] = da[:, width : 2 * width].astype(BF)
            asend.buf[1, at, :] = da[:, 3 * width :].astype(BF)
            asend.flush(slice(None), ds)
            ak0.buf[at, :] = da[:, 0:width]
            ak0.flush(ds)
            ak2.buf[at, :] = da[:, 2 * width : 3 * width].astype(BF)
            ak2.flush(ds)
            dsend.buf[0, at, :] = ds_[:, piece(ids_ref, 1, width)].astype(BF)
            dsend.buf[1, at, :] = ds_[:, piece(ids_ref, 3, width)].astype(BF)
            dsend.flush(slice(None), ds)
            dk0.buf[at, :] = ds_[:, piece(ids_ref, 0, width)]
            dk0.flush(ds)
            dk2.buf[at, :] = ds_[:, piece(ids_ref, 2, width)].astype(BF)
            dk2.flush(ds)
        gg_out.buf[...] = jnp.broadcast_to(sums, (8, dim))
        gg_out.flush()

    return call(
        body,
        ids,
        [(w_down, 1), (near, blocks), (far, blocks), (fg, blocks), (fu, blocks)]
        + [(w_gate, 1), (w_up, 1), (x1, blocks), (gain, 1)]
        + [(w, 1) for w in w_pieces],
        [
            ((count, units), BF, blocks),
            ((count, units), BF, blocks),
            ((count, width), F32, blocks),
            ((count, width), BF, blocks),
            ((2, count, width), BF, blocks),
            ((count, width), F32, blocks),
            ((count, width), BF, blocks),
            ((2, count, width), BF, blocks),
            ((8, dim), F32, 1),
        ],
        scratch=[
            pltpu.VMEM((size, dim), F32),
            pltpu.VMEM((size, dim), BF),
            pltpu.VMEM((4 * width, dim), BF),
        ],
        mib=60,
        name="feed_backward",
    )


def attention_backward(ids, qkv, o, lse, a_parts, start_row, cos, sin, x, gain, w_qkv, gg2):
    count, width = o.shape
    dim = x.shape[1]
    heads = width // HEAD_DIM
    blocks = count // BLK
    half = width // 2
    part = HEAD_DIM // 2

    def body(ids_ref, ins, outs, scratch):
        qkv_in, a0, a1, a2, o_in, lse_in, start_in, cos_in, sin_in, w_in, x_in, gain_in, g2_in = ins
        dv_out, dqkv_out, ek0, ek2, esend, gg_out = outs
        kt, dk, dv, es = scratch
        qkv_ref = qkv_in()
        for b in range(blocks):
            at = slice(b * BLK, (b + 1) * BLK)
            kt[:, at] = jnp.transpose(qkv_ref[at, width : 2 * width].astype(F32)).astype(BF)
        sums = jnp.zeros((1, dim), F32)
        pick = (iota((8, width), 1) // HEAD_DIM == iota((8, width), 0)).astype(F32)
        sp = split_perm(width)

        def rope_back(g, c, s):
            a, b = g[:, :half], g[:, half:]
            return jnp.concatenate([a * c + b * s, b * c - a * s], axis=1).astype(BF)

        for j in reversed(range(blocks)):
            at = slice(j * BLK, (j + 1) * BLK)
            ds = pl.ds(j * BLK, BLK)
            q = qkv_ref[at, 0:width]
            do = (a0()[at, :] + a1()[at, :].astype(F32) + a2()[at, :].astype(F32)).astype(BF)
            prod = do.astype(F32) * o_in()[at, :].astype(F32)
            delta = lax.dot_general(
                pick, prod, (((1,), (1,)), ((), ())),
                precision=lax.Precision.HIGHEST, preferred_element_type=F32,
            )
            start = start_in()[:, at]
            lse = lse_in()[:, at]
            n = (j + 1) * BLK
            keys = qkv_ref[0:n, width : 2 * width]
            vals = qkv_ref[0:n, 2 * width :]
            key = iota((n, BLK), 0)
            valid = (key >= start) & (key <= iota((n, BLK), 1) + j * BLK)
            probs, grads, q_heads, do_heads = [], [], [], []
            first, second = [], []
            for h in range(heads):
                qh = jnp.where(head_mask((BLK, width), h, True), q, jnp.zeros_like(q))
                dh = jnp.where(head_mask((BLK, width), h, False), do, jnp.zeros_like(do))
                sc = jnp.where(valid, nt(keys, qh) - lse[h : h + 1, :], NEG)
                pr = jnp.exp(sc)
                dsc = (pr * (nt(vals, dh) - delta[h : h + 1, :])).astype(BF)
                probs.append(pr.astype(BF))
                grads.append(dsc)
                q_heads.append(qh)
                do_heads.append(dh)
                kh = jnp.concatenate(
                    [
                        kt[h * part : (h + 1) * part, 0:n],
                        kt[half + h * part : half + (h + 1) * part, 0:n],
                    ],
                    axis=0,
                )
                dqh = nn(kh, dsc)
                first.append(dqh[:part])
                second.append(dqh[part:])
            dvn = nn(jnp.concatenate(probs, 1), jnp.concatenate(do_heads, 0))
            dkn = nn(jnp.concatenate(grads, 1), jnp.concatenate(q_heads, 0))
            if j == blocks - 1:
                dv[...] = dvn
                dk[...] = dkn
            else:
                dv[0:n, :] += dvn
                dk[0:n, :] += dkn
            dqj = jnp.transpose(jnp.concatenate(first + second, axis=0)) * HEAD_DIM ** (-0.5)
            c, s = cos_in()[at, :], sin_in()[at, :]
            dqp = rope_back(dqj, c, s)
            dkp = rope_back(dk[at, :], c, s)
            dvp = (0.5 * dv[at, :].astype(BF).astype(F32)).astype(BF)
            dv_out.buf[at, :] = dvp
            dv_out.flush(ds)
            dqkv_out.buf[at, 0:width] = nt(dqp, sp).astype(BF)
            dqkv_out.buf[at, width : 2 * width] = nt(dkp, sp).astype(BF)
            dqkv_out.buf[at, 2 * width :] = dvp
            dqkv_out.flush(ds)
            dn = nt(jnp.concatenate([dqp, dkp, dvp], axis=1), w_in()[...])
            x = x_in()[at, :].astype(F32)
            scale = lax.rsqrt(jnp.sum(x * x, axis=1, keepdims=True) / dim + EPS)
            sums = sums + jnp.sum(dn * (x * scale), axis=0, keepdims=True)
            z = dn * gain_in()[...]
            dot_row = jnp.sum(z * x, axis=1, keepdims=True)
            es[...] = scale * z - x * (scale * scale * scale * dot_row / dim)
            esend.buf[0, at, :] = es[:, piece(ids_ref, 1, width)].astype(BF)
            esend.buf[1, at, :] = es[:, piece(ids_ref, 3, width)].astype(BF)
            esend.flush(slice(None), ds)
            ek0.buf[at, :] = es[:, piece(ids_ref, 0, width)]
            ek0.flush(ds)
            ek2.buf[at, :] = es[:, piece(ids_ref, 2, width)].astype(BF)
            ek2.flush(ds)
        both = jnp.where(iota((8, dim), 0) == 0, sums, g2_in()[...])
        gg_out.buf[...] = both
        esend.buf[0, count:, :] = gg_out.buf[:, piece(ids_ref, 1, width)].astype(BF)
        esend.buf[1, count:, :] = gg_out.buf[:, piece(ids_ref, 3, width)].astype(BF)
        esend.flush(slice(None), pl.ds(count, EXTRA))
        gg_out.flush()

    return call(
        body,
        ids,
        [(qkv, 1)]
        + [(a, 1) for a in a_parts]
        + [(a, 1) for a in (o, lse, start_row, cos, sin, w_qkv, x, gain, gg2)],
        [
            ((count, width), BF, blocks),
            ((count, 3 * width), BF, blocks),
            ((count, width), F32, blocks),
            ((count, width), BF, blocks),
            ((2, count + EXTRA, width), BF, blocks + 1),
            ((8, dim), F32, 1),
        ],
        scratch=[
            pltpu.VMEM((width, count), BF),
            pltpu.VMEM((count, width), F32),
            pltpu.VMEM((count, width), F32),
            pltpu.VMEM((BLK, dim), F32),
        ],
        mib=56,
        name="attention_backward",
    )


def halves(ids_ref, size):
    y = ids_ref[1] & 1
    keep = pl.ds(pl.multiple_of(y * size, size), size)
    send = pl.ds(pl.multiple_of((1 - y) * size, size), size)
    return keep, send


def weight_grads(ids, pairs, by_rows, name):
    count, dim = pairs[0][0].shape
    chunk = dim // 8
    lefts = []
    for left, _ in pairs:
        if not any(left is x for x in lefts):
            lefts.append(left)
    m = len(lefts)

    def body(ids_ref, ins, outs, scratch):
        (tmp,) = scratch
        z = ids_ref[1] >> 1
        keep, send = halves(ids_ref, chunk)
        for p, (left, right_) in enumerate(pairs):
            k = [left is x for x in lefts].index(True)
            right = ins[m + p]()[...]
            for half in range(2):
                part = ins[k]()[:, half * 4 * chunk : (half + 1) * 4 * chunk]
                full = tn(part, right) if by_rows else tn(right, part)
                for b in range(2):
                    rel = z ^ (2 * half + b)
                    low, high = rel & 1, rel >> 1
                    at = slice(b * 2 * chunk, (b + 1) * 2 * chunk)
                    if by_rows:
                        tmp[...] = full[at, :]
                        outs[2 * p + 1].buf[low, high] = tmp[send, :].astype(BF)
                        outs[2 * p].buf[low, high] = tmp[keep, :].astype(BF)
                    else:
                        tmp[...] = full[:, at]
                        outs[2 * p + 1].buf[low, high] = tmp[:, send].astype(BF)
                        outs[2 * p].buf[low, high] = tmp[:, keep].astype(BF)
            outs[2 * p + 1].flush()
            outs[2 * p].flush()

    outs = []
    for left, right in pairs:
        n = right.shape[1]
        outs += [((2, 2) + ((chunk, n) if by_rows else (n, chunk)), BF, 1)] * 2
    flat = call(
        body,
        ids,
        [(a, 1) for a in lefts] + [(r, 1) for _, r in pairs],
        outs,
        scratch=[pltpu.VMEM((2 * chunk, n) if by_rows else (n, 2 * chunk), F32)],
        name=name,
    )
    return [(flat[2 * p], flat[2 * p + 1]) for p in range(len(pairs))]


def down_grads(ids, hidden, near, far):
    count, units = hidden.shape
    two = near.shape[1]
    width = two // 2
    chunk = width // 2

    def body(ids_ref, ins, outs, scratch):
        h_in, a_in, b_in = ins
        keep_out, send_out = outs
        (tmp,) = scratch
        keep, send = halves(ids_ref, chunk)
        for low, ref in ((0, a_in), (1, b_in)):
            full = tn(h_in()[...], ref()[...])
            for high in range(2):
                tmp[...] = full[:, high * width : (high + 1) * width]
                rel = ids_ref[0] ^ (ids_ref[1] >> 1) ^ (low + 2 * high)
                send_out.buf[rel & 1, rel >> 1] = tmp[:, send].astype(BF)
                keep_out.buf[rel & 1, rel >> 1] = tmp[:, keep].astype(BF)
        send_out.flush()
        keep_out.flush()

    shape = (2, 2, units, chunk)
    return call(
        body,
        ids,
        [(hidden, 1), (near, 1), (far, 1)],
        [(shape, BF, 1)] * 2,
        scratch=[pltpu.VMEM((units, width), F32)],
        name="grads_down",
    )


def out_grads(ids, o_pieces, parts):
    count, width = o_pieces[0].shape
    half = width // 2

    def body(ids_ref, ins, outs, scratch):
        keep_out, send_out = outs
        (tmp,) = scratch
        keep, send = halves(ids_ref, half)
        total = ins[0]()[...]
        for p in ins[1:3]:
            total = total + p()[...].astype(F32)
        grad = total.astype(BF)
        for flip, o in enumerate(ins[3:]):
            tmp[...] = tn(o()[...], grad)
            rel = (ids_ref[1] >> 1) ^ flip
            send_out.buf[rel & 1, rel >> 1] = tmp[:, send].astype(BF)
            keep_out.buf[rel & 1, rel >> 1] = tmp[:, keep].astype(BF)
        send_out.flush()
        keep_out.flush()

    shape = (2, 2, width, half)
    return call(
        body,
        ids,
        [(p, 1) for p in parts] + [(o, 1) for o in o_pieces],
        [(shape, BF, 1)] * 2,
        scratch=[pltpu.VMEM((width, width), F32)],
        name="grads_out",
    )


def flip_dp(value, bit):
    n = lax.axis_size("dp")
    return lax.ppermute(value, "dp", [(d, d ^ bit) for d in range(n)])


def flip_tensor(value, bit):
    return lax.ppermute(value, "tensor", [(d, d ^ bit) for d in range(4)])


def tie(values, *others):
    return lax.optimization_barrier((values, others))[0]


def halve_sum(keep, got, first, second, third):
    total = keep.astype(F32) + tie(got, first).astype(F32)
    total = total[0] + tie(flip_dp(total[1].astype(BF), 2), second).astype(F32)
    return total[0] + tie(flip_dp(total[1].astype(BF), 4), third).astype(F32)


def gather_pieces(own):
    two = flip_tensor(own, 2)
    one = flip_tensor(own, 1)
    three = flip_tensor(two, 1)
    return (own, one, two, three)


def middle(keep2, got):
    return (keep2.astype(F32) + got[1].astype(F32)).astype(BF)


def pack_grads(ids, slot_row, parts, other, gains, n_dp):
    count, width = other.shape
    per = count // n_dp
    k = len(parts)

    def body(ids_ref, ins, outs, scratch):
        (out,) = outs
        gain = ins[k + 2]()[...].astype(F32)
        for r in ins[k + 3 :]:
            gain = gain + r()[...].astype(F32)
        gain = jnp.concatenate([gain.astype(BF)] * 2, axis=1)
        total = ins[1]()[0:count, :].astype(F32)
        for r in ins[2 : k + 1]:
            total = total + r()[0:count, :].astype(F32)
        both = jnp.concatenate([total.astype(BF), ins[k + 1]()[...]], axis=1)
        moved = tn(picks(ins[0]()[...], 0, count), both).astype(BF)
        for d in range(n_dp):
            out.buf[d, 0:per, :] = moved[d * per : (d + 1) * per, :]
            out.buf[d, per:, :] = gain
        out.flush()

    return call(
        body,
        ids,
        [(slot_row, 1)] + [(p, 1) for p in (*parts, other, *gains)],
        [((n_dp, per + EXTRA, 2 * width), BF, 1)],
        name="pack_grads",
    )[0]


def unpack_grads(ids, pos8, back):
    n_dp, padded, two = back.shape
    width = two // 2
    per = padded - EXTRA
    count = n_dp * per

    def body(ids_ref, ins, outs, scratch):
        a_out, b_out, gain_out = outs
        pos_in, back_in = ins
        picked = picks(pos_in()[0:1, :], 0, count)
        ref = back_in()
        moved = tn(picked, ref[:, 0:per, :].reshape(count, two)).astype(BF)
        a_out.buf[...] = moved[:, :width]
        a_out.flush()
        b_out.buf[...] = moved[:, width:]
        b_out.flush()
        total = ref[0, per:, 0:width].astype(F32)
        for d in range(1, n_dp):
            total = total + ref[d, per:, 0:width].astype(F32)
        gain_out.buf[...] = total
        gain_out.flush()

    return call(
        body,
        ids,
        [(pos8, 1), (back, 1)],
        [((count, width), BF, 1), ((count, width), BF, 1), ((EXTRA, width), F32, 1)],
        name="unpack_grads",
    )


def per_device(
    tokens,
    dealing,
    seq_ids,
    first_values,
    out_grad,
    norm1_gain,
    norm2_gain,
    w_query,
    w_key,
    w_value,
    w_out,
    w_gate,
    w_up,
    w_down,
):
    n_dp = lax.axis_size("dp")
    count, width = tokens.shape
    dim = norm1_gain.shape[0]
    per = count // n_dp
    t = lax.axis_index("tensor")
    d = lax.axis_index("dp")
    ids = jnp.stack([t, d]).astype(jnp.int32)
    gate_t, up_t = w_gate.T, w_up.T

    def exchange(packed):
        return lax.all_to_all(packed, "dp", split_axis=0, concat_axis=0, tiled=True)

    deal_row = dealing.reshape(1, count)
    sent, pos8 = pack_tokens(ids, deal_row, tokens, n_dp)
    arrived = exchange(sent)
    grad_far = flip_tensor(tie(out_grad, sent), 2)
    pos8 = tie(pos8, sent)
    first_sent = permuted(ids, pos8, [first_values], False, "pack_rows")
    first_sent = first_sent.reshape(n_dp, per, width)

    start = jnp.sum(seq_ids[None, :] < seq_ids[:, None], axis=1, dtype=jnp.int32)
    offset = (jnp.arange(count, dtype=jnp.int32) - start).astype(F32)
    half = HEAD_DIM // 2
    freqs = THETA ** (-jnp.arange(half, dtype=F32) / half)
    angles = offset[:, None] * freqs[None, :]
    reps = (1, width // HEAD_DIM)
    cos = jnp.tile(jnp.cos(angles), reps)
    sin = jnp.tile(jnp.sin(angles), reps)
    start_row = start.reshape(1, count)
    gain1 = norm1_gain.astype(F32).reshape(1, dim)
    gain2 = norm2_gain.astype(F32).reshape(1, dim)

    arrived = tie(arrived, first_sent, cos, sin, start_row, grad_far)
    pieces = gather_pieces(arrived)
    first_sent = tie(first_sent, pieces[1])
    firsts = exchange(first_sent)
    slots = (
        arrived[:, per, :per].astype(F32) * 32.0 + arrived[:, per + 1, :per].astype(F32)
    ).astype(jnp.int32)
    slot_row = slots.reshape(1, count)
    grad_near = tie(out_grad, slot_row)
    grad_sent = permuted(
        ids, pos8, [jnp.concatenate([grad_near, grad_far], axis=1)], False, "pack_rows"
    ).reshape(n_dp, per, 2 * width)
    near = exchange(tie(grad_sent, firsts))
    w_pieces = gather_pieces(tie(w_out, pieces[3]))

    x, normed1, qkv, attended, lse, w_qkv = qkv_attention(
        ids, tie(slot_row, grad_sent), pieces, firsts, cos, sin, gain1, w_query, w_key, w_value,
        start_row,
    )
    o_pieces = gather_pieces(attended)
    near = tie(near, attended).reshape(count, 2 * width)
    near = permuted(ids, slot_row, [near], False, "sort_rows")
    far = flip_tensor(near, 1)
    x1, normed2, fg, fu, hidden, yk0, yk2, ysend = feed_forward(
        ids, tie(x, near), o_pieces, w_pieces, gain2, gate_t, up_t, w_down
    )
    fast = n_dp == 8
    y_got = flip_tensor(ysend, 1)
    y_mid = middle(yk2, y_got)
    y_far = flip_tensor(y_mid, 2)
    x1 = tie(x1, y_mid)
    if fast:
        down_keep, down_send = down_grads(ids, hidden, near, far)
        down_got = flip_dp(down_send, 1)
        x1 = tie(x1, down_keep)
    dgate, dup, ak0, ak2, asend, dk0, dk2, dsend, gg2 = feed_backward(
        ids, x1, near, far, fg, fu, w_pieces, gain2, gate_t, up_t, w_down
    )
    asend = tie(asend, y_far)
    if fast:
        asend = tie(asend, down_got)
    a_got = flip_tensor(asend, 1)
    a_mid = middle(ak2, a_got)
    a_far = flip_tensor(a_mid, 2)
    d_got = flip_tensor(tie(dsend, a_mid), 1)

    def send_back(parts, name):
        packed = permuted(ids, slot_row, parts, True, name).reshape(n_dp, per, width)
        return exchange(packed).reshape(count, width)

    y_back = send_back([tie(yk0, a_mid), y_got[0], y_far], "return_rows")
    d_mid = middle(dk2, d_got)
    if fast:
        gup = tie((dgate, dup), a_mid)
        (gate_keep, gate_send), (up_keep, up_send) = weight_grads(
            ids, [(normed2, gup[0]), (normed2, gup[1])], False, "grads_mlp"
        )
        a_far = tie(a_far, gate_keep)
        gate_got = flip_dp(gate_send, 1)
    d_far = flip_tensor(tie(d_mid, a_far), 2)
    dvp, dqkv, ek0, ek2, esend, gg1 = attention_backward(
        ids, qkv, attended, lse, (ak0, a_got[0], tie(a_far, d_mid)), start_row, cos, sin, x,
        gain1, w_qkv, gg2,
    )
    if fast:
        esend = tie(esend, gate_got)
    e_got = flip_tensor(esend, 1)
    gains = [
        lax.dynamic_slice(gg1, (0, (t ^ flip) * width), (EXTRA, width)) for flip in (0, 2)
    ]
    e_mid = jnp.concatenate(
        [
            (ek2.astype(F32) + e_got[1, :count].astype(F32)).astype(BF),
            (gains[1] + e_got[1, count:].astype(F32)).astype(BF),
        ],
        axis=0,
    )
    e_far = flip_tensor(e_mid, 2)
    d_parts = (dk0, d_got[0], d_far)
    if fast:
        up_got = flip_dp(tie(up_send, gate_got), 1)
        ((att_keep, att_send),) = weight_grads(
            ids, [(normed1, tie(dqkv, e_mid))], True, "grads_qkv"
        )
        out_keep, out_send = out_grads(ids, o_pieces, (tie(dk0, e_mid), d_got[0], d_far))
        e_far = tie(e_far, att_keep, out_keep)
    i_sent = pack_grads(
        ids,
        slot_row,
        [ek0, e_got[0], e_far, *d_parts],
        dvp,
        [gains[0], e_got[0, count:], e_far[count:]],
        n_dp,
    )
    i_back = exchange(i_sent)

    if fast:
        att_got = flip_dp(tie(att_send, up_got), 1)
        out_got = flip_dp(out_send, 1)
        gw_down = halve_sum(down_keep, down_got, e_mid, e_mid, e_far)
        gw_gate = halve_sum(gate_keep, gate_got, att_keep, i_sent, i_sent).T
        gw_up = halve_sum(up_keep, up_got, i_sent, i_sent, i_sent).T
        gw_qkv = halve_sum(att_keep, att_got, i_sent, i_sent, i_sent)
        gw_q, gw_k, gw_v = jnp.split(gw_qkv, 3, axis=1)
        gw_out = halve_sum(out_keep, out_got, i_sent, i_sent, i_sent)
        gw_out = lax.ppermute(
            gw_out,
            ("dp", "tensor"),
            [
                ((2 * z + y) * 4 + r, (2 * r + y) * 4 + (r ^ z))
                for z in range(4)
                for y in range(2)
                for r in range(4)
            ],
        )
    else:

        def scattered(left, right, dim_):
            full = jnp.einsum("ta,tb->ab", left, right, preferred_element_type=F32)
            return lax.psum_scatter(full, "dp", scatter_dimension=dim_, tiled=True)

        def natural(parts):
            full = jnp.zeros((count, dim), BF)
            for flip, part in enumerate(parts):
                full = lax.dynamic_update_slice(full, part, (0, (t ^ flip) * width))
            return full

        dy = natural((near[:, :width], far[:, :width], near[:, width:], far[:, width:]))
        dx1 = (dk0 + d_got[0].astype(F32) + d_far.astype(F32)).astype(BF)
        dx1 = lax.all_gather(dx1, "tensor", axis=1, tiled=True)
        gw_gate = scattered(normed2, dgate, 0)
        gw_up = scattered(normed2, dup, 0)
        gw_down = scattered(hidden, dy, 1)
        gw_q, gw_k, gw_v = [scattered(normed1, p, 0) for p in jnp.split(dqkv, 3, axis=1)]
        gw_out = scattered(attended, dx1, 1)

    output = permuted(ids, pos8, [tie(y_back, i_sent)], True, "restore_rows")
    input_grad, first_grad, gain_rows = unpack_grads(ids, pos8, i_back)
    part = width // n_dp
    mine = lax.dynamic_slice(gain_rows, (0, d * part), (2, part))
    return (
        output,
        input_grad,
        first_grad,
        mine[0:1],
        mine[1:2],
        gw_q,
        gw_k,
        gw_v,
        gw_out,
        gw_gate,
        gw_up,
        gw_down,
    )


def solution(mesh):
    in_specs = (
        P("dp", "tensor"),
        P("dp"),
        P("dp"),
        P("dp", "tensor"),
        P("dp", "tensor"),
        P(),
        P(),
        P(None, "tensor"),
        P(None, "tensor"),
        P(None, "tensor"),
        P("tensor", None),
        P(None, "tensor"),
        P(None, "tensor"),
        P("tensor", None),
    )
    out_specs = (
        P("dp", "tensor"),
        P("dp", "tensor"),
        P("dp", "tensor"),
        P("tensor", "dp"),
        P("tensor", "dp"),
        P("dp", "tensor"),
        P("dp", "tensor"),
        P("dp", "tensor"),
        P("tensor", "dp"),
        P("dp", "tensor"),
        P("dp", "tensor"),
        P("tensor", "dp"),
    )
    return jax.shard_map(
        per_device, mesh=mesh, in_specs=in_specs, out_specs=out_specs, check_vma=False
    )
```

```python
import functools

import jax
import jax.numpy as jnp
from jax import lax
from jax.experimental import pallas as pl
from jax.experimental.pallas import tpu as pltpu
from jax.sharding import PartitionSpec as P

HEAD_DIM = 64
EPS = 1e-06
THETA = 10000.0
NEG = -1e30
BF = jnp.bfloat16
F32 = jnp.float32
BLK = 256
EXTRA = 8
MIB = 1 << 20


def nn(a, b):
    return lax.dot_general(a, b, (((1,), (0,)), ((), ())), preferred_element_type=F32)


def nt(a, b):
    return lax.dot_general(a, b, (((1,), (1,)), ((), ())), preferred_element_type=F32)


def tn(a, b):
    return lax.dot_general(a, b, (((0,), (0,)), ((), ())), preferred_element_type=F32)


def iota(shape, dim):
    return lax.broadcasted_iota(jnp.int32, shape, dim)


TIMES = {
    "pack_tokens": 3,
    "pack_rows": 3,
    "qkv_attention": 14,
    "feed_forward": 12,
    "sort_rows": 3,
    "grads_down": 5,
    "feed_backward": 15,
    "grads_mlp": 8,
    "return_rows": 3,
    "attention_backward": 17,
    "grads_att": 8,
    "pack_grads": 4,
    "unpack_grads": 4,
    "restore_rows": 3,
    "add_pairs": 3,
    "finish_attention": 2,
}


SCALE_F = 1_150_000_000 // 16
SCALE_B = 3_690_000 // 16


class Fetched:
    def __init__(self, src, buf, sems, base, parts):
        size = src.shape[0] // parts
        self.buf = buf
        self.copies = [
            pltpu.make_async_copy(
                src.at[pl.ds(p * size, size)], buf.at[pl.ds(p * size, size)], sems.at[base + p]
            )
            for p in range(parts)
        ]
        self.waited = [False] * parts

    def start(self):
        for c in self.copies:
            c.start()

    def __call__(self, part=None):
        for p in range(len(self.copies)) if part is None else (part,):
            if not self.waited[p]:
                self.copies[p].wait()
                self.waited[p] = True
        return self.buf


class Stored:
    def __init__(self, dst, buf, sems, base):
        self.dst, self.buf, self.sems, self.at = dst, buf, sems, base
        self.copies = []

    def flush(self, *index):
        src = self.buf.at[index] if index else self.buf
        dst = self.dst.at[index] if index else self.dst
        c = pltpu.make_async_copy(src, dst, self.sems.at[self.at + len(self.copies)])
        c.start()
        self.copies.append(c)


def call(body, ids, ins, outs, scratch=(), mib=48, name=None):
    took = TIMES[name]
    ins = [tuple(i) + (None, False)[len(i) - 2 :] for i in ins]
    n_in, n_out = len(ins), len(outs)
    in_at = [sum(i[1] for i in ins[:k]) for k in range(n_in + 1)]
    out_at = [sum(p for _, _, p in outs[:k]) for k in range(n_out + 1)]

    def kernel(ids_ref, *refs):
        srcs, refs = refs[:n_in], refs[n_in:]
        dsts, refs = refs[:n_out], refs[n_out:]
        bufs, refs = refs[:n_in], refs[n_in:]
        obufs, refs = refs[:n_out], refs[n_out:]
        in_sems, out_sems, refs = refs[0], refs[1], refs[2:]
        inputs = [
            Fetched(
                src if ins[k][2] is None else src.at[ins[k][2]], buf, in_sems, in_at[k], ins[k][1]
            )
            for k, (src, buf) in enumerate(zip(srcs, bufs))
        ]
        outputs = [
            Stored(dst, buf, out_sems, out_at[k]) for k, (dst, buf) in enumerate(zip(dsts, obufs))
        ]
        for i in inputs:
            i.start()
        body(ids_ref, inputs, outputs, refs)
        for i in inputs:
            i()
        for k, o in enumerate(outputs):
            assert len(o.copies) == outs[k][2]
            for c in o.copies:
                c.wait()

    return pl.pallas_call(
        kernel,
        out_shape=tuple(pltpu.HBM(s, d) for s, d, _ in outs),
        in_specs=[pl.BlockSpec(memory_space=pltpu.SMEM)]
        + [pl.BlockSpec(memory_space=pl.ANY)] * n_in,
        out_specs=tuple(pl.BlockSpec(memory_space=pl.ANY) for _ in outs),
        scratch_shapes=[
            pltpu.VMEM(a.shape if index is None else a.shape[1:], a.dtype) for a, _, index, _ in ins
        ]
        + [pltpu.VMEM(s, d) for s, d, _ in outs]
        + [pltpu.SemaphoreType.DMA((in_at[-1],)), pltpu.SemaphoreType.DMA((out_at[-1],))]
        + list(scratch),
        compiler_params=pltpu.CompilerParams(vmem_limit_bytes=mib * MIB),
        cost_estimate=pl.CostEstimate(
            flops=took * SCALE_F, transcendentals=0, bytes_accessed=took * SCALE_B
        ),
        name=name,
    )(
        ids,
        *[
            a if anywhere else pltpu.with_memory_space_constraint(a, pltpu.HBM)
            for a, _, _, anywhere in ins
        ],
    )


def given(array, index=None):
    return (array, 1, index, True)


def own_first(pieces):
    return [(pieces[0], 1)] + [given(p) for p in pieces[1:]]


def piece(ids_ref, flip, width):
    return pl.ds(pl.multiple_of((ids_ref[0] ^ flip) * width, width), width)


def picks(index, first, size):
    shape = (size, index.shape[1])
    return jnp.where(iota(shape, 0) + first == index, 1.0, 0.0).astype(BF)


def pack_tokens(ids, deal_row, tok, n_dp):
    count, width = tok.shape
    per = count // n_dp
    lanes = 128

    def body(ids_ref, ins, outs, scratch):
        deal_in, tok_in = ins
        out, pos_out = outs
        deal = deal_in()[...]
        dest = deal // count
        slot = deal % count
        oh = jnp.where(iota((n_dp, count), 0) == dest, 1.0, 0.0)
        upto = jnp.where(iota((lanes, lanes), 0) <= iota((lanes, lanes), 1), 1.0, 0.0)
        parts = [oh[:, b * lanes : (b + 1) * lanes] for b in range(count // lanes)]
        inner = nn(jnp.concatenate(parts, axis=0).astype(BF), upto.astype(BF))
        base = (iota((n_dp, 1), 0) * per - 1).astype(F32)
        rows_ = []
        for b, part in enumerate(parts):
            seen = inner[b * n_dp : (b + 1) * n_dp]
            rows_.append(jnp.sum(part * (seen + base), axis=0, keepdims=True))
            base = base + seen[:, lanes - 1 :]
        pos = jnp.concatenate(rows_, axis=1).astype(jnp.int32)
        pos_out.buf[...] = jnp.broadcast_to(pos, (8, count))
        pos_out.flush()
        high = jnp.broadcast_to(slot // 32, (8, count))
        low = jnp.broadcast_to(slot % 32, (8, count))
        hl = jnp.where(iota((8, count), 0) == 0, high, low).astype(F32).astype(BF)
        out.buf[:, per : per + EXTRA, :] = jnp.zeros((n_dp, EXTRA, width), BF)
        size = min(count, 512)
        group = size // per
        for g in range(count // size):
            pick = picks(pos, g * size, size)
            moved = nn(pick, tok_in()[...]).astype(BF)
            marks = nt(hl, pick).astype(BF)
            for e in range(group):
                d = g * group + e
                out.buf[d, 0:per, :] = moved[e * per : (e + 1) * per]
                out.buf[d, per : per + 8, 0:per] = marks[:, e * per : (e + 1) * per]
            out.flush(pl.ds(g * group, group))

    return call(
        body,
        ids,
        [(deal_row, 1), (tok, 1)],
        [
            ((n_dp, per + EXTRA, width), BF, count // min(count, 512)),
            ((8, count), jnp.int32, 1),
        ],
        name="pack_tokens",
    )


def sort_rows(ids, index, parts, name):
    count, width = parts[0][0].shape
    blocks = 2
    size = count // blocks

    def body(ids_ref, ins, outs, scratch):
        idx = ins[0]()[0:1, :]
        (out,) = outs
        for b in range(blocks):
            at = slice(b * size, (b + 1) * size)
            pick = picks(idx, b * size, size)
            for k, part in enumerate(ins[1:]):
                out.buf[at, k * width : (k + 1) * width] = nn(pick, part()[...]).astype(BF)
            out.flush(pl.ds(b * size, size))

    return call(
        body,
        ids,
        [(index, 1)] + parts,
        [((count, width * len(parts)), BF, blocks)],
        name=name,
    )[0]


def add_halves(keep, got, send_out, total_out):
    sums = keep[...].astype(F32) + got[...].astype(F32)
    send_out.buf[...] = sums[1].astype(BF)
    send_out.flush()
    total_out.buf[...] = sums[0]
    total_out.flush()


def return_rows(ids, index, parts, name, sums=()):
    count, width = parts[0][0].shape[-2:]
    m = 1 + len(parts)

    def body(ids_ref, ins, outs, scratch):
        total = ins[1]()[...]
        for r in ins[2:m]:
            total = total.astype(F32) + r()[...].astype(F32)
        outs[0].buf[...] = tn(picks(ins[0]()[0:1, :], 0, count), total.astype(BF)).astype(BF)
        outs[0].flush()
        for k in range(len(sums)):
            at = m + 2 * k
            add_halves(ins[at](), ins[at + 1](), outs[1 + 2 * k], outs[2 + 2 * k])

    outs = [((count, width), BF, 1)]
    ins = [(index, 1)] + parts
    for keep, got in sums:
        outs += [(keep.shape[1:], BF, 1), (keep.shape[1:], F32, 1)]
        ins += [(keep, 1), (got, 1)]
    return call(body, ids, ins, outs, name=name)


def restore_rows(ids, index, backs, name):
    count, width = backs[0].shape

    def body(ids_ref, ins, outs, scratch):
        pick = picks(ins[0]()[0:1, :], 0, count)
        both = tn(pick, jnp.concatenate([b()[...] for b in ins[1:]], axis=1)).astype(BF)
        for k, out in enumerate(outs):
            out.buf[...] = both[:, k * width : (k + 1) * width]
            out.flush()

    return call(
        body,
        ids,
        [(index, 1)] + [(b, 1) for b in backs],
        [((count, width), BF, 1)] * len(backs),
        name=name,
    )


def head_mask(shape, head, split):
    lane = iota(shape, 1)
    if split:
        return (lane % (shape[1] // 2)) // (HEAD_DIM // 2) == head
    return lane // HEAD_DIM == head


def split_perm(width):
    half = HEAD_DIM // 2
    src = iota((width, width), 0)
    dst = iota((width, width), 1)
    second = dst // (width // 2)
    rest = dst % (width // 2)
    want = (rest // half) * HEAD_DIM + second * half + rest % half
    return (src == want).astype(F32).astype(BF)


def qkv_attention(ids, slot_row, pieces, firsts, cos, sin, gain, wq, wk, wv, start_row):
    n_dp, padded, width = pieces[0].shape
    per = firsts.shape[1]
    count = n_dp * per
    dim = gain.shape[1]
    heads = width // HEAD_DIM
    blocks = count // BLK
    half = width // 2

    def body(ids_ref, ins, outs, scratch):
        slot_in, x0, x1, x2, x3, fv_in, wq_in, wk_in, wv_in, cos_in, sin_in, gain_in, start_in = ins
        x_out, n_out, qkv_out, o_out, lse_out, w_out = outs
        cat, vt = scratch
        slots = slot_in()[...]
        for flip, ref in enumerate((x0, x1, x2, x3)):
            cat[:, piece(ids_ref, flip, width)] = ref()[:, 0:per, :].reshape(count, width)
        cat[:, dim:] = fv_in()[...].reshape(count, width)
        sp = split_perm(width)
        w_out.buf[:, 0:width] = nn(wq_in()[...], sp).astype(BF)
        w_out.buf[:, width : 2 * width] = nn(wk_in()[...], sp).astype(BF)
        w_out.buf[:, 2 * width :] = wv_in()[...]
        w_out.flush()
        lse_out.buf[...] = jnp.zeros_like(lse_out.buf)

        def rope(v, c, s):
            a, b = v[:, :half], v[:, half:]
            return jnp.concatenate([a * c - b * s, b * c + a * s], axis=1).astype(BF)

        for j in range(blocks):
            at = slice(j * BLK, (j + 1) * BLK)
            ds = pl.ds(j * BLK, BLK)
            moved = nn(picks(slots, j * BLK, BLK), cat[...])
            x = moved[:, :dim]
            x_out.buf[at, :] = x.astype(BF)
            x_out.flush(ds)
            scale = lax.rsqrt(jnp.sum(x * x, axis=1, keepdims=True) / dim + EPS)
            normed = (x * scale * gain_in()[...].astype(F32)).astype(BF)
            n_out.buf[at, :] = normed
            n_out.flush(ds)
            qkv = nn(normed, w_out.buf[...])
            c, s = cos_in()[at, :], sin_in()[at, :]
            q = rope(qkv[:, 0:width], c, s)
            v = 0.5 * qkv[:, 2 * width :] + 0.5 * moved[:, dim:]
            q = (q.astype(F32) * HEAD_DIM ** (-0.5)).astype(BF)
            qkv_out.buf[at, 0:width] = q
            qkv_out.buf[at, width : 2 * width] = rope(qkv[:, width : 2 * width], c, s)
            qkv_out.buf[at, 2 * width :] = v.astype(BF)
            qkv_out.flush(ds)
            vt[:, at] = jnp.transpose(v).astype(BF)
            start = start_in()[:, at]
            n = (j + 1) * BLK
            keys = qkv_out.buf[0:n, width : 2 * width]
            key = iota((n, BLK), 0)
            valid = (key >= start) & (key <= iota((n, BLK), 1) + j * BLK)
            out = []
            for h in range(heads):
                qh = jnp.where(head_mask((BLK, width), h, True), q, jnp.zeros_like(q))
                sc = jnp.where(valid, nt(keys, qh), NEG)
                top = jnp.max(sc, axis=0, keepdims=True)
                ex = jnp.exp(sc - top)
                total = jnp.sum(ex, axis=0, keepdims=True)
                vals = vt[h * HEAD_DIM : (h + 1) * HEAD_DIM, 0:n]
                out.append(nn(vals, ex.astype(BF)) * (1.0 / total))
                lse_out.buf[h : h + 1, at] = top + jnp.log(total)
            o_out.buf[at, :] = jnp.transpose(jnp.concatenate(out, axis=0)).astype(BF)
            o_out.flush(ds)
        lse_out.flush()

    return call(
        body,
        ids,
        [(slot_row, 1)]
        + [given(p) for p in pieces]
        + [given(firsts)]
        + [(a, 1) for a in (wq, wk, wv, cos, sin, gain, start_row)],
        [
            ((count, dim), BF, blocks),
            ((count, dim), BF, blocks),
            ((count, 3 * width), BF, blocks),
            ((count, width), BF, blocks),
            ((8, count), F32, 1),
            ((dim, 3 * width), BF, 1),
        ],
        scratch=[pltpu.VMEM((count, dim + width), BF), pltpu.VMEM((width, count), BF)],
        name="qkv_attention",
    )


FEED = 512


def feed_forward(ids, x, o_pieces, w_pieces, gain, w_gate, w_up, w_down):
    count, dim = x.shape
    width = o_pieces[0].shape[1]
    units = w_gate.shape[0]
    size = min(FEED, count)
    blocks = count // size

    def body(ids_ref, ins, outs, scratch):
        w_ins, o_ins = ins[0:4], ins[4:8]
        x_in, gain_in, wg_in, wu_in, wd_in = ins[8:]
        x1_out, n_out, fg_out, fu_out, h_out, yk0, yk2, ysend = outs
        ys, xs, wo = scratch
        for k, w in enumerate(w_ins):
            wo[k * width : (k + 1) * width, :] = w()[...]
        for j in range(blocks):
            at = slice(j * size, (j + 1) * size)
            ds = pl.ds(j * size, size)
            heads = jnp.concatenate([o()[at, :] for o in o_ins], axis=1)
            x1 = x_in(j)[at, :].astype(F32) + nn(heads, wo[...])
            xs[...] = x1
            x1_out.buf[at, :] = x1.astype(BF)
            x1_out.flush(ds)
            scale = lax.rsqrt(jnp.sum(x1 * x1, axis=1, keepdims=True) / dim + EPS)
            normed = (x1 * scale * gain_in()[...].astype(F32)).astype(BF)
            n_out.buf[at, :] = normed
            n_out.flush(ds)
            g = nt(normed, wg_in()[...])
            u = nt(normed, wu_in()[...])
            sg = jax.nn.sigmoid(g)
            silu = g * sg
            hid = (silu * u).astype(BF)
            h_out.buf[at, :] = hid
            h_out.flush(ds)
            fu_out.buf[at, :] = silu.astype(BF)
            fu_out.flush(ds)
            fg_out.buf[at, :] = (u * sg * (1.0 + g * (1.0 - sg))).astype(BF)
            fg_out.flush(ds)
            ys[...] = nn(hid, wd_in()[...])
            ysend.buf[0, at, :] = ys[:, piece(ids_ref, 1, width)].astype(BF)
            ysend.buf[1, at, :] = ys[:, piece(ids_ref, 3, width)].astype(BF)
            ysend.flush(slice(None), ds)
            own = piece(ids_ref, 0, width)
            yk0.buf[at, :] = ys[:, own] + xs[:, own]
            yk0.flush(ds)
            yk2.buf[at, :] = ys[:, piece(ids_ref, 2, width)].astype(BF)
            yk2.flush(ds)

    return call(
        body,
        ids,
        own_first(w_pieces)
        + own_first(o_pieces)
        + [(x, blocks), (gain, 1), (w_gate, 1), (w_up, 1), (w_down, 1)],
        [
            ((count, dim), BF, blocks),
            ((count, dim), BF, blocks),
            ((count, units), BF, blocks),
            ((count, units), BF, blocks),
            ((count, units), BF, blocks),
            ((count, width), F32, blocks),
            ((count, width), BF, blocks),
            ((2, count, width), BF, blocks),
        ],
        scratch=[
            pltpu.VMEM((size, dim), F32),
            pltpu.VMEM((size, dim), F32),
            pltpu.VMEM((4 * width, dim), BF),
        ],
        mib=60,
        name="feed_forward",
    )


def feed_backward(ids, x1, near, far, fg, fu, w_pieces, gain, w_gate, w_up, w_down):
    count, dim = x1.shape
    width = w_pieces[0].shape[0]
    units = w_gate.shape[0]
    size = min(FEED, count)
    blocks = count // size

    def body(ids_ref, ins, outs, scratch):
        wd_in, near_in, far_in, fg_in, fu_in, wg_in, wu_in, x1_in, gain_in = ins[:9]
        w_ins = ins[9:]
        dg_out, du_out, ak0, ak2, asend, dk0, dk2, dsend, gg_out = outs
        ds_, ys, wo = scratch
        sums = jnp.zeros((1, dim), F32)
        for j in range(blocks):
            at = slice(j * size, (j + 1) * size)
            ds = pl.ds(j * size, size)
            near_, far_ = near_in(j)[at, :], far_in(j)[at, :]
            ys[:, piece(ids_ref, 0, width)] = near_[:, :width]
            ys[:, piece(ids_ref, 2, width)] = near_[:, width:]
            ys[:, piece(ids_ref, 1, width)] = far_[:, :width]
            ys[:, piece(ids_ref, 3, width)] = far_[:, width:]
            dy = ys[...]
            dh = nt(dy, wd_in()[...])
            dg = (dh * fg_in(j)[at, :].astype(F32)).astype(BF)
            du = (dh * fu_in(j)[at, :].astype(F32)).astype(BF)
            dg_out.buf[at, :] = dg
            du_out.buf[at, :] = du
            dg_out.flush(ds)
            du_out.flush(ds)
            dn = nn(dg, wg_in()[...]) + nn(du, wu_in()[...])
            x1 = x1_in(j)[at, :].astype(F32)
            scale = lax.rsqrt(jnp.sum(x1 * x1, axis=1, keepdims=True) / dim + EPS)
            sums = sums + jnp.sum(dn * (x1 * scale), axis=0, keepdims=True)
            z = dn * gain_in()[...].astype(F32)
            dot_row = jnp.sum(z * x1, axis=1, keepdims=True)
            part = scale * z - x1 * (scale * scale * scale * dot_row / dim)
            part = part + 0.25 * dy.astype(F32)
            ds_[...] = part
            if j == 0:
                for k, w in enumerate(w_ins):
                    wo[k * width : (k + 1) * width, :] = w()[...]
            da = nt(part.astype(BF), wo[...])
            asend.buf[0, at, :] = da[:, width : 2 * width].astype(BF)
            asend.buf[1, at, :] = da[:, 3 * width :].astype(BF)
            asend.flush(slice(None), ds)
            ak0.buf[at, :] = da[:, 0:width]
            ak0.flush(ds)
            ak2.buf[at, :] = da[:, 2 * width : 3 * width].astype(BF)
            ak2.flush(ds)
            dsend.buf[0, at, :] = ds_[:, piece(ids_ref, 1, width)].astype(BF)
            dsend.buf[1, at, :] = ds_[:, piece(ids_ref, 3, width)].astype(BF)
            dsend.flush(slice(None), ds)
            dk0.buf[at, :] = ds_[:, piece(ids_ref, 0, width)]
            dk0.flush(ds)
            dk2.buf[at, :] = ds_[:, piece(ids_ref, 2, width)].astype(BF)
            dk2.flush(ds)
        gg_out.buf[...] = jnp.broadcast_to(sums, (8, dim))
        gg_out.flush()

    return call(
        body,
        ids,
        [(w_down, 1), (near, blocks), (far, blocks, None, True), (fg, blocks), (fu, blocks)]
        + [(w_gate, 1), (w_up, 1), (x1, blocks), (gain, 1)]
        + own_first(w_pieces),
        [
            ((count, units), BF, blocks),
            ((count, units), BF, blocks),
            ((count, width), F32, blocks),
            ((count, width), BF, blocks),
            ((2, count, width), BF, blocks),
            ((count, width), F32, blocks),
            ((count, width), BF, blocks),
            ((2, count, width), BF, blocks),
            ((8, dim), F32, 1),
        ],
        scratch=[
            pltpu.VMEM((size, dim), F32),
            pltpu.VMEM((size, dim), BF),
            pltpu.VMEM((4 * width, dim), BF),
        ],
        mib=60,
        name="feed_backward",
    )


def attention_backward(ids, qkv, o, lse, a_parts, start_row, cos, sin, x, gain, w_qkv, gg2):
    count, width = o.shape
    dim = x.shape[1]
    heads = width // HEAD_DIM
    blocks = count // BLK
    half = width // 2
    part = HEAD_DIM // 2

    def body(ids_ref, ins, outs, scratch):
        qkv_in, a0, a1, a2, o_in, lse_in, start_in, cos_in, sin_in, w_in, x_in, gain_in, g2_in = ins
        dv_out, dqkv_out, ek0, ek2, esend = outs
        kt, dk, dv, es = scratch
        qkv_ref = qkv_in()
        for b in range(blocks):
            at = slice(b * BLK, (b + 1) * BLK)
            kt[:, at] = jnp.transpose(qkv_ref[at, width : 2 * width].astype(F32)).astype(BF)
        sums = jnp.zeros((1, dim), F32)
        pick = (iota((8, width), 1) // HEAD_DIM == iota((8, width), 0)).astype(F32)
        sp = split_perm(width)

        def rope_back(g, c, s):
            a, b = g[:, :half], g[:, half:]
            return jnp.concatenate([a * c + b * s, b * c - a * s], axis=1).astype(BF)

        for j in reversed(range(blocks)):
            at = slice(j * BLK, (j + 1) * BLK)
            ds = pl.ds(j * BLK, BLK)
            q = qkv_ref[at, 0:width]
            do = (a0()[at, :] + a1()[at, :].astype(F32) + a2()[at, :].astype(F32)).astype(BF)
            prod = do.astype(F32) * o_in()[at, :].astype(F32)
            delta = lax.dot_general(
                pick, prod, (((1,), (1,)), ((), ())),
                precision=lax.Precision.HIGHEST, preferred_element_type=F32,
            )
            start = start_in()[:, at]
            lse = lse_in()[:, at]
            n = (j + 1) * BLK
            keys = qkv_ref[0:n, width : 2 * width]
            vals = qkv_ref[0:n, 2 * width :]
            key = iota((n, BLK), 0)
            valid = (key >= start) & (key <= iota((n, BLK), 1) + j * BLK)
            probs, grads, q_heads, do_heads = [], [], [], []
            first, second = [], []
            for h in range(heads):
                qh = jnp.where(head_mask((BLK, width), h, True), q, jnp.zeros_like(q))
                dh = jnp.where(head_mask((BLK, width), h, False), do, jnp.zeros_like(do))
                sc = jnp.where(valid, nt(keys, qh) - lse[h : h + 1, :], NEG)
                pr = jnp.exp(sc)
                dsc = (pr * (nt(vals, dh) - delta[h : h + 1, :])).astype(BF)
                probs.append(pr.astype(BF))
                grads.append(dsc)
                q_heads.append(qh)
                do_heads.append(dh)
                kh = jnp.concatenate(
                    [
                        kt[h * part : (h + 1) * part, 0:n],
                        kt[half + h * part : half + (h + 1) * part, 0:n],
                    ],
                    axis=0,
                )
                dqh = nn(kh, dsc)
                first.append(dqh[:part])
                second.append(dqh[part:])
            dvn = nn(jnp.concatenate(probs, 1), jnp.concatenate(do_heads, 0))
            dkn = nn(jnp.concatenate(grads, 1), jnp.concatenate(q_heads, 0))
            if j == blocks - 1:
                dv[...] = dvn
                dk[...] = dkn
            else:
                dv[0:n, :] += dvn
                dk[0:n, :] += dkn
            dqj = jnp.transpose(jnp.concatenate(first + second, axis=0)) * HEAD_DIM ** (-0.5)
            c, s = cos_in()[at, :], sin_in()[at, :]
            dqp = rope_back(dqj, c, s)
            dkp = rope_back(dk[at, :], c, s)
            dvp = (0.5 * dv[at, :].astype(BF).astype(F32)).astype(BF)
            dv_out.buf[at, :] = dvp
            dv_out.flush(ds)
            dqkv_out.buf[at, 0:width] = nt(dqp, sp).astype(BF)
            dqkv_out.buf[at, width : 2 * width] = nt(dkp, sp).astype(BF)
            dqkv_out.buf[at, 2 * width :] = dvp
            dqkv_out.flush(ds)
            dn = nt(jnp.concatenate([dqp, dkp, dvp], axis=1), w_in()[...])
            x = x_in()[at, :].astype(F32)
            scale = lax.rsqrt(jnp.sum(x * x, axis=1, keepdims=True) / dim + EPS)
            sums = sums + jnp.sum(dn * (x * scale), axis=0, keepdims=True)
            z = dn * gain_in()[...].astype(F32)
            dot_row = jnp.sum(z * x, axis=1, keepdims=True)
            es[...] = scale * z - x * (scale * scale * scale * dot_row / dim)
            esend.buf[0, at, :] = es[:, piece(ids_ref, 1, width)].astype(BF)
            esend.buf[1, at, :] = es[:, piece(ids_ref, 3, width)].astype(BF)
            esend.flush(slice(None), ds)
            ek0.buf[at, :] = es[:, piece(ids_ref, 0, width)]
            ek0.flush(ds)
            ek2.buf[at, :] = es[:, piece(ids_ref, 2, width)].astype(BF)
            ek2.flush(ds)
        last = pl.ds(count, EXTRA)
        es[0:8, :] = jnp.where(iota((8, dim), 0) == 0, sums, g2_in()[...])
        esend.buf[0, count:, :] = es[0:8, piece(ids_ref, 1, width)].astype(BF)
        esend.buf[1, count:, :] = es[0:8, piece(ids_ref, 3, width)].astype(BF)
        esend.flush(slice(None), last)
        ek0.buf[count:, :] = es[0:8, piece(ids_ref, 0, width)]
        ek0.flush(last)
        ek2.buf[count:, :] = es[0:8, piece(ids_ref, 2, width)].astype(BF)
        ek2.flush(last)

    return call(
        body,
        ids,
        [(qkv, 1)]
        + a_parts
        + [(a, 1) for a in (o, lse, start_row, cos, sin, w_qkv, x, gain, gg2)],
        [
            ((count, width), BF, blocks),
            ((count, 3 * width), BF, blocks),
            ((count + EXTRA, width), F32, blocks + 1),
            ((count + EXTRA, width), BF, blocks + 1),
            ((2, count + EXTRA, width), BF, blocks + 1),
        ],
        scratch=[
            pltpu.VMEM((width, count), BF),
            pltpu.VMEM((count, width), F32),
            pltpu.VMEM((count, width), F32),
            pltpu.VMEM((BLK, dim), F32),
        ],
        mib=56,
        name="attention_backward",
    )


def halves(ids_ref, size):
    y = ids_ref[1] & 1
    keep = pl.ds(pl.multiple_of(y * size, size), size)
    send = pl.ds(pl.multiple_of((1 - y) * size, size), size)
    return keep, send


def put_chunks(ids_ref, tmp, full, rel, size, keep_buf, send_buf, at):
    keep, send = halves(ids_ref, size)
    rows_ = slice(at, at + full.shape[0])
    tmp[0 : full.shape[0], :] = full
    low, high = rel & 1, rel >> 1
    keep_buf[low, high, rows_, :] = tmp[0 : full.shape[0], keep].astype(BF)
    send_buf[low, high, rows_, :] = tmp[0 : full.shape[0], send].astype(BF)


def put_low(ids_ref, tmp, full, rel, size, buf, at):
    keep, send = halves(ids_ref, size)
    rows_ = slice(at, at + full.shape[0])
    tmp[0 : full.shape[0], :] = full
    low, high = rel & 1, rel >> 1
    buf[low, 0, high, rows_, :] = tmp[0 : full.shape[0], keep].astype(BF)
    buf[low, 1, high, rows_, :] = tmp[0 : full.shape[0], send].astype(BF)


def mlp_grads(ids, left, first, second, sums):
    count, dim = left.shape
    chunk = dim // 8
    units = first.shape[1]

    def body(ids_ref, ins, outs, scratch):
        left_in, first_in, second_in = ins[:3]
        send1, keep1, send2, keep2, send_sum, total = outs
        tmp, buf = scratch
        z = ids_ref[1] >> 1
        for right, low_first in ((first_in, False), (second_in, True)):
            for half in range(2):
                part = left_in()[:, half * 4 * chunk : (half + 1) * 4 * chunk]
                full = tn(right()[...], part)
                for b in range(2):
                    one = full[:, b * 2 * chunk : (b + 1) * 2 * chunk]
                    rel = z ^ (2 * half + b)
                    if low_first:
                        put_low(ids_ref, tmp, one, rel, chunk, buf, 0)
                    else:
                        put_chunks(ids_ref, tmp, one, rel, chunk, keep1.buf, send1.buf, 0)
            if low_first:
                send2.buf[...] = buf[1]
                send2.flush()
                keep2.buf[...] = buf[0]
                keep2.flush()
            else:
                send1.flush()
                keep1.flush()
        for k in range(len(sums)):
            at = slice(k * size, (k + 1) * size)
            both = ins[3 + 2 * k]()[...] + ins[4 + 2 * k]()[...].astype(F32)
            send_sum.buf[at, :] = both[1].astype(BF)
            total.buf[at, :] = both[0]
        send_sum.flush()
        total.flush()

    shape = (2, 2, units, chunk)
    size = sums[0][0].shape[1]
    added = (size * len(sums), chunk)
    return call(
        body,
        ids,
        [(left, 1), (first, 1), (second, 1)] + [(a, 1) for pair in sums for a in pair],
        [(shape, BF, 1)] * 4 + [(added, BF, 1), (added, F32, 1)],
        scratch=[
            pltpu.VMEM((units, 2 * chunk), F32),
            pltpu.VMEM((2, 2, 2, units, chunk), BF),
        ],
        name="grads_mlp",
    )


def attention_grads(ids, left, right, o_pieces, parts):
    count, dim = left.shape
    chunk = dim // 8
    three = right.shape[1]
    width = three // 3
    two = 2 * width

    def body(ids_ref, ins, outs, scratch):
        left_in, right_in, o_ins, p_ins = ins[0], ins[1], ins[2:6], ins[6:9]
        send1, keep1, send2, keep2 = outs[:4]
        tmp, buf = scratch
        z = ids_ref[1] >> 1
        for half in range(2):
            part = left_in()[:, half * 4 * chunk : (half + 1) * 4 * chunk]
            full = tn(right_in()[...], part)
            for b in range(2):
                cols = slice(b * 2 * chunk, (b + 1) * 2 * chunk)
                rel = z ^ (2 * half + b)
                put_chunks(ids_ref, tmp, full[:two, cols], rel, chunk, keep1.buf, send1.buf, 0)
                put_low(ids_ref, tmp, full[two:, cols], rel, chunk, buf, 0)
        send1.flush()
        keep1.flush()
        total = p_ins[0]()[...]
        for p in p_ins[1:]:
            total = total + p()[...].astype(F32)
        grad = total.astype(BF)
        for flip, o in enumerate(o_ins):
            put_low(ids_ref, tmp, tn(o()[...], grad), z ^ flip, chunk, buf, width)
        send2.buf[...] = buf[1]
        send2.flush()
        keep2.buf[...] = buf[0]
        keep2.flush()
    shape = (2, 2, two, chunk)
    return call(
        body,
        ids,
        [(left, 1), (right, 1)] + [(o, 1) for o in o_pieces] + parts,
        [(shape, BF, 1)] * 4,
        scratch=[
            pltpu.VMEM((two, 2 * chunk), F32),
            pltpu.VMEM((2, 2, 2, two, chunk), BF),
        ],
        name="grads_att",
    )


def down_grads(ids, hidden, near, far):
    count, units = hidden.shape
    two = near.shape[1]
    width = two // 2
    chunk = width // 2
    half = units // 2

    def body(ids_ref, ins, outs, scratch):
        h_in, a_in, b_in = ins
        send1, keep1, send2, keep2 = outs
        tmp, buf = scratch
        for low, ref in ((0, a_in), (1, b_in)):
            full = tn(h_in()[...], ref()[...])
            for high in range(2):
                one = full[:, high * width : (high + 1) * width]
                rel = ids_ref[0] ^ (ids_ref[1] >> 1) ^ (low + 2 * high)
                put_chunks(ids_ref, tmp, one[:half], rel, chunk, keep1.buf, send1.buf, 0)
                put_low(ids_ref, tmp, one[half:], rel, chunk, buf, 0)
        send1.flush()
        keep1.flush()
        send2.buf[...] = buf[1]
        send2.flush()
        keep2.buf[...] = buf[0]
        keep2.flush()

    shape = (2, 2, half, chunk)
    return call(
        body,
        ids,
        [(hidden, 1), (near, 1), given(far)],
        [(shape, BF, 1)] * 4,
        scratch=[pltpu.VMEM((half, width), F32), pltpu.VMEM((2, 2, 2, half, chunk), BF)],
        name="grads_down",
    )


def add_pairs(ids, sums, name):
    def body(ids_ref, ins, outs, scratch):
        for k in range(len(sums)):
            add_halves(ins[2 * k](), ins[2 * k + 1](), outs[2 * k], outs[2 * k + 1])

    outs, ins = [], []
    for keep, got in sums:
        outs += [(keep.shape[1:], BF, 1), (keep.shape[1:], F32, 1)]
        ins += [(keep, 1), (got, 1)]
    return call(body, ids, ins, outs, name=name)


def flip_dp(value, bit):
    n = lax.axis_size("dp")
    return lax.ppermute(value, "dp", [(d, d ^ bit) for d in range(n)])


def flip_tensor(value, bit):
    return lax.ppermute(value, "tensor", [(d, d ^ bit) for d in range(4)])


def tie(values, *others):
    return lax.optimization_barrier((values, others))[0]


def gather_pieces(own, *others):
    two = flip_tensor(own, 2)
    one = flip_tensor(own, 1)
    three = flip_tensor(tie(two, *others) if others else two, 1)
    return (own, one, two, three)


def middle(keep2, got):
    return (keep2.astype(F32) + got[1].astype(F32)).astype(BF)


def pack_grads(ids, slot_row, parts, others, last, n_dp):
    count, width = last.shape
    per = count // n_dp
    k, m = len(parts), len(others)

    def body(ids_ref, ins, outs, scratch):
        (out,) = outs
        total = ins[k + 1]()[...].astype(F32)
        for r in ins[k + 2 : k + m + 1]:
            total = total + r()[...].astype(F32)
        gain = ins[1]()[count:, :].astype(F32)
        total = total + ins[1]()[0:count, :].astype(F32)
        for r in ins[2 : k + 1]:
            total = total + r()[0:count, :].astype(F32)
            gain = gain + r()[count:, :].astype(F32)
        gain = jnp.concatenate([gain.astype(BF)] * 2, axis=1)
        both = jnp.concatenate([total.astype(BF), ins[-1]()[...]], axis=1)
        packed = tn(picks(ins[0]()[...], 0, count), both).astype(BF)
        for d in range(n_dp):
            out.buf[d, 0:per, :] = packed[d * per : (d + 1) * per, :]
            out.buf[d, per:, :] = gain
        out.flush()

    return call(
        body,
        ids,
        [(slot_row, 1)] + parts + others + [(last, 1)],
        [((n_dp, per + EXTRA, 2 * width), BF, 1)],
        name="pack_grads",
    )[0]


def unpack_grads(ids, pos8, back):
    n_dp, padded, two = back.shape
    width = two // 2
    part = width // n_dp
    per = padded - EXTRA
    count = n_dp * per

    def body(ids_ref, ins, outs, scratch):
        a_out, b_out, gain_out = outs
        picked = picks(ins[0]()[0:1, :], 0, count)
        ref = ins[1]()
        both = tn(picked, ref[:, 0:per, :].reshape(count, two)).astype(BF)
        a_out.buf[...] = both[:, :width]
        a_out.flush()
        b_out.buf[...] = both[:, width:]
        b_out.flush()
        total = ref[0, per:, 0:width].astype(F32)
        for d in range(1, n_dp):
            total = total + ref[d, per:, 0:width].astype(F32)
        own = iota((width, part), 1) + ids_ref[1] * part
        pick = jnp.where(iota((width, part), 0) == own, 1.0, 0.0)
        gain_out.buf[...] = lax.dot_general(
            total, pick, (((1,), (0,)), ((), ())),
            precision=lax.Precision.HIGHEST, preferred_element_type=F32,
        )
        gain_out.flush()

    return call(
        body,
        ids,
        [(pos8, 1), given(back)],
        [((count, width), BF, 1), ((count, width), BF, 1), ((EXTRA, part), F32, 1)],
        name="unpack_grads",
    )


def finish_attention(ids, qk_total, vo_total, got):
    two, chunk = qk_total.shape[1:]
    width = two // 2

    def body(ids_ref, ins, outs, scratch):
        q_out, k_out, v_out, o_out = outs
        qk, vo, add = ins[0](), ins[1](), ins[2]()
        o_out.buf[...] = vo[width:, :] + add[two + width :, :].astype(F32)
        o_out.flush()
        for out, ref, at, off in ((q_out, qk, 0, 0), (k_out, qk, width, 0), (v_out, vo, 0, two)):
            total = ref[at : at + width, :] + add[off + at : off + at + width, :].astype(F32)
            out.buf[...] = jnp.transpose(total)
            out.flush()

    return call(
        body,
        ids,
        [(qk_total, 1, 0), (vo_total, 1, 0), given(got)],
        [((chunk, width), F32, 1)] * 3 + [((width, chunk), F32, 1)],
        name="finish_attention",
    )


def per_device(
    tokens,
    dealing,
    seq_ids,
    first_values,
    out_grad,
    norm1_gain,
    norm2_gain,
    w_query,
    w_key,
    w_value,
    w_out,
    w_gate,
    w_up,
    w_down,
):
    n_dp = lax.axis_size("dp")
    count, width = tokens.shape
    dim = norm1_gain.shape[0]
    per = count // n_dp
    t = lax.axis_index("tensor")
    d = lax.axis_index("dp")
    ids = jnp.stack([t, d]).astype(jnp.int32)
    gate_t, up_t = w_gate.T, w_up.T

    def exchange(packed):
        return lax.all_to_all(packed, "dp", split_axis=0, concat_axis=0, tiled=True)

    deal_row = dealing.reshape(1, count)
    sent, pos8 = pack_tokens(ids, deal_row, tokens, n_dp)
    arrived = exchange(sent)
    grad_far = flip_tensor(tie(out_grad, sent), 2)
    pos8 = tie(pos8, sent)
    first_sent = sort_rows(ids, pos8, [(first_values, 1)], "pack_rows")
    first_sent = first_sent.reshape(n_dp, per, width)

    start = jnp.sum(seq_ids[None, :] < seq_ids[:, None], axis=1, dtype=jnp.int32)
    offset = (jnp.arange(count, dtype=jnp.int32) - start).astype(F32)
    half = HEAD_DIM // 2
    freqs = THETA ** (-jnp.arange(half, dtype=F32) / half)
    angles = offset[:, None] * jnp.tile(freqs, width // HEAD_DIM)[None, :]
    cos = jnp.cos(angles)
    sin = jnp.sin(angles)
    start_row = start.reshape(1, count)
    gain1 = norm1_gain.reshape(1, dim)
    gain2 = norm2_gain.reshape(1, dim)

    arrived = tie(arrived, first_sent, cos, sin, start_row, grad_far, gain1, gain2)
    slots = (
        arrived[:, per, :per].astype(F32) * 32.0 + arrived[:, per + 1, :per].astype(F32)
    ).astype(jnp.int32)
    slot_row = slots.reshape(1, count)
    grad_near = tie(out_grad, slot_row)
    grad_sent = sort_rows(ids, pos8, [(grad_near, 1), given(grad_far)], "pack_rows")
    grad_sent = grad_sent.reshape(n_dp, per, 2 * width)
    pieces = gather_pieces(arrived, grad_sent)
    firsts = exchange(tie(first_sent, pieces[1]))
    near = exchange(tie(grad_sent, firsts, pieces[2]))
    w_pieces = gather_pieces(tie(w_out, pieces[2]))

    x, normed1, qkv, attended, lse, w_qkv = qkv_attention(
        ids, tie(slot_row, grad_sent), pieces, firsts, cos, sin, gain1, w_query, w_key, w_value,
        start_row,
    )
    near = tie(near, attended).reshape(count, 2 * width)
    near = sort_rows(ids, slot_row, [given(near)], "sort_rows")
    far = flip_tensor(near, 1)
    o_pieces = gather_pieces(attended, near)
    x1, normed2, fg, fu, hidden, yk0, yk2, ysend = feed_forward(
        ids, x, o_pieces, w_pieces, gain2, gate_t, up_t, w_down
    )
    fast = n_dp == 8
    y_got = flip_tensor(ysend, 1)
    early, sums = (), []
    if fast:
        da_send, da_keep, db_send, db_keep = down_grads(ids, hidden, near, far)
        early = (flip_dp(da_send, 1), flip_dp(db_send, 2))
        sums = [(da_keep, early[0]), (db_keep, early[1])]
        yk2 = tie(yk2, da_keep)
    y_mid = middle(yk2, y_got)
    y_far = flip_tensor(y_mid, 2)
    dgate, dup, ak0, ak2, asend, dk0, dk2, dsend, gg2 = feed_backward(
        ids, tie(x1, y_mid), near, far, fg, fu, w_pieces, gain2, gate_t, up_t, w_down
    )
    a_got = flip_tensor(tie(asend, y_far, *early), 1)
    y_sent, *down_sums = return_rows(
        ids,
        slot_row,
        [(tie(yk0, ak0), 1), (y_got, 1, 0), (y_far, 1)],
        "return_rows",
        sums,
    )
    a_mid = middle(tie(ak2, y_sent), a_got)
    a_far = flip_tensor(a_mid, 2)
    y_back = exchange(tie(y_sent, a_mid).reshape(n_dp, per, width)).reshape(count, width)
    d_got = flip_tensor(tie(dsend, a_mid), 1)
    d_mid = middle(dk2, d_got)
    early = ()
    if fast:
        da_send, da_total, db_send, db_total = down_sums
        da_got = flip_dp(tie(da_send, a_mid), 2)
        db_got = flip_dp(tie(db_send, a_mid), 1)
        dgate, dup = tie((dgate, dup), a_mid)
        gate_send, gate_keep, up_send, up_keep, down_send, down_sum = mlp_grads(
            ids, normed2, dgate, dup, [(da_total, da_got), (db_total, db_got)]
        )
        a_far = tie(a_far, gate_keep)
        gate_got = flip_dp(gate_send, 1)
        up_got = flip_dp(up_send, 2)
        down_got = flip_dp(down_send, 4)
        early = (gate_got, up_got, down_got)
    a_far = tie(a_far, d_mid)
    d_far = flip_tensor(tie(d_mid, a_far), 2)
    dvp, dqkv, ek0, ek2, esend = attention_backward(
        ids, qkv, attended, lse, [(ak0, 1), given(a_got, 0), given(a_far)], start_row, cos, sin, x,
        gain1, w_qkv, gg2,
    )
    e_got = flip_tensor(tie(esend, d_far, y_back, *early), 1)
    if fast:
        gate_send, gate_total, up_send, up_total = add_pairs(
            ids, [(tie(gate_keep, ek2), gate_got), (up_keep, up_got)], "add_pairs"
        )
        ek2 = tie(ek2, gate_send)
    e_mid = middle(ek2, e_got)
    e_far = flip_tensor(e_mid, 2)
    d_parts = [(dk0, 1), (d_got, 1, 0), (d_far, 1)]
    if fast:
        gate_got = flip_dp(tie(gate_send, e_mid), 2)
        up_got = flip_dp(tie(up_send, e_mid), 1)
        qk_send, qk_keep, vo_send, vo_keep = attention_grads(
            ids, normed1, tie(dqkv, e_mid), o_pieces, d_parts
        )
        qk_got = flip_dp(qk_send, 1)
        vo_got = flip_dp(vo_send, 2)

        def plus(keep, got, *after):
            return keep.astype(F32) + tie(got, *after).astype(F32)

        gate_total = plus(gate_total, gate_got, qk_keep)
        up_total = plus(up_total, up_got, qk_keep)
        mlp_send = jnp.concatenate([gate_total[1], up_total[1]], axis=0).astype(BF)
        mlp_keep = jnp.concatenate([gate_total[0], up_total[0]], axis=0)
        e_far = tie(e_far, mlp_send)
        mlp_got = flip_dp(mlp_send, 4)
    i_sent = pack_grads(
        ids, slot_row, [(ek0, 1), given(e_got, 0), given(e_far)], d_parts, dvp, n_dp
    )
    i_back = exchange(i_sent)
    (output,) = restore_rows(ids, pos8, [tie(y_back, i_sent)], "restore_rows")
    input_grad, first_grad, gain_rows = unpack_grads(ids, pos8, i_back)
    if fast:
        units = w_down.shape[0]
        mlp_total = plus(mlp_keep, mlp_got, output)
        qk_total = plus(qk_keep, qk_got, output)
        vo_total = plus(vo_keep, vo_got, output)
        qk_total = plus(qk_total[0], flip_dp(qk_total[1].astype(BF), 2))
        vo_total = plus(vo_total[0], flip_dp(vo_total[1].astype(BF), 1))
        att_got = flip_dp(jnp.concatenate([qk_total[1], vo_total[1]], axis=0).astype(BF), 4)
        gw_q, gw_k, gw_v, gw_out = finish_attention(
            ids, qk_total, vo_total, tie(att_got, input_grad)
        )
        gw_down = plus(down_sum, down_got, i_sent)
        gw_gate, gw_up = mlp_total[:units].T, mlp_total[units:].T
        gw_out = lax.ppermute(
            gw_out,
            ("dp", "tensor"),
            [
                ((2 * z + y) * 4 + r, (2 * r + y) * 4 + (r ^ z))
                for z in range(4)
                for y in range(2)
                for r in range(4)
            ],
        )
    else:

        def scattered(left, right, dim_):
            full = jnp.einsum("ta,tb->ab", left, right, preferred_element_type=F32)
            return lax.psum_scatter(full, "dp", scatter_dimension=dim_, tiled=True)

        def natural(parts):
            full = jnp.zeros((count, dim), BF)
            for flip, part in enumerate(parts):
                full = lax.dynamic_update_slice(full, part, (0, (t ^ flip) * width))
            return full

        dy = natural((near[:, :width], far[:, :width], near[:, width:], far[:, width:]))
        dx1 = (dk0 + d_got[0].astype(F32) + d_far.astype(F32)).astype(BF)
        dx1 = lax.all_gather(dx1, "tensor", axis=1, tiled=True)
        gw_gate = scattered(normed2, dgate, 0)
        gw_up = scattered(normed2, dup, 0)
        gw_down = scattered(hidden, dy, 1)
        gw_q, gw_k, gw_v = [scattered(normed1, p, 0) for p in jnp.split(dqkv, 3, axis=1)]
        gw_out = scattered(attended, dx1, 1)

    return (
        output,
        input_grad,
        first_grad,
        gain_rows[0:1],
        gain_rows[1:2],
        gw_q,
        gw_k,
        gw_v,
        gw_out,
        gw_gate,
        gw_up,
        gw_down,
    )


def solution(mesh):
    in_specs = (
        P("dp", "tensor"),
        P("dp"),
        P("dp"),
        P("dp", "tensor"),
        P("dp", "tensor"),
        P(),
        P(),
        P(None, "tensor"),
        P(None, "tensor"),
        P(None, "tensor"),
        P("tensor", None),
        P(None, "tensor"),
        P(None, "tensor"),
        P("tensor", None),
    )
    out_specs = (
        P("dp", "tensor"),
        P("dp", "tensor"),
        P("dp", "tensor"),
        P("tensor", "dp"),
        P("tensor", "dp"),
        P("dp", "tensor"),
        P("dp", "tensor"),
        P("dp", "tensor"),
        P("tensor", "dp"),
        P("dp", "tensor"),
        P("dp", "tensor"),
        P("tensor", "dp"),
    )
    return jax.shard_map(
        per_device, mesh=mesh, in_specs=in_specs, out_specs=out_specs, check_vma=False
    )
```

```python
import functools

import jax
import jax.numpy as jnp
from jax import lax
from jax.experimental import pallas as pl
from jax.experimental.pallas import tpu as pltpu
from jax.sharding import PartitionSpec as P

HEAD_DIM = 64
EPS = 1e-06
THETA = 10000.0
NEG = -1e30
BF = jnp.bfloat16
F32 = jnp.float32
BLK = 256
EXTRA = 8
MIB = 1 << 20


def nn(a, b):
    return lax.dot_general(a, b, (((1,), (0,)), ((), ())), preferred_element_type=F32)


def nt(a, b):
    return lax.dot_general(a, b, (((1,), (1,)), ((), ())), preferred_element_type=F32)


def tn(a, b):
    return lax.dot_general(a, b, (((0,), (0,)), ((), ())), preferred_element_type=F32)


def iota(shape, dim):
    return lax.broadcasted_iota(jnp.int32, shape, dim)


TIMES = {
    "pack_tokens": 3,
    "pack_rows": 3,
    "qkv_attention": 14,
    "feed_forward": 12,
    "sort_rows": 3,
    "grads_down": 5,
    "feed_backward": 15,
    "grads_mlp": 8,
    "return_rows": 3,
    "attention_backward": 17,
    "grads_att": 8,
    "pack_grads": 4,
    "unpack_grads": 4,
    "restore_rows": 3,
    "add_pairs": 3,
    "finish_attention": 2,
}


SCALE_F = 1_150_000_000 // 16
SCALE_B = 3_690_000 // 16


class Fetched:
    def __init__(self, src, buf, sems, base, parts):
        self.buf = buf
        size = src.shape[0] // parts if parts else 0
        self.copies = [
            pltpu.make_async_copy(
                src.at[pl.ds(p * size, size)], buf.at[pl.ds(p * size, size)], sems.at[base + p]
            )
            for p in range(parts)
        ]
        self.waited = [False] * parts

    def __call__(self, part=None):
        one = part is not None and len(self.copies) > 1
        for p in (part,) if one else range(len(self.copies)):
            if not self.waited[p]:
                self.copies[p].wait()
                self.waited[p] = True
        return self.buf


class Stored:
    def __init__(self, dst, buf, sems, base):
        self.dst, self.buf, self.sems, self.at = dst, buf, sems, base
        self.copies = []

    def flush(self, *index):
        if self.sems is None:
            return
        src = self.buf.at[index] if index else self.buf
        dst = self.dst.at[index] if index else self.dst
        c = pltpu.make_async_copy(src, dst, self.sems.at[self.at + len(self.copies)])
        c.start()
        self.copies.append(c)


def call(body, ids, ins, outs, scratch=(), mib=28, name=None, ahead=()):
    ins = [tuple(i) + (None,)[len(i) - 2 :] for i in ins]
    took = TIMES[name]
    n_in, n_out = len(ins), len(outs)
    in_at = [sum(i[1] for i in ins[:k]) for k in range(n_in + 1)]
    out_at = [sum(o[2] for o in outs[:k]) for k in range(n_out + 1)]
    stored = [k for k in range(n_out) if outs[k][2] != HOLD]
    fetched = [k for k in range(n_in) if ins[k][1] != HOLD]
    n_ahead = len(ahead)

    def kernel(ids_ref, *refs):
        srcs, refs = refs[:n_in], refs[n_in:]
        early, refs = refs[:n_ahead], refs[n_ahead:]
        dsts, refs = refs[:n_out], refs[n_out:]
        late, refs = refs[:n_ahead], refs[n_ahead:]
        bufs, refs = refs[: len(fetched)], refs[len(fetched) :]
        obufs, refs = refs[: len(stored)], refs[len(stored) :]
        in_sems, out_sems, refs = refs[0], refs[1], refs[2:]
        srcs = [src if i[2] is None else src.at[i[2]] for src, i in zip(srcs, ins)]
        inputs = [Fetched(None, src, None, 0, 0) for src in srcs]
        for k, buf in zip(fetched, bufs):
            inputs[k] = Fetched(srcs[k], buf, in_sems, in_at[k], ins[k][1])
        outputs = [Stored(None, dst, None, 0) for dst in dsts]
        for k, buf in zip(stored, obufs):
            outputs[k] = Stored(dsts[k], buf, out_sems, out_at[k])
        for p in range(max(i[1] for i in ins)):
            for i in inputs:
                if p < len(i.copies):
                    i.copies[p].start()
        copies = [
            pltpu.make_async_copy(a, b, in_sems.at[in_at[-1] + k])
            for k, (a, b) in enumerate(zip(early, late))
        ]
        for c in copies:
            c.start()
        body(ids_ref, inputs, outputs, refs)
        for i in inputs:
            i()
        for k in stored:
            assert len(outputs[k].copies) == outs[k][2]
            for c in outputs[k].copies:
                c.wait()
        for c in copies:
            c.wait()

    return pl.pallas_call(
        kernel,
        out_shape=tuple(
            (pltpu.HBM if k in stored else pltpu.VMEM)(s, d) for k, (s, d, _) in enumerate(outs)
        )
        + tuple(pltpu.VMEM(a.shape, a.dtype) for a in ahead),
        in_specs=[pl.BlockSpec(memory_space=pltpu.SMEM)]
        + [
            pl.BlockSpec(memory_space=pl.ANY if k in fetched else pltpu.VMEM) for k in range(n_in)
        ]
        + [pl.BlockSpec(memory_space=pl.ANY)] * n_ahead,
        out_specs=tuple(
            pl.BlockSpec(memory_space=pl.ANY if k in stored else pltpu.VMEM) for k in range(n_out)
        )
        + tuple(pl.BlockSpec(memory_space=pltpu.VMEM) for _ in ahead),
        scratch_shapes=[
            pltpu.VMEM(a.shape if index is None else a.shape[1:], a.dtype)
            for a, _, index in (ins[k] for k in fetched)
        ]
        + [pltpu.VMEM(outs[k][0], outs[k][1]) for k in stored]
        + [
            pltpu.SemaphoreType.DMA((max(in_at[-1] + n_ahead, 1),)),
            pltpu.SemaphoreType.DMA((max(out_at[-1], 1),)),
        ]
        + list(scratch),
        compiler_params=pltpu.CompilerParams(vmem_limit_bytes=mib * MIB),
        cost_estimate=pl.CostEstimate(
            flops=took * SCALE_F, transcendentals=0, bytes_accessed=took * SCALE_B
        ),
        name=name,
    )(
        ids,
        *[
            pltpu.with_memory_space_constraint(a, pltpu.VMEM if parts == HOLD else pltpu.HBM)
            for a, parts, _ in ins
        ],
        *[pltpu.with_memory_space_constraint(a, pltpu.HBM) for a in ahead],
    )


HOLD = 0


def given(array, index=None):
    return (array, HOLD, index)


def own_first(pieces, parts=1):
    return [(pieces[0], parts)] + [given(p) for p in pieces[1:]]


def piece(ids_ref, flip, width):
    return pl.ds(pl.multiple_of((ids_ref[0] ^ flip) * width, width), width)


def picks(index, first, size):
    shape = (size, index.shape[1])
    return jnp.where(iota(shape, 0) + first == index, 1.0, 0.0).astype(BF)


def pack_tokens(ids, deal_row, tok, n_dp):
    count, width = tok.shape
    per = count // n_dp
    lanes = 128

    def body(ids_ref, ins, outs, scratch):
        deal_in, tok_in = ins
        out, pos_out = outs
        deal = deal_in()[...]
        dest = deal // count
        slot = deal % count
        oh = jnp.where(iota((n_dp, count), 0) == dest, 1.0, 0.0)
        upto = jnp.where(iota((lanes, lanes), 0) <= iota((lanes, lanes), 1), 1.0, 0.0)
        parts = [oh[:, b * lanes : (b + 1) * lanes] for b in range(count // lanes)]
        inner = nn(jnp.concatenate(parts, axis=0).astype(BF), upto.astype(BF))
        base = (iota((n_dp, 1), 0) * per - 1).astype(F32)
        rows_ = []
        for b, part in enumerate(parts):
            seen = inner[b * n_dp : (b + 1) * n_dp]
            rows_.append(jnp.sum(part * (seen + base), axis=0, keepdims=True))
            base = base + seen[:, lanes - 1 :]
        pos = jnp.concatenate(rows_, axis=1).astype(jnp.int32)
        pos_out.buf[...] = jnp.broadcast_to(pos, (8, count))
        pos_out.flush()
        high = jnp.broadcast_to(slot // 32, (8, count))
        low = jnp.broadcast_to(slot % 32, (8, count))
        hl = jnp.where(iota((8, count), 0) == 0, high, low).astype(F32).astype(BF)
        out.buf[:, per : per + EXTRA, :] = jnp.zeros((n_dp, EXTRA, width), BF)
        size = min(count, 512)
        group = size // per
        for g in range(count // size):
            pick = picks(pos, g * size, size)
            moved = nn(pick, tok_in()[...]).astype(BF)
            marks = nt(hl, pick).astype(BF)
            for e in range(group):
                d = g * group + e
                out.buf[d, 0:per, :] = moved[e * per : (e + 1) * per]
                out.buf[d, per : per + 8, 0:per] = marks[:, e * per : (e + 1) * per]
            out.flush(pl.ds(g * group, group))

    return call(
        body,
        ids,
        [(deal_row, 1), (tok, 1)],
        [
            ((n_dp, per + EXTRA, width), BF, HOLD),
            ((8, count), jnp.int32, 1),
        ],
        name="pack_tokens",
    )


def sort_rows(ids, index, parts, name, ahead=()):
    count, width = parts[0][0].shape
    blocks = 2
    size = count // blocks

    def body(ids_ref, ins, outs, scratch):
        idx = ins[0]()[0:1, :]
        (out,) = outs
        for b in range(blocks):
            at = slice(b * size, (b + 1) * size)
            pick = picks(idx, b * size, size)
            for k, part in enumerate(ins[1:]):
                out.buf[at, k * width : (k + 1) * width] = nn(pick, part()[...]).astype(BF)
            out.flush(pl.ds(b * size, size))

    return call(
        body,
        ids,
        [(index, 1)] + parts,
        [((count, width * len(parts)), BF, HOLD)],
        name=name,
        ahead=ahead,
    )


def add_halves(keep, got, send_out, total_out):
    sums = keep[...].astype(F32) + got[...].astype(F32)
    send_out.buf[...] = sums[1].astype(BF)
    send_out.flush()
    total_out.buf[...] = sums[0]
    total_out.flush()


def return_rows(ids, index, parts, name, sums=()):
    count, width = parts[0][0].shape[-2:]
    m = 1 + len(parts)

    def body(ids_ref, ins, outs, scratch):
        total = ins[1]()[...]
        for r in ins[2:m]:
            total = total.astype(F32) + r()[...].astype(F32)
        outs[0].buf[...] = tn(picks(ins[0]()[0:1, :], 0, count), total.astype(BF)).astype(BF)
        outs[0].flush()
        for k in range(len(sums)):
            at = m + 2 * k
            add_halves(ins[at](), ins[at + 1](), outs[1 + 2 * k], outs[2 + 2 * k])

    outs = [((count, width), BF, HOLD)]
    ins = [(index, 1)] + parts
    for keep, got in sums:
        outs += [(keep.shape[1:], BF, HOLD), (keep.shape[1:], F32, 1)]
        ins += [(keep, 1), (got, 1)]
    return call(body, ids, ins, outs, name=name)


def restore_rows(ids, index, backs, name):
    count, width = backs[0].shape

    def body(ids_ref, ins, outs, scratch):
        pick = picks(ins[0]()[0:1, :], 0, count)
        both = tn(pick, jnp.concatenate([b()[...] for b in ins[1:]], axis=1)).astype(BF)
        for k, out in enumerate(outs):
            out.buf[...] = both[:, k * width : (k + 1) * width]
            out.flush()

    return call(
        body,
        ids,
        [(index, 1)] + [(b, 1) for b in backs],
        [((count, width), BF, 1)] * len(backs),
        name=name,
    )


def head_mask(shape, head, split):
    lane = iota(shape, 1)
    if split:
        return (lane % (shape[1] // 2)) // (HEAD_DIM // 2) == head
    return lane // HEAD_DIM == head


def split_perm(width):
    half = HEAD_DIM // 2
    src = iota((width, width), 0)
    dst = iota((width, width), 1)
    second = dst // (width // 2)
    rest = dst % (width // 2)
    want = (rest // half) * HEAD_DIM + second * half + rest % half
    return (src == want).astype(F32).astype(BF)


def qkv_attention(ids, slot_row, pieces, firsts, cos, sin, gain, wq, wk, wv, start_row):
    n_dp, padded, width = pieces[0].shape
    per = firsts.shape[1]
    count = n_dp * per
    dim = gain.shape[1]
    heads = width // HEAD_DIM
    blocks = count // BLK
    half = width // 2

    def body(ids_ref, ins, outs, scratch):
        slot_in, x0, x1, x2, x3, fv_in, wq_in, wk_in, wv_in, cos_in, sin_in, gain_in, start_in = ins
        x_out, n_out, qkv_out, o_out, lse_out, w_out = outs
        cat, vt = scratch
        slots = slot_in()[...]
        for flip, ref in enumerate((x0, x1, x2, x3)):
            cat[:, piece(ids_ref, flip, width)] = ref()[:, 0:per, :].reshape(count, width)
        cat[:, dim:] = fv_in()[...].reshape(count, width)
        sp = split_perm(width)
        w_out.buf[:, 0:width] = nn(wq_in()[...], sp).astype(BF)
        w_out.buf[:, width : 2 * width] = nn(wk_in()[...], sp).astype(BF)
        w_out.buf[:, 2 * width :] = wv_in()[...]
        w_out.flush()
        lse_out.buf[...] = jnp.zeros_like(lse_out.buf)

        def rope(v, c, s):
            a, b = v[:, :half], v[:, half:]
            return jnp.concatenate([a * c - b * s, b * c + a * s], axis=1).astype(BF)

        for j in range(blocks):
            at = slice(j * BLK, (j + 1) * BLK)
            ds = pl.ds(j * BLK, BLK)
            moved = nn(picks(slots, j * BLK, BLK), cat[...])
            x = moved[:, :dim]
            x_out.buf[at, :] = x.astype(BF)
            x_out.flush(ds)
            scale = lax.rsqrt(jnp.sum(x * x, axis=1, keepdims=True) / dim + EPS)
            normed = (x * scale * gain_in()[...].astype(F32)).astype(BF)
            n_out.buf[at, :] = normed
            n_out.flush(ds)
            qkv = nn(normed, w_out.buf[...])
            c, s = cos_in(j)[at, :], sin_in(j)[at, :]
            q = rope(qkv[:, 0:width], c, s)
            v = 0.5 * qkv[:, 2 * width :] + 0.5 * moved[:, dim:]
            q = (q.astype(F32) * HEAD_DIM ** (-0.5)).astype(BF)
            qkv_out.buf[at, 0:width] = q
            qkv_out.buf[at, width : 2 * width] = rope(qkv[:, width : 2 * width], c, s)
            qkv_out.buf[at, 2 * width :] = v.astype(BF)
            qkv_out.flush(ds)
            vt[:, at] = jnp.transpose(v).astype(BF)
            start = start_in()[:, at]
            n = (j + 1) * BLK
            keys = qkv_out.buf[0:n, width : 2 * width]
            key = iota((n, BLK), 0)
            valid = (key >= start) & (key <= iota((n, BLK), 1) + j * BLK)
            out = []
            for h in range(heads):
                qh = jnp.where(head_mask((BLK, width), h, True), q, jnp.zeros_like(q))
                sc = jnp.where(valid, nt(keys, qh), NEG)
                top = jnp.max(sc, axis=0, keepdims=True)
                ex = jnp.exp(sc - top)
                total = jnp.sum(ex, axis=0, keepdims=True)
                vals = vt[h * HEAD_DIM : (h + 1) * HEAD_DIM, 0:n]
                out.append(nn(vals, ex.astype(BF)) * (1.0 / total))
                lse_out.buf[h : h + 1, at] = top + jnp.log(total)
            o_out.buf[at, :] = jnp.transpose(jnp.concatenate(out, axis=0)).astype(BF)
            o_out.flush(ds)
        lse_out.flush()

    return call(
        body,
        ids,
        [(slot_row, 1)]
        + [given(p) for p in pieces]
        + [given(firsts)]
        + [(wq, 1), (wk, 1), (wv, 1), (cos, 1), (sin, 1), (gain, 1), (start_row, 1)],
        [
            ((count, dim), BF, blocks),
            ((count, dim), BF, blocks),
            ((count, 3 * width), BF, blocks),
            ((count, width), BF, HOLD),
            ((8, count), F32, 1),
            ((dim, 3 * width), BF, 1),
        ],
        scratch=[pltpu.VMEM((count, dim + width), BF), pltpu.VMEM((width, count), BF)],
        name="qkv_attention",
    )


FEED = 512


def feed_forward(ids, x, o_pieces, w_pieces, gain, w_gate, w_up, w_down):
    count, dim = x.shape
    width = o_pieces[0].shape[1]
    units = w_gate.shape[0]
    size = min(FEED, count)
    blocks = count // size

    def body(ids_ref, ins, outs, scratch):
        w_ins, o_ins = ins[0:4], ins[4:8]
        x_in, gain_in, wg_in, wu_in, wd_in = ins[8:]
        x1_out, n_out, fg_out, fu_out, h_out, yk0, yk2, ysend = outs
        ys, xs, wo = scratch
        for k, w in enumerate(w_ins):
            wo[k * width : (k + 1) * width, :] = w()[...]
        for j in range(blocks):
            at = slice(j * size, (j + 1) * size)
            ds = pl.ds(j * size, size)
            heads = jnp.concatenate([o(j)[at, :] for o in o_ins], axis=1)
            x1 = x_in(j)[at, :].astype(F32) + nn(heads, wo[...])
            xs[...] = x1
            x1_out.buf[at, :] = x1.astype(BF)
            x1_out.flush(ds)
            scale = lax.rsqrt(jnp.sum(x1 * x1, axis=1, keepdims=True) / dim + EPS)
            normed = (x1 * scale * gain_in()[...].astype(F32)).astype(BF)
            n_out.buf[at, :] = normed
            n_out.flush(ds)
            g = nt(normed, wg_in()[...])
            u = nt(normed, wu_in()[...])
            sg = jax.nn.sigmoid(g)
            silu = g * sg
            hid = (silu * u).astype(BF)
            h_out.buf[at, :] = hid
            h_out.flush(ds)
            fu_out.buf[at, :] = silu.astype(BF)
            fu_out.flush(ds)
            fg_out.buf[at, :] = (u * sg * (1.0 + g * (1.0 - sg))).astype(BF)
            fg_out.flush(ds)
            ys[...] = nn(hid, wd_in()[...])
            ysend.buf[0, at, :] = ys[:, piece(ids_ref, 1, width)].astype(BF)
            ysend.buf[1, at, :] = ys[:, piece(ids_ref, 3, width)].astype(BF)
            ysend.flush(slice(None), ds)
            own = piece(ids_ref, 0, width)
            yk0.buf[at, :] = (ys[:, own] + xs[:, own]).astype(BF)
            yk0.flush(ds)
            yk2.buf[at, :] = ys[:, piece(ids_ref, 2, width)].astype(BF)
            yk2.flush(ds)

    return call(
        body,
        ids,
        [(w, 1) for w in w_pieces]
        + own_first(o_pieces)
        + [given(x), (gain, 1), given(w_gate), given(w_up), given(w_down)],
        [
            ((count, dim), BF, HOLD),
            ((count, dim), BF, blocks),
            ((count, units), BF, HOLD),
            ((count, units), BF, HOLD),
            ((count, units), BF, HOLD),
            ((count, width), BF, blocks),
            ((count, width), BF, HOLD),
            ((2, count, width), BF, HOLD),
        ],
        scratch=[
            pltpu.VMEM((size, dim), F32),
            pltpu.VMEM((size, dim), F32),
            pltpu.VMEM((4 * width, dim), BF),
        ],
        mib=44,
        name="feed_forward",
    )


def feed_backward(ids, x1, near, far, fg, fu, w_pieces, gain, w_gate, w_up, w_down):
    count, dim = x1.shape
    width = w_pieces[0].shape[0]
    units = w_gate.shape[0]
    size = min(FEED, count)
    blocks = count // size

    def body(ids_ref, ins, outs, scratch):
        wd_in, near_in, far_in, fg_in, fu_in, x1_in, wg_in, wu_in, gain_in = ins[:9]
        w_ins = ins[9:]
        dg_out, du_out, ak0, ak2, asend, dk0, dk2, dsend, gg_out = outs
        ds_, ys, wo = scratch
        sums = jnp.zeros((1, dim), F32)
        for j in range(blocks):
            at = slice(j * size, (j + 1) * size)
            ds = pl.ds(j * size, size)
            near_, far_ = near_in(j)[at, :], far_in(j)[at, :]
            ys[:, piece(ids_ref, 0, width)] = near_[:, :width]
            ys[:, piece(ids_ref, 2, width)] = near_[:, width:]
            ys[:, piece(ids_ref, 1, width)] = far_[:, :width]
            ys[:, piece(ids_ref, 3, width)] = far_[:, width:]
            dy = ys[...]
            dh = nt(dy, wd_in()[...])
            dg = (dh * fg_in(j)[at, :].astype(F32)).astype(BF)
            du = (dh * fu_in(j)[at, :].astype(F32)).astype(BF)
            dg_out.buf[at, :] = dg
            du_out.buf[at, :] = du
            dg_out.flush(ds)
            du_out.flush(ds)
            dn = nn(dg, wg_in()[...]) + nn(du, wu_in()[...])
            x1 = x1_in(j)[at, :].astype(F32)
            scale = lax.rsqrt(jnp.sum(x1 * x1, axis=1, keepdims=True) / dim + EPS)
            sums = sums + jnp.sum(dn * (x1 * scale), axis=0, keepdims=True)
            z = dn * gain_in()[...].astype(F32)
            dot_row = jnp.sum(z * x1, axis=1, keepdims=True)
            part = scale * z - x1 * (scale * scale * scale * dot_row / dim)
            part = part + 0.25 * dy.astype(F32)
            ds_[...] = part
            if j == 0:
                for k, w in enumerate(w_ins):
                    wo[k * width : (k + 1) * width, :] = w()[...]
            da = nt(part.astype(BF), wo[...])
            asend.buf[0, at, :] = da[:, width : 2 * width].astype(BF)
            asend.buf[1, at, :] = da[:, 3 * width :].astype(BF)
            asend.flush(slice(None), ds)
            ak0.buf[at, :] = da[:, 0:width].astype(BF)
            ak0.flush(ds)
            ak2.buf[at, :] = da[:, 2 * width : 3 * width].astype(BF)
            ak2.flush(ds)
            dsend.buf[0, at, :] = ds_[:, piece(ids_ref, 1, width)].astype(BF)
            dsend.buf[1, at, :] = ds_[:, piece(ids_ref, 3, width)].astype(BF)
            dsend.flush(slice(None), ds)
            dk0.buf[at, :] = ds_[:, piece(ids_ref, 0, width)].astype(BF)
            dk0.flush(ds)
            dk2.buf[at, :] = ds_[:, piece(ids_ref, 2, width)].astype(BF)
            dk2.flush(ds)
        gg_out.buf[...] = jnp.broadcast_to(sums, (8, dim))
        gg_out.flush()

    return call(
        body,
        ids,
        [(w_down, 1)]
        + [given(a) for a in (near, far, fg, fu, x1)]
        + [(w_gate, 1), (w_up, 1), (gain, 1)]
        + [(w, 1) for w in w_pieces],
        [
            ((count, units), BF, HOLD),
            ((count, units), BF, HOLD),
            ((count, width), BF, blocks),
            ((count, width), BF, HOLD),
            ((2, count, width), BF, HOLD),
            ((count, width), BF, blocks),
            ((count, width), BF, HOLD),
            ((2, count, width), BF, HOLD),
            ((8, dim), F32, 1),
        ],
        scratch=[
            pltpu.VMEM((size, dim), F32),
            pltpu.VMEM((size, dim), BF),
            pltpu.VMEM((4 * width, dim), BF),
        ],
        mib=44,
        name="feed_backward",
    )


def attention_backward(
    ids, qkv, o, lse, a_parts, start_row, cos, sin, x, gain, w_qkv, gg2
):
    count, width = o.shape
    dim = x.shape[1]
    heads = width // HEAD_DIM
    blocks = count // BLK
    half = width // 2
    part = HEAD_DIM // 2

    def body(ids_ref, ins, outs, scratch):
        qkv_in, a0, a1, a2, o_in, lse_in, start_in, cos_in, sin_in, w_in, x_in, gain_in, g2_in = ins
        dv_out, dqkv_out, ek0, ek2, esend = outs
        kt, dk, dv, es = scratch
        qkv_ref = qkv_in()
        for b in range(blocks):
            at = slice(b * BLK, (b + 1) * BLK)
            kt[:, at] = jnp.transpose(qkv_ref[at, width : 2 * width].astype(F32)).astype(BF)
        sums = jnp.zeros((1, dim), F32)
        pick = (iota((8, width), 1) // HEAD_DIM == iota((8, width), 0)).astype(F32)
        sp = split_perm(width)

        def rope_back(g, c, s):
            a, b = g[:, :half], g[:, half:]
            return jnp.concatenate([a * c + b * s, b * c - a * s], axis=1).astype(BF)

        for j in reversed(range(blocks)):
            at = slice(j * BLK, (j + 1) * BLK)
            ds = pl.ds(j * BLK, BLK)
            q = qkv_ref[at, 0:width]
            do = (a0(j)[at, :].astype(F32) + a1(j)[at, :].astype(F32) + a2(j)[at, :].astype(F32)).astype(BF)
            prod = do.astype(F32) * o_in(j)[at, :].astype(F32)
            delta = lax.dot_general(
                pick, prod, (((1,), (1,)), ((), ())),
                precision=lax.Precision.HIGHEST, preferred_element_type=F32,
            )
            start = start_in()[:, at]
            lse = lse_in()[:, at]
            n = (j + 1) * BLK
            keys = qkv_ref[0:n, width : 2 * width]
            vals = qkv_ref[0:n, 2 * width :]
            key = iota((n, BLK), 0)
            valid = (key >= start) & (key <= iota((n, BLK), 1) + j * BLK)
            probs, grads, q_heads, do_heads = [], [], [], []
            first, second = [], []
            for h in range(heads):
                qh = jnp.where(head_mask((BLK, width), h, True), q, jnp.zeros_like(q))
                dh = jnp.where(head_mask((BLK, width), h, False), do, jnp.zeros_like(do))
                sc = jnp.where(valid, nt(keys, qh) - lse[h : h + 1, :], NEG)
                pr = jnp.exp(sc)
                dsc = (pr * (nt(vals, dh) - delta[h : h + 1, :])).astype(BF)
                probs.append(pr.astype(BF))
                grads.append(dsc)
                q_heads.append(qh)
                do_heads.append(dh)
                kh = jnp.concatenate(
                    [
                        kt[h * part : (h + 1) * part, 0:n],
                        kt[half + h * part : half + (h + 1) * part, 0:n],
                    ],
                    axis=0,
                )
                dqh = nn(kh, dsc)
                first.append(dqh[:part])
                second.append(dqh[part:])
            dvn = nn(jnp.concatenate(probs, 1), jnp.concatenate(do_heads, 0))
            dkn = nn(jnp.concatenate(grads, 1), jnp.concatenate(q_heads, 0))
            if j == blocks - 1:
                dv[...] = dvn
                dk[...] = dkn
            else:
                dv[0:n, :] += dvn
                dk[0:n, :] += dkn
            dqj = jnp.transpose(jnp.concatenate(first + second, axis=0)) * HEAD_DIM ** (-0.5)
            c, s = cos_in(j)[at, :], sin_in(j)[at, :]
            dqp = rope_back(dqj, c, s)
            dkp = rope_back(dk[at, :], c, s)
            dvp = (0.5 * dv[at, :].astype(BF).astype(F32)).astype(BF)
            dv_out.buf[at, :] = dvp
            dv_out.flush(ds)
            dqkv_out.buf[at, 0:width] = nt(dqp, sp).astype(BF)
            dqkv_out.buf[at, width : 2 * width] = nt(dkp, sp).astype(BF)
            dqkv_out.buf[at, 2 * width :] = dvp
            dqkv_out.flush(ds)
            dn = nt(jnp.concatenate([dqp, dkp, dvp], axis=1), w_in()[...])
            x = x_in(j)[at, :].astype(F32)
            scale = lax.rsqrt(jnp.sum(x * x, axis=1, keepdims=True) / dim + EPS)
            sums = sums + jnp.sum(dn * (x * scale), axis=0, keepdims=True)
            z = dn * gain_in()[...].astype(F32)
            dot_row = jnp.sum(z * x, axis=1, keepdims=True)
            es[...] = scale * z - x * (scale * scale * scale * dot_row / dim)
            esend.buf[0, at, :] = es[:, piece(ids_ref, 1, width)].astype(BF)
            esend.buf[1, at, :] = es[:, piece(ids_ref, 3, width)].astype(BF)
            esend.flush(slice(None), ds)
            ek0.buf[at, :] = es[:, piece(ids_ref, 0, width)].astype(BF)
            ek0.flush(ds)
            ek2.buf[at, :] = es[:, piece(ids_ref, 2, width)].astype(BF)
            ek2.flush(ds)
        last = pl.ds(count, EXTRA)
        es[0:8, :] = jnp.where(iota((8, dim), 0) == 0, sums, g2_in()[...])
        esend.buf[0, count:, :] = es[0:8, piece(ids_ref, 1, width)].astype(BF)
        esend.buf[1, count:, :] = es[0:8, piece(ids_ref, 3, width)].astype(BF)
        esend.flush(slice(None), last)
        ek0.buf[count:, :] = es[0:8, piece(ids_ref, 0, width)].astype(BF)
        ek0.flush(last)
        ek2.buf[count:, :] = es[0:8, piece(ids_ref, 2, width)].astype(BF)
        ek2.flush(last)

    return call(
        body,
        ids,
        [given(qkv)]
        + a_parts
        + [given(o), (lse, 1), (start_row, 1), given(cos), given(sin), given(w_qkv)]
        + [given(x), (gain, 1), (gg2, 1)],
        [
            ((count, width), BF, blocks),
            ((count, 3 * width), BF, HOLD),
            ((count + EXTRA, width), BF, blocks + 1),
            ((count + EXTRA, width), BF, HOLD),
            ((2, count + EXTRA, width), BF, HOLD),
        ],
        scratch=[
            pltpu.VMEM((width, count), BF),
            pltpu.VMEM((count, width), F32),
            pltpu.VMEM((count, width), F32),
            pltpu.VMEM((BLK, dim), F32),
        ],
        mib=36,
        name="attention_backward",
    )


def halves(ids_ref, size):
    y = ids_ref[1] & 1
    keep = pl.ds(pl.multiple_of(y * size, size), size)
    send = pl.ds(pl.multiple_of((1 - y) * size, size), size)
    return keep, send


def put_chunks(ids_ref, tmp, full, rel, size, keep_buf, send_buf, at):
    keep, send = halves(ids_ref, size)
    rows_ = slice(at, at + full.shape[0])
    tmp[0 : full.shape[0], :] = full
    low, high = rel & 1, rel >> 1
    keep_buf[low, high, rows_, :] = tmp[0 : full.shape[0], keep].astype(BF)
    send_buf[low, high, rows_, :] = tmp[0 : full.shape[0], send].astype(BF)


def put_low(ids_ref, tmp, full, rel, size, buf, at):
    keep, send = halves(ids_ref, size)
    rows_ = slice(at, at + full.shape[0])
    tmp[0 : full.shape[0], :] = full
    low, high = rel & 1, rel >> 1
    buf[low, 0, high, rows_, :] = tmp[0 : full.shape[0], keep].astype(BF)
    buf[low, 1, high, rows_, :] = tmp[0 : full.shape[0], send].astype(BF)


def mlp_grads(ids, left, first, second, sums, mid, ahead):
    count, dim = left.shape
    chunk = dim // 8
    units = first.shape[1]

    def body(ids_ref, ins, outs, scratch):
        left_in, first_in, second_in = ins[:3]
        send1, keep1, send2, keep2, send_sum, total, mid_out = outs
        mid_out.buf[...] = (ins[-2]()[...].astype(F32) + ins[-1]()[...].astype(F32)).astype(BF)
        tmp, buf = scratch
        z = ids_ref[1] >> 1
        for right, low_first in ((first_in, False), (second_in, True)):
            for half in range(2):
                part = left_in()[:, half * 4 * chunk : (half + 1) * 4 * chunk]
                full = tn(right()[...], part)
                for b in range(2):
                    one = full[:, b * 2 * chunk : (b + 1) * 2 * chunk]
                    rel = z ^ (2 * half + b)
                    if low_first:
                        put_low(ids_ref, tmp, one, rel, chunk, buf, 0)
                    else:
                        put_chunks(ids_ref, tmp, one, rel, chunk, keep1.buf, send1.buf, 0)
            if low_first:
                send2.buf[...] = buf[1]
                send2.flush()
                keep2.buf[...] = buf[0]
                keep2.flush()
            else:
                send1.flush()
                keep1.flush()
        for k in range(len(sums)):
            at = slice(k * size, (k + 1) * size)
            both = ins[3 + 2 * k]()[...] + ins[4 + 2 * k]()[...].astype(F32)
            send_sum.buf[at, :] = both[1].astype(BF)
            total.buf[at, :] = both[0]
        send_sum.flush()
        total.flush()

    shape = (2, 2, units, chunk)
    size = sums[0][0].shape[1]
    added = (size * len(sums), chunk)
    return call(
        body,
        ids,
        [(left, 1), given(first), given(second)] + [(a, 1) for pair in sums for a in pair] + mid,
        [(shape, BF, HOLD), (shape, BF, 1)] * 2
        + [(added, BF, HOLD), (added, F32, 1), (mid[0][0].shape, BF, HOLD)],
        scratch=[
            pltpu.VMEM((units, 2 * chunk), F32),
            pltpu.VMEM((2, 2, 2, units, chunk), BF),
        ],
        name="grads_mlp",
        ahead=ahead,
    )


def attention_grads(ids, left, right, o_pieces, parts, ahead):
    count, dim = left.shape
    chunk = dim // 8
    three = right.shape[1]
    width = three // 3
    two = 2 * width

    def body(ids_ref, ins, outs, scratch):
        left_in, right_in, o_ins, p_ins = ins[0], ins[1], ins[2:6], ins[6:9]
        send1, keep1, send2, keep2 = outs[:4]
        tmp, buf = scratch
        z = ids_ref[1] >> 1
        for half in range(2):
            part = left_in()[:, half * 4 * chunk : (half + 1) * 4 * chunk]
            full = tn(right_in()[...], part)
            for b in range(2):
                cols = slice(b * 2 * chunk, (b + 1) * 2 * chunk)
                rel = z ^ (2 * half + b)
                put_chunks(ids_ref, tmp, full[:two, cols], rel, chunk, keep1.buf, send1.buf, 0)
                put_low(ids_ref, tmp, full[two:, cols], rel, chunk, buf, 0)
        send1.flush()
        keep1.flush()
        total = p_ins[0]()[...].astype(F32)
        for p in p_ins[1:]:
            total = total + p()[...].astype(F32)
        grad = total.astype(BF)
        for flip, o in enumerate(o_ins):
            put_low(ids_ref, tmp, tn(o()[...], grad), z ^ flip, chunk, buf, width)
        send2.buf[...] = buf[1]
        send2.flush()
        keep2.buf[...] = buf[0]
        keep2.flush()
    shape = (2, 2, two, chunk)
    return call(
        body,
        ids,
        [given(left), given(right)] + [given(o) for o in o_pieces] + parts,
        [(shape, BF, HOLD), (shape, BF, 1)] * 2,
        scratch=[
            pltpu.VMEM((two, 2 * chunk), F32),
            pltpu.VMEM((2, 2, 2, two, chunk), BF),
        ],
        name="grads_att",
        ahead=ahead,
    )


def down_grads(ids, hidden, near, far):
    count, units = hidden.shape
    two = near.shape[1]
    width = two // 2
    chunk = width // 2
    half = units // 2

    def body(ids_ref, ins, outs, scratch):
        h_in, a_in, b_in = ins
        send1, keep1, send2, keep2 = outs
        tmp, buf = scratch
        for low, ref in ((0, a_in), (1, b_in)):
            full = tn(h_in()[...], ref()[...])
            for high in range(2):
                one = full[:, high * width : (high + 1) * width]
                rel = ids_ref[0] ^ (ids_ref[1] >> 1) ^ (low + 2 * high)
                put_chunks(ids_ref, tmp, one[:half], rel, chunk, keep1.buf, send1.buf, 0)
                put_low(ids_ref, tmp, one[half:], rel, chunk, buf, 0)
        send1.flush()
        keep1.flush()
        send2.buf[...] = buf[1]
        send2.flush()
        keep2.buf[...] = buf[0]
        keep2.flush()

    shape = (2, 2, half, chunk)
    return call(
        body,
        ids,
        [given(hidden), given(near), given(far)],
        [(shape, BF, HOLD), (shape, BF, 1)] * 2,
        scratch=[pltpu.VMEM((half, width), F32), pltpu.VMEM((2, 2, 2, half, chunk), BF)],
        name="grads_down",
    )


def add_pairs(ids, sums, name, ahead):
    def body(ids_ref, ins, outs, scratch):
        for k in range(len(sums)):
            add_halves(ins[2 * k](), ins[2 * k + 1](), outs[2 * k], outs[2 * k + 1])

    outs, ins = [], []
    for keep, got in sums:
        outs += [(keep.shape[1:], BF, HOLD), (keep.shape[1:], F32, 1)]
        ins += [(keep, 1), given(got)]
    return call(body, ids, ins, outs, name=name, ahead=ahead)


def flip_dp(value, bit):
    n = lax.axis_size("dp")
    return lax.ppermute(value, "dp", [(d, d ^ bit) for d in range(n)])


def flip_tensor(value, bit):
    return lax.ppermute(value, "tensor", [(d, d ^ bit) for d in range(4)])


def tie(values, *others):
    return lax.optimization_barrier((values, others))[0]


def gather_pieces(own, *others):
    two = flip_tensor(own, 2)
    one = flip_tensor(own, 1)
    three = flip_tensor(tie(two, *others) if others else two, 1)
    return (own, one, two, three)


def middle(keep2, got):
    return (keep2.astype(F32) + got[1].astype(F32)).astype(BF)


def pack_grads(ids, slot_row, parts, others, last, n_dp):
    count, width = last.shape
    per = count // n_dp
    k, m = len(parts), len(others)

    def body(ids_ref, ins, outs, scratch):
        (out,) = outs
        total = ins[k + 1]()[...].astype(F32)
        for r in ins[k + 2 : k + m + 1]:
            total = total + r()[...].astype(F32)
        gain = ins[1]()[count:, :].astype(F32)
        total = total + ins[1]()[0:count, :].astype(F32)
        for r in ins[2 : k + 1]:
            total = total + r()[0:count, :].astype(F32)
            gain = gain + r()[count:, :].astype(F32)
        gain = jnp.concatenate([gain.astype(BF)] * 2, axis=1)
        both = jnp.concatenate([total.astype(BF), ins[-1]()[...]], axis=1)
        packed = tn(picks(ins[0]()[...], 0, count), both).astype(BF)
        for d in range(n_dp):
            out.buf[d, 0:per, :] = packed[d * per : (d + 1) * per, :]
            out.buf[d, per:, :] = gain
        out.flush()

    return call(
        body,
        ids,
        [(slot_row, 1)] + parts + others + [given(last)],
        [((n_dp, per + EXTRA, 2 * width), BF, HOLD)],
        name="pack_grads",
    )[0]


def unpack_grads(ids, pos8, back):
    n_dp, padded, two = back.shape
    width = two // 2
    part = width // n_dp
    per = padded - EXTRA
    count = n_dp * per

    def body(ids_ref, ins, outs, scratch):
        a_out, b_out, gain_out = outs
        picked = picks(ins[0]()[0:1, :], 0, count)
        ref = ins[1]()
        both = tn(picked, ref[:, 0:per, :].reshape(count, two)).astype(BF)
        a_out.buf[...] = both[:, :width]
        a_out.flush()
        b_out.buf[...] = both[:, width:]
        b_out.flush()
        total = ref[0, per:, 0:width].astype(F32)
        for d in range(1, n_dp):
            total = total + ref[d, per:, 0:width].astype(F32)
        own = iota((width, part), 1) + ids_ref[1] * part
        pick = jnp.where(iota((width, part), 0) == own, 1.0, 0.0)
        gain_out.buf[...] = lax.dot_general(
            total, pick, (((1,), (0,)), ((), ())),
            precision=lax.Precision.HIGHEST, preferred_element_type=F32,
        )
        gain_out.flush()

    return call(
        body,
        ids,
        [(pos8, 1), given(back)],
        [((count, width), BF, 1), ((count, width), BF, 1), ((EXTRA, part), F32, 1)],
        name="unpack_grads",
    )


def finish_attention(ids, qk_total, vo_total, got, outs_got):
    two, chunk = qk_total.shape[1:]
    width = two // 2

    def body(ids_ref, ins, outs, scratch):
        q_out, k_out, v_out, o_out = outs
        qk, vo, add = ins[0](), ins[1](), ins[2]()
        o_out.buf[...] = ins[3]()[...].astype(F32) + ins[4]()[...].astype(F32)
        o_out.flush()
        for out, ref, at, off in ((q_out, qk, 0, 0), (k_out, qk, width, 0), (v_out, vo, 0, two)):
            total = ref[at : at + width, :] + add[off + at : off + at + width, :].astype(F32)
            out.buf[...] = jnp.transpose(total)
            out.flush()

    return call(
        body,
        ids,
        [(qk_total, 1, 0), (vo_total, 1, 0), given(got)] + [given(o) for o in outs_got],
        [((chunk, width), F32, 1)] * 3 + [((width, chunk), F32, 1)],
        name="finish_attention",
    )


def per_device(
    tokens,
    dealing,
    seq_ids,
    first_values,
    out_grad,
    norm1_gain,
    norm2_gain,
    w_query,
    w_key,
    w_value,
    w_out,
    w_gate,
    w_up,
    w_down,
):
    n_dp = lax.axis_size("dp")
    count, width = tokens.shape
    dim = norm1_gain.shape[0]
    per = count // n_dp
    t = lax.axis_index("tensor")
    d = lax.axis_index("dp")
    ids = jnp.stack([t, d]).astype(jnp.int32)
    gate_t, up_t = w_gate.T, w_up.T

    def exchange(packed):
        return lax.all_to_all(packed, "dp", split_axis=0, concat_axis=0, tiled=True)

    deal_row = dealing.reshape(1, count)
    sent, pos8 = pack_tokens(ids, deal_row, tokens, n_dp)
    arrived = exchange(sent)
    grad_far = flip_tensor(tie(out_grad, sent), 2)
    pos8 = tie(pos8, sent)
    (first_sent,) = sort_rows(ids, pos8, [(first_values, 1)], "pack_rows")
    first_sent = first_sent.reshape(n_dp, per, width)

    start = jnp.sum(seq_ids[None, :] < seq_ids[:, None], axis=1, dtype=jnp.int32)
    offset = (jnp.arange(count, dtype=jnp.int32) - start).astype(F32)
    half = HEAD_DIM // 2
    freqs = THETA ** (-jnp.arange(half, dtype=F32) / half)
    angles = offset[:, None] * jnp.tile(freqs, width // HEAD_DIM)[None, :]
    cos = jnp.cos(angles)
    sin = jnp.sin(angles)
    start_row = start.reshape(1, count)
    gain1 = norm1_gain.reshape(1, dim)
    gain2 = norm2_gain.reshape(1, dim)

    arrived = tie(arrived, first_sent, cos, sin, start_row, grad_far, gain1, gain2)
    slots = (
        arrived[:, per, :per].astype(F32) * 32.0 + arrived[:, per + 1, :per].astype(F32)
    ).astype(jnp.int32)
    slot_row = slots.reshape(1, count)
    grad_near = tie(out_grad, slot_row)
    (grad_sent,) = sort_rows(ids, pos8, [(grad_near, 1), given(grad_far)], "pack_rows")
    grad_sent = grad_sent.reshape(n_dp, per, 2 * width)
    pieces = gather_pieces(arrived, grad_sent)
    firsts = exchange(tie(first_sent, pieces[1]))
    near = exchange(tie(grad_sent, firsts, pieces[2]))
    w_pieces = gather_pieces(tie(w_out, pieces[2]))

    x, normed1, qkv, attended, lse, w_qkv = qkv_attention(
        ids, tie(slot_row, grad_sent), pieces, firsts, cos, sin, gain1, w_query, w_key, w_value,
        start_row,
    )
    near = tie(near, attended).reshape(count, 2 * width)
    near, *early = sort_rows(
        ids, slot_row, [given(near)], "sort_rows", ahead=(gate_t, up_t, w_down, x)
    )
    far = flip_tensor(near, 1)
    o_pieces = gather_pieces(attended, near)
    x1, normed2, fg, fu, hidden, yk0, yk2, ysend = feed_forward(
        ids, early[3], o_pieces, w_pieces, gain2, *early[:3]
    )
    fast = n_dp == 8
    y_got = flip_tensor(ysend, 1)
    early, sums = (), []
    if fast:
        da_send, da_keep, db_send, db_keep = down_grads(ids, hidden, near, far)
        early = (flip_dp(da_send, 1), flip_dp(db_send, 2))
        sums = [(da_keep, early[0]), (db_keep, early[1])]
        yk2 = tie(yk2, da_keep)
    y_mid = middle(yk2, y_got)
    y_far = flip_tensor(y_mid, 2)
    dgate, dup, ak0, ak2, asend, dk0, dk2, dsend, gg2 = feed_backward(
        ids, tie(x1, y_mid), near, far, fg, fu, w_pieces, gain2, gate_t, up_t, w_down
    )
    a_got = flip_tensor(tie(asend, y_far, *early), 1)
    y_sent, *down_sums = return_rows(
        ids,
        slot_row,
        [(tie(yk0, ak0), 1), (y_got, 1, 0), (y_far, 1)],
        "return_rows",
        sums,
    )
    a_mid = middle(tie(ak2, y_sent), a_got)
    a_far = flip_tensor(a_mid, 2)
    y_back = exchange(tie(y_sent, a_mid).reshape(n_dp, per, width)).reshape(count, width)
    d_got = flip_tensor(tie(dsend, a_mid), 1)
    early = ()
    held = (qkv, attended, cos, sin, w_qkv, x)
    if fast:
        da_send, da_total, db_send, db_total = down_sums
        da_got = flip_dp(tie(da_send, a_mid), 2)
        db_got = flip_dp(tie(db_send, a_mid), 1)
        dgate, dup = tie((dgate, dup), a_mid)
        gate_send, gate_keep, up_send, up_keep, down_send, down_sum, d_mid, *held = mlp_grads(
            ids, normed2, dgate, dup, [(da_total, da_got), (db_total, db_got)],
            [given(dk2), given(d_got, 1)], held,
        )
        a_far = tie(a_far, gate_keep)
        gate_got = flip_dp(gate_send, 1)
        up_got = flip_dp(up_send, 2)
        down_got = flip_dp(down_send, 4)
        early = (gate_got, up_got, down_got)
    else:
        d_mid = middle(dk2, d_got)
    a_far = tie(a_far, d_mid)
    d_far = flip_tensor(tie(d_mid, a_far), 2)
    dvp, dqkv, ek0, ek2, esend = attention_backward(
        ids, *held[:2], lse, [(ak0, 1), given(a_got, 0), given(a_far)], start_row, *held[2:4],
        held[5], gain1, held[4], gg2,
    )
    e_got = flip_tensor(tie(esend, d_far, y_back, *early), 1)
    if fast:
        gate_send, gate_total, up_send, up_total, *held = add_pairs(
            ids, [(tie(gate_keep, ek2), gate_got), (up_keep, up_got)], "add_pairs",
            (normed1, *o_pieces, dk0, d_far),
        )
        ek2 = tie(ek2, gate_send)
    e_mid = middle(ek2, e_got)
    e_far = flip_tensor(e_mid, 2)
    if fast:
        gate_got = flip_dp(tie(gate_send, e_mid), 2)
        up_got = flip_dp(tie(up_send, e_mid), 1)
        qk_send, qk_keep, vo_send, vo_keep, *held = attention_grads(
            ids, held[0], tie(dqkv, e_mid), held[1:5],
            [given(held[5]), (d_got, 1, 0), given(held[6])], (ek0, dvp, dk0, d_far),
        )
        ek0, dvp, dk0, d_far = held
        qk_got = flip_dp(qk_send, 1)
        vo_got = flip_dp(vo_send, 2)

        def plus(keep, got, *after):
            return keep.astype(F32) + tie(got, *after).astype(F32)

        gate_total = plus(gate_total, gate_got, qk_keep)
        up_total = plus(up_total, up_got, qk_keep)
        mlp_send = jnp.concatenate([gate_total[1], up_total[1]], axis=0).astype(BF)
        mlp_keep = jnp.concatenate([gate_total[0], up_total[0]], axis=0)
        e_far = tie(e_far, mlp_send)
        mlp_got = flip_dp(mlp_send, 4)
    i_sent = pack_grads(
        ids, slot_row, [given(ek0), (e_got, 1, 0), given(e_far)],
        [given(dk0), (d_got, 1, 0), given(d_far)], dvp, n_dp,
    )
    i_back = exchange(i_sent)
    (output,) = restore_rows(ids, pos8, [tie(y_back, i_sent)], "restore_rows")
    input_grad, first_grad, gain_rows = unpack_grads(ids, pos8, i_back)
    if fast:
        units = w_down.shape[0]
        mlp_total = plus(mlp_keep, mlp_got, output)
        qk_total = plus(qk_keep, qk_got, output)
        vo_total = plus(vo_keep, vo_got, output)
        qk_total = plus(qk_total[0], flip_dp(qk_total[1].astype(BF), 2))
        vo_total = plus(vo_total[0], flip_dp(vo_total[1].astype(BF), 1))
        vo_low = vo_total[:, width:].astype(BF)
        outs_got = [
            lax.ppermute(
                vo_low[b],
                ("dp", "tensor"),
                [
                    ((2 * z + y) * 4 + r, (2 * r + y) * 4 + (r ^ z ^ (2 * b)))
                    for z in range(4)
                    for y in range(2)
                    for r in range(4)
                ],
            )
            for b in range(2)
        ]
        att_send = jnp.concatenate([qk_total[1], vo_total[1, :width]], axis=0).astype(BF)
        att_got = flip_dp(att_send, 4)
        gw_q, gw_k, gw_v, gw_out = finish_attention(
            ids, qk_total, vo_total, tie(att_got, input_grad), outs_got
        )
        gw_down = plus(down_sum, down_got, i_sent)
        gw_gate, gw_up = mlp_total[:units].T, mlp_total[units:].T
    else:

        def scattered(left, right, dim_):
            full = jnp.einsum("ta,tb->ab", left, right, preferred_element_type=F32)
            return lax.psum_scatter(full, "dp", scatter_dimension=dim_, tiled=True)

        def natural(parts):
            full = jnp.zeros((count, dim), BF)
            for flip, part in enumerate(parts):
                full = lax.dynamic_update_slice(full, part, (0, (t ^ flip) * width))
            return full

        dy = natural((near[:, :width], far[:, :width], near[:, width:], far[:, width:]))
        dx1 = (dk0 + d_got[0].astype(F32) + d_far.astype(F32)).astype(BF)
        dx1 = lax.all_gather(dx1, "tensor", axis=1, tiled=True)
        gw_gate = scattered(normed2, dgate, 0)
        gw_up = scattered(normed2, dup, 0)
        gw_down = scattered(hidden, dy, 1)
        gw_q, gw_k, gw_v = [scattered(normed1, p, 0) for p in jnp.split(dqkv, 3, axis=1)]
        gw_out = scattered(attended, dx1, 1)

    return (
        output,
        input_grad,
        first_grad,
        gain_rows[0:1],
        gain_rows[1:2],
        gw_q,
        gw_k,
        gw_v,
        gw_out,
        gw_gate,
        gw_up,
        gw_down,
    )


def solution(mesh):
    in_specs = (
        P("dp", "tensor"),
        P("dp"),
        P("dp"),
        P("dp", "tensor"),
        P("dp", "tensor"),
        P(),
        P(),
        P(None, "tensor"),
        P(None, "tensor"),
        P(None, "tensor"),
        P("tensor", None),
        P(None, "tensor"),
        P(None, "tensor"),
        P("tensor", None),
    )
    out_specs = (
        P("dp", "tensor"),
        P("dp", "tensor"),
        P("dp", "tensor"),
        P("tensor", "dp"),
        P("tensor", "dp"),
        P("dp", "tensor"),
        P("dp", "tensor"),
        P("dp", "tensor"),
        P("tensor", "dp"),
        P("dp", "tensor"),
        P("dp", "tensor"),
        P("tensor", "dp"),
    )
    return jax.shard_map(
        per_device, mesh=mesh, in_specs=in_specs, out_specs=out_specs, check_vma=False
    )
```

```python
import functools

import jax
import jax.numpy as jnp
from jax import lax
from jax.experimental import pallas as pl
from jax.experimental.pallas import tpu as pltpu
from jax.sharding import PartitionSpec as P

HEAD_DIM = 64
EPS = 1e-06
THETA = 10000.0
NEG = -1e30
BF = jnp.bfloat16
F32 = jnp.float32
BLK = 256
EXTRA = 8
MIB = 1 << 20


def nn(a, b):
    return lax.dot_general(a, b, (((1,), (0,)), ((), ())), preferred_element_type=F32)


def nt(a, b):
    return lax.dot_general(a, b, (((1,), (1,)), ((), ())), preferred_element_type=F32)


def tn(a, b):
    return lax.dot_general(a, b, (((0,), (0,)), ((), ())), preferred_element_type=F32)


def iota(shape, dim):
    return lax.broadcasted_iota(jnp.int32, shape, dim)


TIMES = {
    "pack_tokens": 3,
    "pack_rows": 3,
    "qkv_attention": 14,
    "feed_forward": 12,
    "sort_rows": 3,
    "grads_down": 5,
    "feed_backward": 15,
    "grads_mlp": 8,
    "return_rows": 3,
    "attention_backward": 17,
    "grads_att": 8,
    "pack_grads": 4,
    "unpack_grads": 4,
    "restore_rows": 3,
    "add_pairs": 3,
    "finish_attention": 2,
}


SCALE_F = 1_150_000_000 // 16
SCALE_B = 3_690_000 // 16


class Fetched:
    def __init__(self, src, buf, sems, base, parts):
        self.buf = buf
        size = src.shape[0] // parts if parts else 0
        self.copies = [
            pltpu.make_async_copy(
                src.at[pl.ds(p * size, size)], buf.at[pl.ds(p * size, size)], sems.at[base + p]
            )
            for p in range(parts)
        ]
        self.waited = [False] * parts

    def __call__(self, part=None):
        one = part is not None and len(self.copies) > 1
        for p in (part,) if one else range(len(self.copies)):
            if not self.waited[p]:
                self.copies[p].wait()
                self.waited[p] = True
        return self.buf


class Stored:
    def __init__(self, dst, buf, sems, base):
        self.dst, self.buf, self.sems, self.at = dst, buf, sems, base
        self.copies = []

    def flush(self, *index):
        if self.sems is None:
            return
        src = self.buf.at[index] if index else self.buf
        dst = self.dst.at[index] if index else self.dst
        c = pltpu.make_async_copy(src, dst, self.sems.at[self.at + len(self.copies)])
        c.start()
        self.copies.append(c)


def call(body, ids, ins, outs, scratch=(), mib=28, name=None, ahead=()):
    ins = [tuple(i) + (None,)[len(i) - 2 :] for i in ins]
    took = TIMES[name]
    n_in, n_out = len(ins), len(outs)
    in_at = [sum(i[1] for i in ins[:k]) for k in range(n_in + 1)]
    out_at = [sum(o[2] for o in outs[:k]) for k in range(n_out + 1)]
    stored = [k for k in range(n_out) if outs[k][2] != HOLD]
    fetched = [k for k in range(n_in) if ins[k][1] != HOLD]
    n_ahead = len(ahead)

    def kernel(ids_ref, *refs):
        srcs, refs = refs[:n_in], refs[n_in:]
        early, refs = refs[:n_ahead], refs[n_ahead:]
        dsts, refs = refs[:n_out], refs[n_out:]
        late, refs = refs[:n_ahead], refs[n_ahead:]
        bufs, refs = refs[: len(fetched)], refs[len(fetched) :]
        obufs, refs = refs[: len(stored)], refs[len(stored) :]
        in_sems, out_sems, refs = refs[0], refs[1], refs[2:]
        srcs = [src if i[2] is None else src.at[i[2]] for src, i in zip(srcs, ins)]
        inputs = [Fetched(None, src, None, 0, 0) for src in srcs]
        for k, buf in zip(fetched, bufs):
            inputs[k] = Fetched(srcs[k], buf, in_sems, in_at[k], ins[k][1])
        outputs = [Stored(None, dst, None, 0) for dst in dsts]
        for k, buf in zip(stored, obufs):
            outputs[k] = Stored(dsts[k], buf, out_sems, out_at[k])
        for p in range(max(i[1] for i in ins)):
            for i in inputs:
                if p < len(i.copies):
                    i.copies[p].start()
        copies = [
            pltpu.make_async_copy(a, b, in_sems.at[in_at[-1] + k])
            for k, (a, b) in enumerate(zip(early, late))
        ]
        for c in copies:
            c.start()
        body(ids_ref, inputs, outputs, refs)
        for i in inputs:
            i()
        for k in stored:
            assert len(outputs[k].copies) == outs[k][2]
            for c in outputs[k].copies:
                c.wait()
        for c in copies:
            c.wait()

    return pl.pallas_call(
        kernel,
        out_shape=tuple(
            (pltpu.HBM if k in stored else pltpu.VMEM)(s, d) for k, (s, d, _) in enumerate(outs)
        )
        + tuple(pltpu.VMEM(a.shape, a.dtype) for a in ahead),
        in_specs=[pl.BlockSpec(memory_space=pltpu.SMEM)]
        + [
            pl.BlockSpec(memory_space=pl.ANY if k in fetched else pltpu.VMEM) for k in range(n_in)
        ]
        + [pl.BlockSpec(memory_space=pl.ANY)] * n_ahead,
        out_specs=tuple(
            pl.BlockSpec(memory_space=pl.ANY if k in stored else pltpu.VMEM) for k in range(n_out)
        )
        + tuple(pl.BlockSpec(memory_space=pltpu.VMEM) for _ in ahead),
        scratch_shapes=[
            pltpu.VMEM(a.shape if index is None else a.shape[1:], a.dtype)
            for a, _, index in (ins[k] for k in fetched)
        ]
        + [pltpu.VMEM(outs[k][0], outs[k][1]) for k in stored]
        + [
            pltpu.SemaphoreType.DMA((max(in_at[-1] + n_ahead, 1),)),
            pltpu.SemaphoreType.DMA((max(out_at[-1], 1),)),
        ]
        + list(scratch),
        compiler_params=pltpu.CompilerParams(vmem_limit_bytes=mib * MIB),
        cost_estimate=pl.CostEstimate(
            flops=took * SCALE_F, transcendentals=0, bytes_accessed=took * SCALE_B
        ),
        name=name,
    )(
        ids,
        *[
            pltpu.with_memory_space_constraint(a, pltpu.VMEM if parts == HOLD else pltpu.HBM)
            for a, parts, _ in ins
        ],
        *[pltpu.with_memory_space_constraint(a, pltpu.HBM) for a in ahead],
    )


HOLD = 0


def given(array, index=None):
    return (array, HOLD, index)


def own_first(pieces, parts=1):
    return [(pieces[0], parts)] + [given(p) for p in pieces[1:]]


def piece(ids_ref, flip, width):
    return pl.ds(pl.multiple_of((ids_ref[0] ^ flip) * width, width), width)


def picks(index, first, size):
    shape = (size, index.shape[1])
    return jnp.where(iota(shape, 0) + first == index, 1.0, 0.0).astype(BF)


def pack_tokens(ids, deal_row, tok, n_dp):
    count, width = tok.shape
    per = count // n_dp
    lanes = 128

    def body(ids_ref, ins, outs, scratch):
        deal_in, tok_in = ins
        out, pos_out = outs
        deal = deal_in()[...]
        dest = deal // count
        slot = deal % count
        oh = jnp.where(iota((n_dp, count), 0) == dest, 1.0, 0.0)
        upto = jnp.where(iota((lanes, lanes), 0) <= iota((lanes, lanes), 1), 1.0, 0.0)
        parts = [oh[:, b * lanes : (b + 1) * lanes] for b in range(count // lanes)]
        inner = nn(jnp.concatenate(parts, axis=0).astype(BF), upto.astype(BF))
        base = (iota((n_dp, 1), 0) * per - 1).astype(F32)
        rows_ = []
        for b, part in enumerate(parts):
            seen = inner[b * n_dp : (b + 1) * n_dp]
            rows_.append(jnp.sum(part * (seen + base), axis=0, keepdims=True))
            base = base + seen[:, lanes - 1 :]
        pos = jnp.concatenate(rows_, axis=1).astype(jnp.int32)
        pos_out.buf[...] = jnp.broadcast_to(pos, (8, count))
        pos_out.flush()
        high = jnp.broadcast_to(slot // 32, (8, count))
        low = jnp.broadcast_to(slot % 32, (8, count))
        hl = jnp.where(iota((8, count), 0) == 0, high, low).astype(F32).astype(BF)
        out.buf[:, per : per + EXTRA, :] = jnp.zeros((n_dp, EXTRA, width), BF)
        size = min(count, 512)
        group = size // per
        for g in range(count // size):
            pick = picks(pos, g * size, size)
            moved = nn(pick, tok_in()[...]).astype(BF)
            marks = nt(hl, pick).astype(BF)
            for e in range(group):
                d = g * group + e
                out.buf[d, 0:per, :] = moved[e * per : (e + 1) * per]
                out.buf[d, per : per + 8, 0:per] = marks[:, e * per : (e + 1) * per]
            out.flush(pl.ds(g * group, group))

    return call(
        body,
        ids,
        [(deal_row, 1), (tok, 1)],
        [
            ((n_dp, per + EXTRA, width), BF, HOLD),
            ((8, count), jnp.int32, 1),
        ],
        name="pack_tokens",
    )


def sort_rows(ids, index, parts, name, ahead=()):
    count, width = parts[0][0].shape
    blocks = 2
    size = count // blocks

    def body(ids_ref, ins, outs, scratch):
        idx = ins[0]()[0:1, :]
        (out,) = outs
        for b in range(blocks):
            at = slice(b * size, (b + 1) * size)
            pick = picks(idx, b * size, size)
            for k, part in enumerate(ins[1:]):
                out.buf[at, k * width : (k + 1) * width] = nn(pick, part()[...]).astype(BF)
            out.flush(pl.ds(b * size, size))

    return call(
        body,
        ids,
        [(index, 1)] + parts,
        [((count, width * len(parts)), BF, HOLD)],
        name=name,
        ahead=ahead,
    )


def add_halves(keep, got, send_out, total_out):
    sums = keep[...].astype(F32) + got[...].astype(F32)
    send_out.buf[...] = sums[1].astype(BF)
    send_out.flush()
    total_out.buf[...] = sums[0]
    total_out.flush()


def return_rows(ids, index, parts, name, sums=()):
    count, width = parts[0][0].shape[-2:]
    m = 1 + len(parts)

    def body(ids_ref, ins, outs, scratch):
        total = ins[1]()[...]
        for r in ins[2:m]:
            total = total.astype(F32) + r()[...].astype(F32)
        outs[0].buf[...] = tn(picks(ins[0]()[0:1, :], 0, count), total.astype(BF)).astype(BF)
        outs[0].flush()
        for k in range(len(sums)):
            at = m + 2 * k
            add_halves(ins[at](), ins[at + 1](), outs[1 + 2 * k], outs[2 + 2 * k])

    outs = [((count, width), BF, HOLD)]
    ins = [(index, 1)] + parts
    for keep, got in sums:
        outs += [(keep.shape[1:], BF, HOLD), (keep.shape[1:], F32, 1)]
        ins += [(keep, 1), (got, 1)]
    return call(body, ids, ins, outs, name=name)


def restore_rows(ids, index, backs, name):
    count, width = backs[0].shape

    def body(ids_ref, ins, outs, scratch):
        pick = picks(ins[0]()[0:1, :], 0, count)
        both = tn(pick, jnp.concatenate([b()[...] for b in ins[1:]], axis=1)).astype(BF)
        for k, out in enumerate(outs):
            out.buf[...] = both[:, k * width : (k + 1) * width]
            out.flush()

    return call(
        body,
        ids,
        [(index, 1)] + [(b, 1) for b in backs],
        [((count, width), BF, 1)] * len(backs),
        name=name,
    )


def head_mask(shape, head, split):
    lane = iota(shape, 1)
    if split:
        return (lane % (shape[1] // 2)) // (HEAD_DIM // 2) == head
    return lane // HEAD_DIM == head


def split_perm(width):
    half = HEAD_DIM // 2
    src = iota((width, width), 0)
    dst = iota((width, width), 1)
    second = dst // (width // 2)
    rest = dst % (width // 2)
    want = (rest // half) * HEAD_DIM + second * half + rest % half
    return (src == want).astype(F32).astype(BF)


def qkv_attention(ids, slot_row, pieces, firsts, cos, sin, gain, wq, wk, wv, start_row):
    n_dp, padded, width = pieces[0].shape
    per = firsts.shape[1]
    count = n_dp * per
    dim = gain.shape[1]
    heads = width // HEAD_DIM
    blocks = count // BLK
    half = width // 2

    def body(ids_ref, ins, outs, scratch):
        slot_in, x0, x1, x2, x3, fv_in, wq_in, wk_in, wv_in, cos_in, sin_in, gain_in, start_in = ins
        x_out, n_out, qkv_out, o_out, lse_out, w_out = outs
        cat, vt = scratch
        slots = slot_in()[...]
        for flip, ref in enumerate((x0, x1, x2, x3)):
            cat[:, piece(ids_ref, flip, width)] = ref()[:, 0:per, :].reshape(count, width)
        cat[:, dim:] = fv_in()[...].reshape(count, width)
        sp = split_perm(width)
        w_out.buf[:, 0:width] = nn(wq_in()[...], sp).astype(BF)
        w_out.buf[:, width : 2 * width] = nn(wk_in()[...], sp).astype(BF)
        w_out.buf[:, 2 * width :] = wv_in()[...]
        w_out.flush()
        lse_out.buf[...] = jnp.zeros_like(lse_out.buf)

        def rope(v, c, s):
            a, b = v[:, :half], v[:, half:]
            return jnp.concatenate([a * c - b * s, b * c + a * s], axis=1).astype(BF)

        for j in range(blocks):
            at = slice(j * BLK, (j + 1) * BLK)
            ds = pl.ds(j * BLK, BLK)
            moved = nn(picks(slots, j * BLK, BLK), cat[...])
            x = moved[:, :dim]
            x_out.buf[at, :] = x.astype(BF)
            x_out.flush(ds)
            scale = lax.rsqrt(jnp.sum(x * x, axis=1, keepdims=True) / dim + EPS)
            normed = (x * scale * gain_in()[...].astype(F32)).astype(BF)
            n_out.buf[at, :] = normed
            n_out.flush(ds)
            qkv = nn(normed, w_out.buf[...])
            c, s = cos_in(j)[at, :], sin_in(j)[at, :]
            q = rope(qkv[:, 0:width], c, s)
            v = 0.5 * qkv[:, 2 * width :] + 0.5 * moved[:, dim:]
            q = (q.astype(F32) * HEAD_DIM ** (-0.5)).astype(BF)
            qkv_out.buf[at, 0:width] = q
            qkv_out.buf[at, width : 2 * width] = rope(qkv[:, width : 2 * width], c, s)
            qkv_out.buf[at, 2 * width :] = v.astype(BF)
            qkv_out.flush(ds)
            vt[:, at] = jnp.transpose(v).astype(BF)
            start = start_in()[:, at]
            n = (j + 1) * BLK
            keys = qkv_out.buf[0:n, width : 2 * width]
            key = iota((n, BLK), 0)
            valid = (key >= start) & (key <= iota((n, BLK), 1) + j * BLK)
            out = []
            for h in range(heads):
                qh = jnp.where(head_mask((BLK, width), h, True), q, jnp.zeros_like(q))
                sc = jnp.where(valid, nt(keys, qh), NEG)
                top = jnp.max(sc, axis=0, keepdims=True)
                ex = jnp.exp(sc - top)
                total = jnp.sum(ex, axis=0, keepdims=True)
                vals = vt[h * HEAD_DIM : (h + 1) * HEAD_DIM, 0:n]
                out.append(nn(vals, ex.astype(BF)) * (1.0 / total))
                lse_out.buf[h : h + 1, at] = top + jnp.log(total)
            o_out.buf[at, :] = jnp.transpose(jnp.concatenate(out, axis=0)).astype(BF)
            o_out.flush(ds)
        lse_out.flush()

    return call(
        body,
        ids,
        [(slot_row, 1)]
        + [given(p) for p in pieces]
        + [given(firsts)]
        + [(wq, 1), (wk, 1), (wv, 1), (cos, 1), (sin, 1), (gain, 1), (start_row, 1)],
        [
            ((count, dim), BF, blocks),
            ((count, dim), BF, blocks),
            ((count, 3 * width), BF, blocks),
            ((count, width), BF, HOLD),
            ((8, count), F32, 1),
            ((dim, 3 * width), BF, 1),
        ],
        scratch=[pltpu.VMEM((count, dim + width), BF), pltpu.VMEM((width, count), BF)],
        name="qkv_attention",
    )


FEED = 512


def feed_forward(ids, x, o_pieces, w_pieces, gain, w_gate, w_up, w_down):
    count, dim = x.shape
    width = o_pieces[0].shape[1]
    units = w_gate.shape[0]
    size = min(FEED, count)
    blocks = count // size

    def body(ids_ref, ins, outs, scratch):
        w_ins, o_ins = ins[0:4], ins[4:8]
        x_in, gain_in, wg_in, wu_in, wd_in = ins[8:]
        x1_out, n_out, fg_out, fu_out, h_out, yk0, yk2, ysend = outs
        ys, xs, wo = scratch
        for k, w in enumerate(w_ins):
            wo[k * width : (k + 1) * width, :] = w()[...]
        for j in range(blocks):
            at = slice(j * size, (j + 1) * size)
            ds = pl.ds(j * size, size)
            heads = jnp.concatenate([o(j)[at, :] for o in o_ins], axis=1)
            x1 = x_in(j)[at, :].astype(F32) + nn(heads, wo[...])
            xs[...] = x1
            x1_out.buf[at, :] = x1.astype(BF)
            x1_out.flush(ds)
            scale = lax.rsqrt(jnp.sum(x1 * x1, axis=1, keepdims=True) / dim + EPS)
            normed = (x1 * scale * gain_in()[...].astype(F32)).astype(BF)
            n_out.buf[at, :] = normed
            n_out.flush(ds)
            g = nt(normed, wg_in()[...])
            u = nt(normed, wu_in()[...])
            sg = jax.nn.sigmoid(g)
            silu = g * sg
            hid = (silu * u).astype(BF)
            h_out.buf[at, :] = hid
            h_out.flush(ds)
            fu_out.buf[at, :] = silu.astype(BF)
            fu_out.flush(ds)
            fg_out.buf[at, :] = (u * sg * (1.0 + g * (1.0 - sg))).astype(BF)
            fg_out.flush(ds)
            ys[...] = nn(hid, wd_in()[...])
            ysend.buf[0, at, :] = ys[:, piece(ids_ref, 1, width)].astype(BF)
            ysend.buf[1, at, :] = ys[:, piece(ids_ref, 3, width)].astype(BF)
            ysend.flush(slice(None), ds)
            own = piece(ids_ref, 0, width)
            yk0.buf[at, :] = (ys[:, own] + xs[:, own]).astype(BF)
            yk0.flush(ds)
            yk2.buf[at, :] = ys[:, piece(ids_ref, 2, width)].astype(BF)
            yk2.flush(ds)

    return call(
        body,
        ids,
        [(w, 1) for w in w_pieces]
        + own_first(o_pieces)
        + [given(x), (gain, 1), given(w_gate), given(w_up), given(w_down)],
        [
            ((count, dim), BF, blocks),
            ((count, dim), BF, blocks),
            ((count, units), BF, blocks),
            ((count, units), BF, blocks),
            ((count, units), BF, HOLD),
            ((count, width), BF, blocks),
            ((count, width), BF, HOLD),
            ((2, count, width), BF, HOLD),
        ],
        scratch=[
            pltpu.VMEM((size, dim), F32),
            pltpu.VMEM((size, dim), F32),
            pltpu.VMEM((4 * width, dim), BF),
        ],
        mib=44,
        name="feed_forward",
    )


def feed_backward(ids, x1, near, far, fg, fu, w_pieces, gain, w_gate, w_up, w_down):
    count, dim = x1.shape
    width = w_pieces[0].shape[0]
    units = w_gate.shape[0]
    size = min(FEED, count)
    blocks = count // size

    def body(ids_ref, ins, outs, scratch):
        wd_in, fg_in, fu_in, wg_in, wu_in, x1_in, near_in, far_in, gain_in = ins[:9]
        w_ins = ins[9:]
        dg_out, du_out, ak0, ak2, asend, dk0, dk2, dsend, gg_out = outs
        ds_, ys, wo = scratch
        sums = jnp.zeros((1, dim), F32)
        for j in range(blocks):
            at = slice(j * size, (j + 1) * size)
            ds = pl.ds(j * size, size)
            near_, far_ = near_in(j)[at, :], far_in(j)[at, :]
            ys[:, piece(ids_ref, 0, width)] = near_[:, :width]
            ys[:, piece(ids_ref, 2, width)] = near_[:, width:]
            ys[:, piece(ids_ref, 1, width)] = far_[:, :width]
            ys[:, piece(ids_ref, 3, width)] = far_[:, width:]
            dy = ys[...]
            dh = nt(dy, wd_in()[...])
            dg = (dh * fg_in(j)[at, :].astype(F32)).astype(BF)
            du = (dh * fu_in(j)[at, :].astype(F32)).astype(BF)
            dg_out.buf[at, :] = dg
            du_out.buf[at, :] = du
            dg_out.flush(ds)
            du_out.flush(ds)
            dn = nn(dg, wg_in()[...]) + nn(du, wu_in()[...])
            x1 = x1_in(j)[at, :].astype(F32)
            scale = lax.rsqrt(jnp.sum(x1 * x1, axis=1, keepdims=True) / dim + EPS)
            sums = sums + jnp.sum(dn * (x1 * scale), axis=0, keepdims=True)
            z = dn * gain_in()[...].astype(F32)
            dot_row = jnp.sum(z * x1, axis=1, keepdims=True)
            part = scale * z - x1 * (scale * scale * scale * dot_row / dim)
            part = part + 0.25 * dy.astype(F32)
            ds_[...] = part
            if j == 0:
                for k, w in enumerate(w_ins):
                    wo[k * width : (k + 1) * width, :] = w()[...]
            da = nt(part.astype(BF), wo[...])
            asend.buf[0, at, :] = da[:, width : 2 * width].astype(BF)
            asend.buf[1, at, :] = da[:, 3 * width :].astype(BF)
            asend.flush(slice(None), ds)
            ak0.buf[at, :] = da[:, 0:width].astype(BF)
            ak0.flush(ds)
            ak2.buf[at, :] = da[:, 2 * width : 3 * width].astype(BF)
            ak2.flush(ds)
            dsend.buf[0, at, :] = ds_[:, piece(ids_ref, 1, width)].astype(BF)
            dsend.buf[1, at, :] = ds_[:, piece(ids_ref, 3, width)].astype(BF)
            dsend.flush(slice(None), ds)
            dk0.buf[at, :] = ds_[:, piece(ids_ref, 0, width)].astype(BF)
            dk0.flush(ds)
            dk2.buf[at, :] = ds_[:, piece(ids_ref, 2, width)].astype(BF)
            dk2.flush(ds)
        gg_out.buf[...] = jnp.broadcast_to(sums, (8, dim))
        gg_out.flush()

    return call(
        body,
        ids,
        [(w_down, 1), (fg, 1), (fu, 1), (w_gate, 1), (w_up, 1), (x1, 1)]
        + [given(near), given(far), (gain, 1)]
        + [(w, 1) for w in w_pieces],
        [
            ((count, units), BF, blocks),
            ((count, units), BF, blocks),
            ((count, width), BF, blocks),
            ((count, width), BF, HOLD),
            ((2, count, width), BF, HOLD),
            ((count, width), BF, blocks),
            ((count, width), BF, HOLD),
            ((2, count, width), BF, HOLD),
            ((8, dim), F32, 1),
        ],
        scratch=[
            pltpu.VMEM((size, dim), F32),
            pltpu.VMEM((size, dim), BF),
            pltpu.VMEM((4 * width, dim), BF),
        ],
        mib=44,
        name="feed_backward",
    )


def attention_backward(
    ids, qkv, o, lse, a_parts, start_row, cos, sin, x, gain, w_qkv, gg2
):
    count, width = o.shape
    dim = x.shape[1]
    heads = width // HEAD_DIM
    blocks = count // BLK
    half = width // 2
    part = HEAD_DIM // 2

    def body(ids_ref, ins, outs, scratch):
        qkv_in, a0, a1, a2, o_in, lse_in, start_in, cos_in, sin_in, w_in, x_in, gain_in, g2_in = ins
        dv_out, dqkv_out, ek0, ek2, esend = outs
        kt, dk, dv, es = scratch
        qkv_ref = qkv_in()
        for b in range(blocks):
            at = slice(b * BLK, (b + 1) * BLK)
            kt[:, at] = jnp.transpose(qkv_ref[at, width : 2 * width].astype(F32)).astype(BF)
        sums = jnp.zeros((1, dim), F32)
        pick = (iota((8, width), 1) // HEAD_DIM == iota((8, width), 0)).astype(F32)
        sp = split_perm(width)

        def rope_back(g, c, s):
            a, b = g[:, :half], g[:, half:]
            return jnp.concatenate([a * c + b * s, b * c - a * s], axis=1).astype(BF)

        for j in reversed(range(blocks)):
            at = slice(j * BLK, (j + 1) * BLK)
            ds = pl.ds(j * BLK, BLK)
            q = qkv_ref[at, 0:width]
            do = (a0(j)[at, :].astype(F32) + a1(j)[at, :].astype(F32) + a2(j)[at, :].astype(F32)).astype(BF)
            prod = do.astype(F32) * o_in(j)[at, :].astype(F32)
            delta = lax.dot_general(
                pick, prod, (((1,), (1,)), ((), ())),
                precision=lax.Precision.HIGHEST, preferred_element_type=F32,
            )
            start = start_in()[:, at]
            lse = lse_in()[:, at]
            n = (j + 1) * BLK
            keys = qkv_ref[0:n, width : 2 * width]
            vals = qkv_ref[0:n, 2 * width :]
            key = iota((n, BLK), 0)
            valid = (key >= start) & (key <= iota((n, BLK), 1) + j * BLK)
            probs, grads, q_heads, do_heads = [], [], [], []
            first, second = [], []
            for h in range(heads):
                qh = jnp.where(head_mask((BLK, width), h, True), q, jnp.zeros_like(q))
                dh = jnp.where(head_mask((BLK, width), h, False), do, jnp.zeros_like(do))
                sc = jnp.where(valid, nt(keys, qh) - lse[h : h + 1, :], NEG)
                pr = jnp.exp(sc)
                dsc = (pr * (nt(vals, dh) - delta[h : h + 1, :])).astype(BF)
                probs.append(pr.astype(BF))
                grads.append(dsc)
                q_heads.append(qh)
                do_heads.append(dh)
                kh = jnp.concatenate(
                    [
                        kt[h * part : (h + 1) * part, 0:n],
                        kt[half + h * part : half + (h + 1) * part, 0:n],
                    ],
                    axis=0,
                )
                dqh = nn(kh, dsc)
                first.append(dqh[:part])
                second.append(dqh[part:])
            dvn = nn(jnp.concatenate(probs, 1), jnp.concatenate(do_heads, 0))
            dkn = nn(jnp.concatenate(grads, 1), jnp.concatenate(q_heads, 0))
            if j == blocks - 1:
                dv[...] = dvn
                dk[...] = dkn
            else:
                dv[0:n, :] += dvn
                dk[0:n, :] += dkn
            dqj = jnp.transpose(jnp.concatenate(first + second, axis=0)) * HEAD_DIM ** (-0.5)
            c, s = cos_in(j)[at, :], sin_in(j)[at, :]
            dqp = rope_back(dqj, c, s)
            dkp = rope_back(dk[at, :], c, s)
            dvp = (0.5 * dv[at, :].astype(BF).astype(F32)).astype(BF)
            dv_out.buf[at, :] = dvp
            dv_out.flush(ds)
            dqkv_out.buf[at, 0:width] = nt(dqp, sp).astype(BF)
            dqkv_out.buf[at, width : 2 * width] = nt(dkp, sp).astype(BF)
            dqkv_out.buf[at, 2 * width :] = dvp
            dqkv_out.flush(ds)
            dn = nt(jnp.concatenate([dqp, dkp, dvp], axis=1), w_in()[...])
            x = x_in(j)[at, :].astype(F32)
            scale = lax.rsqrt(jnp.sum(x * x, axis=1, keepdims=True) / dim + EPS)
            sums = sums + jnp.sum(dn * (x * scale), axis=0, keepdims=True)
            z = dn * gain_in()[...].astype(F32)
            dot_row = jnp.sum(z * x, axis=1, keepdims=True)
            es[...] = scale * z - x * (scale * scale * scale * dot_row / dim)
            esend.buf[0, at, :] = es[:, piece(ids_ref, 1, width)].astype(BF)
            esend.buf[1, at, :] = es[:, piece(ids_ref, 3, width)].astype(BF)
            esend.flush(slice(None), ds)
            ek0.buf[at, :] = es[:, piece(ids_ref, 0, width)].astype(BF)
            ek0.flush(ds)
            ek2.buf[at, :] = es[:, piece(ids_ref, 2, width)].astype(BF)
            ek2.flush(ds)
        last = pl.ds(count, EXTRA)
        es[0:8, :] = jnp.where(iota((8, dim), 0) == 0, sums, g2_in()[...])
        esend.buf[0, count:, :] = es[0:8, piece(ids_ref, 1, width)].astype(BF)
        esend.buf[1, count:, :] = es[0:8, piece(ids_ref, 3, width)].astype(BF)
        esend.flush(slice(None), last)
        ek0.buf[count:, :] = es[0:8, piece(ids_ref, 0, width)].astype(BF)
        ek0.flush(last)
        ek2.buf[count:, :] = es[0:8, piece(ids_ref, 2, width)].astype(BF)
        ek2.flush(last)

    return call(
        body,
        ids,
        [given(qkv)]
        + a_parts
        + [given(o), (lse, 1), (start_row, 1), given(cos), given(sin), given(w_qkv)]
        + [given(x), (gain, 1), (gg2, 1)],
        [
            ((count, width), BF, blocks),
            ((count, 3 * width), BF, HOLD),
            ((count + EXTRA, width), BF, blocks + 1),
            ((count + EXTRA, width), BF, HOLD),
            ((2, count + EXTRA, width), BF, blocks + 1),
        ],
        scratch=[
            pltpu.VMEM((width, count), BF),
            pltpu.VMEM((count, width), F32),
            pltpu.VMEM((count, width), F32),
            pltpu.VMEM((BLK, dim), F32),
        ],
        mib=36,
        name="attention_backward",
    )


def halves(ids_ref, size):
    y = ids_ref[1] & 1
    keep = pl.ds(pl.multiple_of(y * size, size), size)
    send = pl.ds(pl.multiple_of((1 - y) * size, size), size)
    return keep, send


def put_chunks(ids_ref, tmp, full, rel, size, keep_buf, send_buf, at):
    keep, send = halves(ids_ref, size)
    rows_ = slice(at, at + full.shape[0])
    tmp[0 : full.shape[0], :] = full
    low, high = rel & 1, rel >> 1
    keep_buf[low, high, rows_, :] = tmp[0 : full.shape[0], keep].astype(BF)
    send_buf[low, high, rows_, :] = tmp[0 : full.shape[0], send].astype(BF)


def put_low(ids_ref, tmp, full, rel, size, buf, at):
    keep, send = halves(ids_ref, size)
    rows_ = slice(at, at + full.shape[0])
    tmp[0 : full.shape[0], :] = full
    low, high = rel & 1, rel >> 1
    buf[low, 0, high, rows_, :] = tmp[0 : full.shape[0], keep].astype(BF)
    buf[low, 1, high, rows_, :] = tmp[0 : full.shape[0], send].astype(BF)


def mlp_grads(ids, left, first, second, sums, mid, ahead):
    count, dim = left.shape
    chunk = dim // 8
    units = first.shape[1]

    def body(ids_ref, ins, outs, scratch):
        first_in, left_in, second_in = ins[:3]
        send1, keep1, send2, keep2, send_sum, total, mid_out = outs
        mid_out.buf[...] = (ins[-2]()[...].astype(F32) + ins[-1]()[...].astype(F32)).astype(BF)
        tmp, buf = scratch
        z = ids_ref[1] >> 1
        for right, low_first in ((first_in, False), (second_in, True)):
            for half in range(2):
                part = left_in()[:, half * 4 * chunk : (half + 1) * 4 * chunk]
                full = tn(right()[...], part)
                for b in range(2):
                    one = full[:, b * 2 * chunk : (b + 1) * 2 * chunk]
                    rel = z ^ (2 * half + b)
                    if low_first:
                        put_low(ids_ref, tmp, one, rel, chunk, buf, 0)
                    else:
                        put_chunks(ids_ref, tmp, one, rel, chunk, keep1.buf, send1.buf, 0)
            if low_first:
                send2.buf[...] = buf[1]
                send2.flush()
                keep2.buf[...] = buf[0]
                keep2.flush()
            else:
                send1.flush()
                keep1.flush()
        for k in range(len(sums)):
            at = slice(k * size, (k + 1) * size)
            both = ins[3 + 2 * k]()[...] + ins[4 + 2 * k]()[...].astype(F32)
            send_sum.buf[at, :] = both[1].astype(BF)
            total.buf[at, :] = both[0]
        send_sum.flush()
        total.flush()

    shape = (2, 2, units, chunk)
    size = sums[0][0].shape[1]
    added = (size * len(sums), chunk)
    return call(
        body,
        ids,
        [(first, 1), (left, 1), (second, 1)] + [(a, 1) for pair in sums for a in pair] + mid,
        [(shape, BF, HOLD), (shape, BF, 1)] * 2
        + [(added, BF, HOLD), (added, F32, 1), (mid[0][0].shape, BF, HOLD)],
        scratch=[
            pltpu.VMEM((units, 2 * chunk), F32),
            pltpu.VMEM((2, 2, 2, units, chunk), BF),
        ],
        name="grads_mlp",
        ahead=ahead,
    )


def attention_grads(ids, left, right, o_pieces, parts, ahead):
    count, dim = left.shape
    chunk = dim // 8
    three = right.shape[1]
    width = three // 3
    two = 2 * width

    def body(ids_ref, ins, outs, scratch):
        left_in, right_in, o_ins, p_ins = ins[0], ins[1], ins[2:6], ins[6:9]
        send1, keep1, send2, keep2 = outs[:4]
        tmp, buf = scratch
        z = ids_ref[1] >> 1
        for half in range(2):
            part = left_in()[:, half * 4 * chunk : (half + 1) * 4 * chunk]
            full = tn(right_in()[...], part)
            for b in range(2):
                cols = slice(b * 2 * chunk, (b + 1) * 2 * chunk)
                rel = z ^ (2 * half + b)
                put_chunks(ids_ref, tmp, full[:two, cols], rel, chunk, keep1.buf, send1.buf, 0)
                put_low(ids_ref, tmp, full[two:, cols], rel, chunk, buf, 0)
        send1.flush()
        keep1.flush()
        total = p_ins[0]()[...].astype(F32)
        for p in p_ins[1:]:
            total = total + p()[...].astype(F32)
        grad = total.astype(BF)
        for flip, o in enumerate(o_ins):
            put_low(ids_ref, tmp, tn(o()[...], grad), z ^ flip, chunk, buf, width)
        send2.buf[...] = buf[1]
        send2.flush()
        keep2.buf[...] = buf[0]
        keep2.flush()
    shape = (2, 2, two, chunk)
    return call(
        body,
        ids,
        [given(left), given(right)] + [given(o) for o in o_pieces] + parts,
        [(shape, BF, HOLD), (shape, BF, 1)] * 2,
        scratch=[
            pltpu.VMEM((two, 2 * chunk), F32),
            pltpu.VMEM((2, 2, 2, two, chunk), BF),
        ],
        name="grads_att",
        ahead=ahead,
    )


def down_grads(ids, hidden, near, far):
    count, units = hidden.shape
    two = near.shape[1]
    width = two // 2
    chunk = width // 2
    half = units // 2

    def body(ids_ref, ins, outs, scratch):
        h_in, a_in, b_in = ins
        send1, keep1, send2, keep2 = outs
        tmp, buf = scratch
        for low, ref in ((0, a_in), (1, b_in)):
            full = tn(h_in()[...], ref()[...])
            for high in range(2):
                one = full[:, high * width : (high + 1) * width]
                rel = ids_ref[0] ^ (ids_ref[1] >> 1) ^ (low + 2 * high)
                put_chunks(ids_ref, tmp, one[:half], rel, chunk, keep1.buf, send1.buf, 0)
                put_low(ids_ref, tmp, one[half:], rel, chunk, buf, 0)
        send1.flush()
        keep1.flush()
        send2.buf[...] = buf[1]
        send2.flush()
        keep2.buf[...] = buf[0]
        keep2.flush()

    shape = (2, 2, half, chunk)
    return call(
        body,
        ids,
        [given(hidden), given(near), given(far)],
        [(shape, BF, HOLD), (shape, BF, 1)] * 2,
        scratch=[pltpu.VMEM((half, width), F32), pltpu.VMEM((2, 2, 2, half, chunk), BF)],
        name="grads_down",
    )


def add_pairs(ids, sums, name, ahead):
    def body(ids_ref, ins, outs, scratch):
        for k in range(len(sums)):
            add_halves(ins[2 * k](), ins[2 * k + 1](), outs[2 * k], outs[2 * k + 1])

    outs, ins = [], []
    for keep, got in sums:
        outs += [(keep.shape[1:], BF, HOLD), (keep.shape[1:], F32, 1)]
        ins += [(keep, 1), given(got)]
    return call(body, ids, ins, outs, name=name, ahead=ahead)


def flip_dp(value, bit):
    n = lax.axis_size("dp")
    return lax.ppermute(value, "dp", [(d, d ^ bit) for d in range(n)])


def flip_tensor(value, bit):
    return lax.ppermute(value, "tensor", [(d, d ^ bit) for d in range(4)])


def tie(values, *others):
    return lax.optimization_barrier((values, others))[0]


def gather_pieces(own, *others):
    two = flip_tensor(own, 2)
    one = flip_tensor(own, 1)
    three = flip_tensor(tie(two, *others) if others else two, 1)
    return (own, one, two, three)


def middle(keep2, got):
    return (keep2.astype(F32) + got[1].astype(F32)).astype(BF)


def pack_grads(ids, slot_row, parts, others, last, n_dp):
    count, width = last.shape
    per = count // n_dp
    k, m = len(parts), len(others)

    def body(ids_ref, ins, outs, scratch):
        (out,) = outs
        total = ins[k + 1]()[...].astype(F32)
        for r in ins[k + 2 : k + m + 1]:
            total = total + r()[...].astype(F32)
        gain = ins[1]()[count:, :].astype(F32)
        total = total + ins[1]()[0:count, :].astype(F32)
        for r in ins[2 : k + 1]:
            total = total + r()[0:count, :].astype(F32)
            gain = gain + r()[count:, :].astype(F32)
        gain = jnp.concatenate([gain.astype(BF)] * 2, axis=1)
        both = jnp.concatenate([total.astype(BF), ins[-1]()[...]], axis=1)
        packed = tn(picks(ins[0]()[...], 0, count), both).astype(BF)
        for d in range(n_dp):
            out.buf[d, 0:per, :] = packed[d * per : (d + 1) * per, :]
            out.buf[d, per:, :] = gain
        out.flush()

    return call(
        body,
        ids,
        [(slot_row, 1)] + parts + others + [given(last)],
        [((n_dp, per + EXTRA, 2 * width), BF, HOLD)],
        name="pack_grads",
    )[0]


def unpack_grads(ids, pos8, back):
    n_dp, padded, two = back.shape
    width = two // 2
    part = width // n_dp
    per = padded - EXTRA
    count = n_dp * per

    def body(ids_ref, ins, outs, scratch):
        a_out, b_out, gain_out = outs
        picked = picks(ins[0]()[0:1, :], 0, count)
        ref = ins[1]()
        both = tn(picked, ref[:, 0:per, :].reshape(count, two)).astype(BF)
        a_out.buf[...] = both[:, :width]
        a_out.flush()
        b_out.buf[...] = both[:, width:]
        b_out.flush()
        total = ref[0, per:, 0:width].astype(F32)
        for d in range(1, n_dp):
            total = total + ref[d, per:, 0:width].astype(F32)
        own = iota((width, part), 1) + ids_ref[1] * part
        pick = jnp.where(iota((width, part), 0) == own, 1.0, 0.0)
        gain_out.buf[...] = lax.dot_general(
            total, pick, (((1,), (0,)), ((), ())),
            precision=lax.Precision.HIGHEST, preferred_element_type=F32,
        )
        gain_out.flush()

    return call(
        body,
        ids,
        [(pos8, 1), given(back)],
        [((count, width), BF, 1), ((count, width), BF, 1), ((EXTRA, part), F32, 1)],
        name="unpack_grads",
    )


def finish_attention(ids, qk_total, vo_total, got, outs_got):
    two, chunk = qk_total.shape[1:]
    width = two // 2

    def body(ids_ref, ins, outs, scratch):
        q_out, k_out, v_out, o_out = outs
        qk, vo, add = ins[0](), ins[1](), ins[2]()
        o_out.buf[...] = ins[3]()[...].astype(F32) + ins[4]()[...].astype(F32)
        o_out.flush()
        for out, ref, at, off in ((q_out, qk, 0, 0), (k_out, qk, width, 0), (v_out, vo, 0, two)):
            total = ref[at : at + width, :] + add[off + at : off + at + width, :].astype(F32)
            out.buf[...] = jnp.transpose(total)
            out.flush()

    return call(
        body,
        ids,
        [(qk_total, 1, 0), (vo_total, 1, 0), given(got)] + [given(o) for o in outs_got],
        [((chunk, width), F32, 1)] * 3 + [((width, chunk), F32, 1)],
        name="finish_attention",
    )


def per_device(
    tokens,
    dealing,
    seq_ids,
    first_values,
    out_grad,
    norm1_gain,
    norm2_gain,
    w_query,
    w_key,
    w_value,
    w_out,
    w_gate,
    w_up,
    w_down,
):
    n_dp = lax.axis_size("dp")
    count, width = tokens.shape
    dim = norm1_gain.shape[0]
    per = count // n_dp
    t = lax.axis_index("tensor")
    d = lax.axis_index("dp")
    ids = jnp.stack([t, d]).astype(jnp.int32)
    gate_t, up_t = w_gate.T, w_up.T

    def exchange(packed):
        return lax.all_to_all(packed, "dp", split_axis=0, concat_axis=0, tiled=True)

    deal_row = dealing.reshape(1, count)
    sent, pos8 = pack_tokens(ids, deal_row, tokens, n_dp)
    arrived = exchange(sent)
    grad_far = flip_tensor(tie(out_grad, sent), 2)
    pos8 = tie(pos8, sent)
    (first_sent,) = sort_rows(ids, pos8, [(first_values, 1)], "pack_rows")
    first_sent = first_sent.reshape(n_dp, per, width)

    start = jnp.sum(seq_ids[None, :] < seq_ids[:, None], axis=1, dtype=jnp.int32)
    offset = (jnp.arange(count, dtype=jnp.int32) - start).astype(F32)
    half = HEAD_DIM // 2
    freqs = THETA ** (-jnp.arange(half, dtype=F32) / half)
    angles = offset[:, None] * jnp.tile(freqs, width // HEAD_DIM)[None, :]
    cos = jnp.cos(angles)
    sin = jnp.sin(angles)
    start_row = start.reshape(1, count)
    gain1 = norm1_gain.reshape(1, dim)
    gain2 = norm2_gain.reshape(1, dim)

    arrived = tie(arrived, first_sent, cos, sin, start_row, grad_far, gain1, gain2)
    slots = (
        arrived[:, per, :per].astype(F32) * 32.0 + arrived[:, per + 1, :per].astype(F32)
    ).astype(jnp.int32)
    slot_row = slots.reshape(1, count)
    grad_near = tie(out_grad, slot_row)
    (grad_sent,) = sort_rows(ids, pos8, [(grad_near, 1), given(grad_far)], "pack_rows")
    grad_sent = grad_sent.reshape(n_dp, per, 2 * width)
    pieces = gather_pieces(arrived, grad_sent)
    firsts = exchange(tie(first_sent, pieces[1]))
    near = exchange(tie(grad_sent, firsts, pieces[2]))
    w_pieces = gather_pieces(tie(w_out, pieces[2]))

    x, normed1, qkv, attended, lse, w_qkv = qkv_attention(
        ids, tie(slot_row, grad_sent), pieces, firsts, cos, sin, gain1, w_query, w_key, w_value,
        start_row,
    )
    near = tie(near, attended).reshape(count, 2 * width)
    near, *early = sort_rows(
        ids, slot_row, [given(near)], "sort_rows", ahead=(gate_t, up_t, w_down, x)
    )
    far = flip_tensor(near, 1)
    o_pieces = gather_pieces(attended, near)
    x1, normed2, fg, fu, hidden, yk0, yk2, ysend = feed_forward(
        ids, early[3], o_pieces, w_pieces, gain2, *early[:3]
    )
    fast = n_dp == 8
    y_got = flip_tensor(ysend, 1)
    early, sums = (), []
    if fast:
        da_send, da_keep, db_send, db_keep = down_grads(ids, hidden, near, far)
        early = (flip_dp(da_send, 1), flip_dp(db_send, 2))
        sums = [(da_keep, early[0]), (db_keep, early[1])]
        yk2 = tie(yk2, da_keep)
    y_mid = middle(yk2, y_got)
    y_far = flip_tensor(y_mid, 2)
    dgate, dup, ak0, ak2, asend, dk0, dk2, dsend, gg2 = feed_backward(
        ids, tie(x1, y_mid), near, far, fg, fu, w_pieces, gain2, gate_t, up_t, w_down
    )
    a_got = flip_tensor(tie(asend, y_far, *early), 1)
    y_sent, *down_sums = return_rows(
        ids,
        slot_row,
        [(tie(yk0, ak0), 1), (y_got, 1, 0), (y_far, 1)],
        "return_rows",
        sums,
    )
    a_mid = middle(tie(ak2, y_sent), a_got)
    a_far = flip_tensor(a_mid, 2)
    y_back = exchange(tie(y_sent, a_mid).reshape(n_dp, per, width)).reshape(count, width)
    d_got = flip_tensor(tie(dsend, a_mid), 1)
    early = ()
    held = (qkv, attended, cos, sin, w_qkv, x)
    if fast:
        da_send, da_total, db_send, db_total = down_sums
        da_got = flip_dp(tie(da_send, a_mid), 2)
        db_got = flip_dp(tie(db_send, a_mid), 1)
        dgate, dup = tie((dgate, dup), a_mid)
        gate_send, gate_keep, up_send, up_keep, down_send, down_sum, d_mid, *held = mlp_grads(
            ids, normed2, dgate, dup, [(da_total, da_got), (db_total, db_got)],
            [given(dk2), given(d_got, 1)], held,
        )
        a_far = tie(a_far, gate_keep)
        gate_got = flip_dp(gate_send, 1)
        up_got = flip_dp(up_send, 2)
        down_got = flip_dp(down_send, 4)
        early = (gate_got, up_got, down_got)
    else:
        d_mid = middle(dk2, d_got)
    a_far = tie(a_far, d_mid)
    d_far = flip_tensor(tie(d_mid, a_far), 2)
    dvp, dqkv, ek0, ek2, esend = attention_backward(
        ids, *held[:2], lse, [(ak0, 1), given(a_got, 0), given(a_far)], start_row, *held[2:4],
        held[5], gain1, held[4], gg2,
    )
    e_got = flip_tensor(tie(esend, d_far, y_back, *early), 1)
    if fast:
        gate_send, gate_total, up_send, up_total, *held = add_pairs(
            ids, [(tie(gate_keep, ek2), gate_got), (up_keep, up_got)], "add_pairs",
            (normed1, *o_pieces, dk0, d_far),
        )
        ek2 = tie(ek2, gate_send)
    e_mid = middle(ek2, e_got)
    e_far = flip_tensor(e_mid, 2)
    if fast:
        gate_got = flip_dp(tie(gate_send, e_mid), 2)
        up_got = flip_dp(tie(up_send, e_mid), 1)
        qk_send, qk_keep, vo_send, vo_keep, *held = attention_grads(
            ids, held[0], tie(dqkv, e_mid), held[1:5],
            [given(held[5]), (d_got, 1, 0), given(held[6])], (ek0, dvp, dk0, d_far),
        )
        ek0, dvp, dk0, d_far = held
        qk_got = flip_dp(qk_send, 1)
        vo_got = flip_dp(vo_send, 2)

        def plus(keep, got, *after):
            return keep.astype(F32) + tie(got, *after).astype(F32)

        gate_total = plus(gate_total, gate_got, qk_keep)
        up_total = plus(up_total, up_got, qk_keep)
        mlp_send = jnp.concatenate([gate_total[1], up_total[1]], axis=0).astype(BF)
        mlp_keep = jnp.concatenate([gate_total[0], up_total[0]], axis=0)
        e_far = tie(e_far, mlp_send)
        mlp_got = flip_dp(mlp_send, 4)
    i_sent = pack_grads(
        ids, slot_row, [given(ek0), (e_got, 1, 0), given(e_far)],
        [given(dk0), (d_got, 1, 0), given(d_far)], dvp, n_dp,
    )
    i_back = exchange(i_sent)
    (output,) = restore_rows(ids, pos8, [tie(y_back, i_sent)], "restore_rows")
    input_grad, first_grad, gain_rows = unpack_grads(ids, pos8, i_back)
    if fast:
        units = w_down.shape[0]
        mlp_total = plus(mlp_keep, mlp_got, output)
        qk_total = plus(qk_keep, qk_got, output)
        vo_total = plus(vo_keep, vo_got, output)
        qk_total = plus(qk_total[0], flip_dp(qk_total[1].astype(BF), 2))
        vo_total = plus(vo_total[0], flip_dp(vo_total[1].astype(BF), 1))
        vo_low = vo_total[:, width:].astype(BF)
        outs_got = [
            lax.ppermute(
                vo_low[b],
                ("dp", "tensor"),
                [
                    ((2 * z + y) * 4 + r, (2 * r + y) * 4 + (r ^ z ^ (2 * b)))
                    for z in range(4)
                    for y in range(2)
                    for r in range(4)
                ],
            )
            for b in range(2)
        ]
        att_send = jnp.concatenate([qk_total[1], vo_total[1, :width]], axis=0).astype(BF)
        att_got = flip_dp(att_send, 4)
        gw_q, gw_k, gw_v, gw_out = finish_attention(
            ids, qk_total, vo_total, tie(att_got, input_grad), outs_got
        )
        gw_down = plus(down_sum, down_got, i_sent)
        gw_gate, gw_up = mlp_total[:units].T, mlp_total[units:].T
    else:

        def scattered(left, right, dim_):
            full = jnp.einsum("ta,tb->ab", left, right, preferred_element_type=F32)
            return lax.psum_scatter(full, "dp", scatter_dimension=dim_, tiled=True)

        def natural(parts):
            full = jnp.zeros((count, dim), BF)
            for flip, part in enumerate(parts):
                full = lax.dynamic_update_slice(full, part, (0, (t ^ flip) * width))
            return full

        dy = natural((near[:, :width], far[:, :width], near[:, width:], far[:, width:]))
        dx1 = (dk0 + d_got[0].astype(F32) + d_far.astype(F32)).astype(BF)
        dx1 = lax.all_gather(dx1, "tensor", axis=1, tiled=True)
        gw_gate = scattered(normed2, dgate, 0)
        gw_up = scattered(normed2, dup, 0)
        gw_down = scattered(hidden, dy, 1)
        gw_q, gw_k, gw_v = [scattered(normed1, p, 0) for p in jnp.split(dqkv, 3, axis=1)]
        gw_out = scattered(attended, dx1, 1)

    return (
        output,
        input_grad,
        first_grad,
        gain_rows[0:1],
        gain_rows[1:2],
        gw_q,
        gw_k,
        gw_v,
        gw_out,
        gw_gate,
        gw_up,
        gw_down,
    )


def solution(mesh):
    in_specs = (
        P("dp", "tensor"),
        P("dp"),
        P("dp"),
        P("dp", "tensor"),
        P("dp", "tensor"),
        P(),
        P(),
        P(None, "tensor"),
        P(None, "tensor"),
        P(None, "tensor"),
        P("tensor", None),
        P(None, "tensor"),
        P(None, "tensor"),
        P("tensor", None),
    )
    out_specs = (
        P("dp", "tensor"),
        P("dp", "tensor"),
        P("dp", "tensor"),
        P("tensor", "dp"),
        P("tensor", "dp"),
        P("dp", "tensor"),
        P("dp", "tensor"),
        P("dp", "tensor"),
        P("tensor", "dp"),
        P("dp", "tensor"),
        P("dp", "tensor"),
        P("tensor", "dp"),
    )
    return jax.shard_map(
        per_device, mesh=mesh, in_specs=in_specs, out_specs=out_specs, check_vma=False
    )
```

```python
import functools

import jax
import jax.numpy as jnp
from jax import lax
from jax.experimental import pallas as pl
from jax.experimental.pallas import tpu as pltpu
from jax.sharding import PartitionSpec as P

HEAD_DIM = 64
EPS = 1e-06
THETA = 10000.0
NEG = -1e30
BF = jnp.bfloat16
F32 = jnp.float32
BLK = 256
EXTRA = 8
MIB = 1 << 20


def nn(a, b):
    return lax.dot_general(a, b, (((1,), (0,)), ((), ())), preferred_element_type=F32)


def nt(a, b):
    return lax.dot_general(a, b, (((1,), (1,)), ((), ())), preferred_element_type=F32)


def tn(a, b):
    return lax.dot_general(a, b, (((0,), (0,)), ((), ())), preferred_element_type=F32)


def iota(shape, dim):
    return lax.broadcasted_iota(jnp.int32, shape, dim)


TIMES = {
    "pack_tokens": 3,
    "pack_rows": 3,
    "qkv_attention": 14,
    "feed_forward": 12,
    "sort_rows": 3,
    "grads_down": 5,
    "feed_backward": 15,
    "grads_mlp": 8,
    "return_rows": 3,
    "attention_backward": 17,
    "grads_att": 8,
    "pack_grads": 4,
    "unpack_grads": 4,
    "restore_rows": 3,
    "add_pairs": 3,
    "finish_attention": 2,
}


SCALE_F = 1_150_000_000 // 16
SCALE_B = 3_690_000 // 16


class Fetched:
    def __init__(self, src, buf, sems, base, parts):
        self.buf = buf
        size = src.shape[0] // parts if parts else 0
        self.copies = [
            pltpu.make_async_copy(
                src.at[pl.ds(p * size, size)], buf.at[pl.ds(p * size, size)], sems.at[base + p]
            )
            for p in range(parts)
        ]
        self.waited = [False] * parts

    def __call__(self, part=None):
        one = part is not None and len(self.copies) > 1
        for p in (part,) if one else range(len(self.copies)):
            if not self.waited[p]:
                self.copies[p].wait()
                self.waited[p] = True
        return self.buf


class Stored:
    def __init__(self, dst, buf, sems, base):
        self.dst, self.buf, self.sems, self.at = dst, buf, sems, base
        self.copies = []

    def flush(self, *index):
        if self.sems is None:
            return
        src = self.buf.at[index] if index else self.buf
        dst = self.dst.at[index] if index else self.dst
        c = pltpu.make_async_copy(src, dst, self.sems.at[self.at + len(self.copies)])
        c.start()
        self.copies.append(c)


def call(body, ids, ins, outs, scratch=(), mib=28, name=None, ahead=()):
    ins = [tuple(i) + (None,)[len(i) - 2 :] for i in ins]
    took = TIMES[name]
    n_in, n_out = len(ins), len(outs)
    in_at = [sum(i[1] for i in ins[:k]) for k in range(n_in + 1)]
    out_at = [sum(o[2] for o in outs[:k]) for k in range(n_out + 1)]
    stored = [k for k in range(n_out) if outs[k][2] != HOLD]
    fetched = [k for k in range(n_in) if ins[k][1] != HOLD]
    n_ahead = len(ahead)

    def kernel(ids_ref, *refs):
        srcs, refs = refs[:n_in], refs[n_in:]
        early, refs = refs[:n_ahead], refs[n_ahead:]
        dsts, refs = refs[:n_out], refs[n_out:]
        late, refs = refs[:n_ahead], refs[n_ahead:]
        bufs, refs = refs[: len(fetched)], refs[len(fetched) :]
        obufs, refs = refs[: len(stored)], refs[len(stored) :]
        in_sems, out_sems, refs = refs[0], refs[1], refs[2:]
        srcs = [src if i[2] is None else src.at[i[2]] for src, i in zip(srcs, ins)]
        inputs = [Fetched(None, src, None, 0, 0) for src in srcs]
        for k, buf in zip(fetched, bufs):
            inputs[k] = Fetched(srcs[k], buf, in_sems, in_at[k], ins[k][1])
        outputs = [Stored(None, dst, None, 0) for dst in dsts]
        for k, buf in zip(stored, obufs):
            outputs[k] = Stored(dsts[k], buf, out_sems, out_at[k])
        for p in range(max(i[1] for i in ins)):
            for i in inputs:
                if p < len(i.copies):
                    i.copies[p].start()
        copies = [
            pltpu.make_async_copy(a, b, in_sems.at[in_at[-1] + k])
            for k, (a, b) in enumerate(zip(early, late))
        ]
        for c in copies:
            c.start()
        body(ids_ref, inputs, outputs, refs)
        for i in inputs:
            i()
        for k in stored:
            assert len(outputs[k].copies) == outs[k][2]
            for c in outputs[k].copies:
                c.wait()
        for c in copies:
            c.wait()

    return pl.pallas_call(
        kernel,
        out_shape=tuple(
            (pltpu.HBM if k in stored else pltpu.VMEM)(s, d) for k, (s, d, _) in enumerate(outs)
        )
        + tuple(pltpu.VMEM(a.shape, a.dtype) for a in ahead),
        in_specs=[pl.BlockSpec(memory_space=pltpu.SMEM)]
        + [
            pl.BlockSpec(memory_space=pl.ANY if k in fetched else pltpu.VMEM) for k in range(n_in)
        ]
        + [pl.BlockSpec(memory_space=pl.ANY)] * n_ahead,
        out_specs=tuple(
            pl.BlockSpec(memory_space=pl.ANY if k in stored else pltpu.VMEM) for k in range(n_out)
        )
        + tuple(pl.BlockSpec(memory_space=pltpu.VMEM) for _ in ahead),
        scratch_shapes=[
            pltpu.VMEM(a.shape if index is None else a.shape[1:], a.dtype)
            for a, _, index in (ins[k] for k in fetched)
        ]
        + [pltpu.VMEM(outs[k][0], outs[k][1]) for k in stored]
        + [
            pltpu.SemaphoreType.DMA((max(in_at[-1] + n_ahead, 1),)),
            pltpu.SemaphoreType.DMA((max(out_at[-1], 1),)),
        ]
        + list(scratch),
        compiler_params=pltpu.CompilerParams(vmem_limit_bytes=mib * MIB),
        cost_estimate=pl.CostEstimate(
            flops=took * SCALE_F, transcendentals=0, bytes_accessed=took * SCALE_B
        ),
        name=name,
    )(
        ids,
        *[
            pltpu.with_memory_space_constraint(a, pltpu.VMEM if parts == HOLD else pltpu.HBM)
            for a, parts, _ in ins
        ],
        *[pltpu.with_memory_space_constraint(a, pltpu.HBM) for a in ahead],
    )


HOLD = 0


def given(array, index=None):
    return (array, HOLD, index)


def own_first(pieces, parts=1):
    return [(pieces[0], parts)] + [given(p) for p in pieces[1:]]


def piece(ids_ref, flip, width):
    return pl.ds(pl.multiple_of((ids_ref[0] ^ flip) * width, width), width)


def picks(index, first, size):
    shape = (size, index.shape[1])
    return jnp.where(iota(shape, 0) + first == index, 1.0, 0.0).astype(BF)


def pack_tokens(ids, deal_row, tok, n_dp):
    count, width = tok.shape
    per = count // n_dp
    lanes = 128

    def body(ids_ref, ins, outs, scratch):
        deal_in, tok_in = ins
        out, pos_out = outs
        deal = deal_in()[...]
        dest = deal // count
        slot = deal % count
        oh = jnp.where(iota((n_dp, count), 0) == dest, 1.0, 0.0)
        upto = jnp.where(iota((lanes, lanes), 0) <= iota((lanes, lanes), 1), 1.0, 0.0)
        parts = [oh[:, b * lanes : (b + 1) * lanes] for b in range(count // lanes)]
        inner = nn(jnp.concatenate(parts, axis=0).astype(BF), upto.astype(BF))
        base = (iota((n_dp, 1), 0) * per - 1).astype(F32)
        rows_ = []
        for b, part in enumerate(parts):
            seen = inner[b * n_dp : (b + 1) * n_dp]
            rows_.append(jnp.sum(part * (seen + base), axis=0, keepdims=True))
            base = base + seen[:, lanes - 1 :]
        pos = jnp.concatenate(rows_, axis=1).astype(jnp.int32)
        pos_out.buf[...] = jnp.broadcast_to(pos, (8, count))
        pos_out.flush()
        high = jnp.broadcast_to(slot // 32, (8, count))
        low = jnp.broadcast_to(slot % 32, (8, count))
        hl = jnp.where(iota((8, count), 0) == 0, high, low).astype(F32).astype(BF)
        out.buf[:, per : per + EXTRA, :] = jnp.zeros((n_dp, EXTRA, width), BF)
        size = min(count, 512)
        group = size // per
        for g in range(count // size):
            pick = picks(pos, g * size, size)
            moved = nn(pick, tok_in()[...]).astype(BF)
            marks = nt(hl, pick).astype(BF)
            for e in range(group):
                d = g * group + e
                out.buf[d, 0:per, :] = moved[e * per : (e + 1) * per]
                out.buf[d, per : per + 8, 0:per] = marks[:, e * per : (e + 1) * per]
            out.flush(pl.ds(g * group, group))

    return call(
        body,
        ids,
        [(deal_row, 1), (tok, 1)],
        [
            ((n_dp, per + EXTRA, width), BF, HOLD),
            ((8, count), jnp.int32, 1),
        ],
        name="pack_tokens",
    )


def sort_rows(ids, index, parts, name, ahead=()):
    count, width = parts[0][0].shape
    blocks = 2
    size = count // blocks

    def body(ids_ref, ins, outs, scratch):
        idx = ins[0]()[0:1, :]
        (out,) = outs
        for b in range(blocks):
            at = slice(b * size, (b + 1) * size)
            pick = picks(idx, b * size, size)
            for k, part in enumerate(ins[1:]):
                out.buf[at, k * width : (k + 1) * width] = nn(pick, part()[...]).astype(BF)
            out.flush(pl.ds(b * size, size))

    return call(
        body,
        ids,
        [(index, 1)] + parts,
        [((count, width * len(parts)), BF, HOLD)],
        name=name,
        ahead=ahead,
    )


def add_halves(keep, got, send_out, total_out):
    sums = keep[...].astype(F32) + got[...].astype(F32)
    send_out.buf[...] = sums[1].astype(BF)
    send_out.flush()
    total_out.buf[...] = sums[0]
    total_out.flush()


def return_rows(ids, index, parts, name, sums=()):
    count, width = parts[0][0].shape[-2:]
    m = 1 + len(parts)

    def body(ids_ref, ins, outs, scratch):
        total = ins[1]()[...]
        for r in ins[2:m]:
            total = total.astype(F32) + r()[...].astype(F32)
        outs[0].buf[...] = tn(picks(ins[0]()[0:1, :], 0, count), total.astype(BF)).astype(BF)
        outs[0].flush()
        for k in range(len(sums)):
            at = m + 2 * k
            add_halves(ins[at](), ins[at + 1](), outs[1 + 2 * k], outs[2 + 2 * k])

    outs = [((count, width), BF, HOLD)]
    ins = [(index, 1)] + parts
    for keep, got in sums:
        outs += [(keep.shape[1:], BF, HOLD), (keep.shape[1:], F32, 1)]
        ins += [(keep, 1), (got, 1)]
    return call(body, ids, ins, outs, name=name)


def restore_rows(ids, index, backs, name):
    count, width = backs[0].shape

    def body(ids_ref, ins, outs, scratch):
        pick = picks(ins[0]()[0:1, :], 0, count)
        both = tn(pick, jnp.concatenate([b()[...] for b in ins[1:]], axis=1)).astype(BF)
        for k, out in enumerate(outs):
            out.buf[...] = both[:, k * width : (k + 1) * width]
            out.flush()

    return call(
        body,
        ids,
        [(index, 1)] + [(b, 1) for b in backs],
        [((count, width), BF, 1)] * len(backs),
        name=name,
    )


def head_mask(shape, head, split):
    lane = iota(shape, 1)
    if split:
        return (lane % (shape[1] // 2)) // (HEAD_DIM // 2) == head
    return lane // HEAD_DIM == head


def split_perm(width):
    half = HEAD_DIM // 2
    src = iota((width, width), 0)
    dst = iota((width, width), 1)
    second = dst // (width // 2)
    rest = dst % (width // 2)
    want = (rest // half) * HEAD_DIM + second * half + rest % half
    return (src == want).astype(F32).astype(BF)


def qkv_attention(ids, slot_row, pieces, firsts, cos, sin, gain, wq, wk, wv, start_row):
    n_dp, padded, width = pieces[0].shape
    per = firsts.shape[1]
    count = n_dp * per
    dim = gain.shape[1]
    heads = width // HEAD_DIM
    blocks = count // BLK
    half = width // 2

    def body(ids_ref, ins, outs, scratch):
        slot_in, x0, x1, x2, x3, fv_in, wq_in, wk_in, wv_in, cos_in, sin_in, gain_in, start_in = ins
        x_out, n_out, qkv_out, o_out, lse_out, w_out = outs
        cat, vt = scratch
        slots = slot_in()[...]
        for flip, ref in enumerate((x0, x1, x2, x3)):
            cat[:, piece(ids_ref, flip, width)] = ref()[:, 0:per, :].reshape(count, width)
        cat[:, dim:] = fv_in()[...].reshape(count, width)
        sp = split_perm(width)
        w_out.buf[:, 0:width] = nn(wq_in()[...], sp).astype(BF)
        w_out.buf[:, width : 2 * width] = nn(wk_in()[...], sp).astype(BF)
        w_out.buf[:, 2 * width :] = wv_in()[...]
        w_out.flush()
        lse_out.buf[...] = jnp.zeros_like(lse_out.buf)

        def rope(v, c, s):
            a, b = v[:, :half], v[:, half:]
            return jnp.concatenate([a * c - b * s, b * c + a * s], axis=1).astype(BF)

        for j in range(blocks):
            at = slice(j * BLK, (j + 1) * BLK)
            ds = pl.ds(j * BLK, BLK)
            moved = nn(picks(slots, j * BLK, BLK), cat[...])
            x = moved[:, :dim]
            x_out.buf[at, :] = x.astype(BF)
            x_out.flush(ds)
            scale = lax.rsqrt(jnp.sum(x * x, axis=1, keepdims=True) / dim + EPS)
            normed = (x * scale * gain_in()[...].astype(F32)).astype(BF)
            n_out.buf[at, :] = normed
            n_out.flush(ds)
            qkv = nn(normed, w_out.buf[...])
            c, s = cos_in(j)[at, :], sin_in(j)[at, :]
            q = rope(qkv[:, 0:width], c, s)
            v = 0.5 * qkv[:, 2 * width :] + 0.5 * moved[:, dim:]
            q = (q.astype(F32) * HEAD_DIM ** (-0.5)).astype(BF)
            qkv_out.buf[at, 0:width] = q
            qkv_out.buf[at, width : 2 * width] = rope(qkv[:, width : 2 * width], c, s)
            qkv_out.buf[at, 2 * width :] = v.astype(BF)
            qkv_out.flush(ds)
            vt[:, at] = jnp.transpose(v).astype(BF)
            start = start_in()[:, at]
            n = (j + 1) * BLK
            keys = qkv_out.buf[0:n, width : 2 * width]
            key = iota((n, BLK), 0)
            valid = (key >= start) & (key <= iota((n, BLK), 1) + j * BLK)
            out = []
            for h in range(heads):
                qh = jnp.where(head_mask((BLK, width), h, True), q, jnp.zeros_like(q))
                sc = jnp.where(valid, nt(keys, qh), NEG)
                top = jnp.max(sc, axis=0, keepdims=True)
                ex = jnp.exp(sc - top)
                total = jnp.sum(ex, axis=0, keepdims=True)
                vals = vt[h * HEAD_DIM : (h + 1) * HEAD_DIM, 0:n]
                out.append(nn(vals, ex.astype(BF)) * (1.0 / total))
                lse_out.buf[h : h + 1, at] = top + jnp.log(total)
            o_out.buf[at, :] = jnp.transpose(jnp.concatenate(out, axis=0)).astype(BF)
            o_out.flush(ds)
        lse_out.flush()

    return call(
        body,
        ids,
        [(slot_row, 1)]
        + [given(p) for p in pieces]
        + [given(firsts)]
        + [(wq, 1), (wk, 1), (wv, 1), (cos, 1), (sin, 1), (gain, 1), (start_row, 1)],
        [
            ((count, dim), BF, blocks),
            ((count, dim), BF, blocks),
            ((count, 3 * width), BF, blocks),
            ((count, width), BF, HOLD),
            ((8, count), F32, 1),
            ((dim, 3 * width), BF, 1),
        ],
        scratch=[pltpu.VMEM((count, dim + width), BF), pltpu.VMEM((width, count), BF)],
        name="qkv_attention",
    )


FEED = 512


def feed_forward(ids, x, o_pieces, w_pieces, gain, w_gate, w_up, w_down):
    count, dim = x.shape
    width = o_pieces[0].shape[1]
    units = w_gate.shape[0]
    size = min(FEED, count)
    blocks = count // size

    def body(ids_ref, ins, outs, scratch):
        w_ins, o_ins = ins[0:4], ins[4:8]
        x_in, gain_in, wg_in, wu_in, wd_in = ins[8:]
        x1_out, n_out, fg_out, fu_out, h_out, yk0, yk2, ysend = outs
        ys, xs, wo = scratch
        for k, w in enumerate(w_ins):
            wo[k * width : (k + 1) * width, :] = w()[...]
        for j in range(blocks):
            at = slice(j * size, (j + 1) * size)
            ds = pl.ds(j * size, size)
            heads = jnp.concatenate([o(j)[at, :] for o in o_ins], axis=1)
            x1 = x_in(j)[at, :].astype(F32) + nn(heads, wo[...])
            xs[...] = x1
            x1_out.buf[at, :] = x1.astype(BF)
            x1_out.flush(ds)
            scale = lax.rsqrt(jnp.sum(x1 * x1, axis=1, keepdims=True) / dim + EPS)
            normed = (x1 * scale * gain_in()[...].astype(F32)).astype(BF)
            n_out.buf[at, :] = normed
            n_out.flush(ds)
            g = nt(normed, wg_in()[...])
            u = nt(normed, wu_in()[...])
            sg = jax.nn.sigmoid(g)
            silu = g * sg
            hid = (silu * u).astype(BF)
            h_out.buf[at, :] = hid
            h_out.flush(ds)
            fu_out.buf[at, :] = silu.astype(BF)
            fu_out.flush(ds)
            fg_out.buf[at, :] = (u * sg * (1.0 + g * (1.0 - sg))).astype(BF)
            fg_out.flush(ds)
            ys[...] = nn(hid, wd_in()[...])
            ysend.buf[0, at, :] = ys[:, piece(ids_ref, 1, width)].astype(BF)
            ysend.buf[1, at, :] = ys[:, piece(ids_ref, 3, width)].astype(BF)
            ysend.flush(slice(None), ds)
            own = piece(ids_ref, 0, width)
            yk0.buf[at, :] = (ys[:, own] + xs[:, own]).astype(BF)
            yk0.flush(ds)
            yk2.buf[at, :] = ys[:, piece(ids_ref, 2, width)].astype(BF)
            yk2.flush(ds)

    return call(
        body,
        ids,
        [(w, 1) for w in w_pieces]
        + own_first(o_pieces)
        + [given(x), (gain, 1), given(w_gate), given(w_up), given(w_down)],
        [
            ((count, dim), BF, blocks),
            ((count, dim), BF, blocks),
            ((count, units), BF, blocks),
            ((count, units), BF, blocks),
            ((count, units), BF, HOLD),
            ((count, width), BF, blocks),
            ((count, width), BF, HOLD),
            ((2, count, width), BF, HOLD),
        ],
        scratch=[
            pltpu.VMEM((size, dim), F32),
            pltpu.VMEM((size, dim), F32),
            pltpu.VMEM((4 * width, dim), BF),
        ],
        mib=44,
        name="feed_forward",
    )


def feed_backward(ids, x1, near, far, fg, fu, w_pieces, gain, w_gate, w_up, w_down):
    count, dim = x1.shape
    width = w_pieces[0].shape[0]
    units = w_gate.shape[0]
    size = min(FEED, count)
    blocks = count // size

    def body(ids_ref, ins, outs, scratch):
        wd_in, fg_in, fu_in, wg_in, wu_in, x1_in, near_in, far_in, gain_in = ins[:9]
        w_ins = ins[9:]
        dg_out, du_out, ak0, ak2, asend, dk0, dk2, dsend, gg_out = outs
        ds_, ys, wo = scratch
        sums = jnp.zeros((1, dim), F32)
        for j in range(blocks):
            at = slice(j * size, (j + 1) * size)
            ds = pl.ds(j * size, size)
            near_, far_ = near_in(j)[at, :], far_in(j)[at, :]
            ys[:, piece(ids_ref, 0, width)] = near_[:, :width]
            ys[:, piece(ids_ref, 2, width)] = near_[:, width:]
            ys[:, piece(ids_ref, 1, width)] = far_[:, :width]
            ys[:, piece(ids_ref, 3, width)] = far_[:, width:]
            dy = ys[...]
            dh = nt(dy, wd_in()[...])
            dg = (dh * fg_in(j)[at, :].astype(F32)).astype(BF)
            du = (dh * fu_in(j)[at, :].astype(F32)).astype(BF)
            dg_out.buf[at, :] = dg
            du_out.buf[at, :] = du
            dg_out.flush(ds)
            du_out.flush(ds)
            dn = nn(dg, wg_in()[...]) + nn(du, wu_in()[...])
            x1 = x1_in(j)[at, :].astype(F32)
            scale = lax.rsqrt(jnp.sum(x1 * x1, axis=1, keepdims=True) / dim + EPS)
            sums = sums + jnp.sum(dn * (x1 * scale), axis=0, keepdims=True)
            z = dn * gain_in()[...].astype(F32)
            dot_row = jnp.sum(z * x1, axis=1, keepdims=True)
            part = scale * z - x1 * (scale * scale * scale * dot_row / dim)
            part = part + 0.25 * dy.astype(F32)
            ds_[...] = part
            if j == 0:
                for k, w in enumerate(w_ins):
                    wo[k * width : (k + 1) * width, :] = w()[...]
            da = nt(part.astype(BF), wo[...])
            asend.buf[0, at, :] = da[:, width : 2 * width].astype(BF)
            asend.buf[1, at, :] = da[:, 3 * width :].astype(BF)
            asend.flush(slice(None), ds)
            ak0.buf[at, :] = da[:, 0:width].astype(BF)
            ak0.flush(ds)
            ak2.buf[at, :] = da[:, 2 * width : 3 * width].astype(BF)
            ak2.flush(ds)
            dsend.buf[0, at, :] = ds_[:, piece(ids_ref, 1, width)].astype(BF)
            dsend.buf[1, at, :] = ds_[:, piece(ids_ref, 3, width)].astype(BF)
            dsend.flush(slice(None), ds)
            dk0.buf[at, :] = ds_[:, piece(ids_ref, 0, width)].astype(BF)
            dk0.flush(ds)
            dk2.buf[at, :] = ds_[:, piece(ids_ref, 2, width)].astype(BF)
            dk2.flush(ds)
        gg_out.buf[...] = jnp.broadcast_to(sums, (8, dim))
        gg_out.flush()

    return call(
        body,
        ids,
        [(w_down, 1), (fg, 1), (fu, 1), (w_gate, 1), (w_up, 1), (x1, 1)]
        + [given(near), given(far), (gain, 1)]
        + [(w, 1) for w in w_pieces],
        [
            ((count, units), BF, blocks),
            ((count, units), BF, blocks),
            ((count, width), BF, blocks),
            ((count, width), BF, HOLD),
            ((2, count, width), BF, HOLD),
            ((count, width), BF, blocks),
            ((count, width), BF, HOLD),
            ((2, count, width), BF, HOLD),
            ((8, dim), F32, 1),
        ],
        scratch=[
            pltpu.VMEM((size, dim), F32),
            pltpu.VMEM((size, dim), BF),
            pltpu.VMEM((4 * width, dim), BF),
        ],
        mib=44,
        name="feed_backward",
    )


def attention_backward(
    ids, qkv, o, lse, a_parts, start_row, cos, sin, x, gain, w_qkv, gg2
):
    count, width = o.shape
    dim = x.shape[1]
    heads = width // HEAD_DIM
    blocks = count // BLK
    half = width // 2
    part = HEAD_DIM // 2

    def body(ids_ref, ins, outs, scratch):
        qkv_in, a0, a1, a2, o_in, lse_in, start_in, cos_in, sin_in, w_in, x_in, gain_in, g2_in = ins
        dv_out, dqkv_out, ek0, ek2, esend = outs
        kt, dk, dv, es = scratch
        qkv_ref = qkv_in()
        for b in range(blocks):
            at = slice(b * BLK, (b + 1) * BLK)
            kt[:, at] = jnp.transpose(qkv_ref[at, width : 2 * width].astype(F32)).astype(BF)
        sums = jnp.zeros((1, dim), F32)
        pick = (iota((8, width), 1) // HEAD_DIM == iota((8, width), 0)).astype(F32)
        sp = split_perm(width)

        def rope_back(g, c, s):
            a, b = g[:, :half], g[:, half:]
            return jnp.concatenate([a * c + b * s, b * c - a * s], axis=1).astype(BF)

        for j in reversed(range(blocks)):
            at = slice(j * BLK, (j + 1) * BLK)
            ds = pl.ds(j * BLK, BLK)
            q = qkv_ref[at, 0:width]
            do = (a0(j)[at, :].astype(F32) + a1(j)[at, :].astype(F32) + a2(j)[at, :].astype(F32)).astype(BF)
            prod = do.astype(F32) * o_in(j)[at, :].astype(F32)
            delta = lax.dot_general(
                pick, prod, (((1,), (1,)), ((), ())),
                precision=lax.Precision.HIGHEST, preferred_element_type=F32,
            )
            start = start_in()[:, at]
            lse = lse_in()[:, at]
            n = (j + 1) * BLK
            keys = qkv_ref[0:n, width : 2 * width]
            vals = qkv_ref[0:n, 2 * width :]
            key = iota((n, BLK), 0)
            valid = (key >= start) & (key <= iota((n, BLK), 1) + j * BLK)
            probs, grads, q_heads, do_heads = [], [], [], []
            first, second = [], []
            for h in range(heads):
                qh = jnp.where(head_mask((BLK, width), h, True), q, jnp.zeros_like(q))
                dh = jnp.where(head_mask((BLK, width), h, False), do, jnp.zeros_like(do))
                sc = jnp.where(valid, nt(keys, qh) - lse[h : h + 1, :], NEG)
                pr = jnp.exp(sc)
                dsc = (pr * (nt(vals, dh) - delta[h : h + 1, :])).astype(BF)
                probs.append(pr.astype(BF))
                grads.append(dsc)
                q_heads.append(qh)
                do_heads.append(dh)
                kh = jnp.concatenate(
                    [
                        kt[h * part : (h + 1) * part, 0:n],
                        kt[half + h * part : half + (h + 1) * part, 0:n],
                    ],
                    axis=0,
                )
                dqh = nn(kh, dsc)
                first.append(dqh[:part])
                second.append(dqh[part:])
            dvn = nn(jnp.concatenate(probs, 1), jnp.concatenate(do_heads, 0))
            dkn = nn(jnp.concatenate(grads, 1), jnp.concatenate(q_heads, 0))
            if j == blocks - 1:
                dv[...] = dvn
                dk[...] = dkn
            else:
                dv[0:n, :] += dvn
                dk[0:n, :] += dkn
            dqj = jnp.transpose(jnp.concatenate(first + second, axis=0)) * HEAD_DIM ** (-0.5)
            c, s = cos_in(j)[at, :], sin_in(j)[at, :]
            dqp = rope_back(dqj, c, s)
            dkp = rope_back(dk[at, :], c, s)
            dvp = (0.5 * dv[at, :].astype(BF).astype(F32)).astype(BF)
            dv_out.buf[at, :] = dvp
            dv_out.flush(ds)
            dqkv_out.buf[at, 0:width] = nt(dqp, sp).astype(BF)
            dqkv_out.buf[at, width : 2 * width] = nt(dkp, sp).astype(BF)
            dqkv_out.buf[at, 2 * width :] = dvp
            dqkv_out.flush(ds)
            dn = nt(jnp.concatenate([dqp, dkp, dvp], axis=1), w_in()[...])
            x = x_in(j)[at, :].astype(F32)
            scale = lax.rsqrt(jnp.sum(x * x, axis=1, keepdims=True) / dim + EPS)
            sums = sums + jnp.sum(dn * (x * scale), axis=0, keepdims=True)
            z = dn * gain_in()[...].astype(F32)
            dot_row = jnp.sum(z * x, axis=1, keepdims=True)
            es[...] = scale * z - x * (scale * scale * scale * dot_row / dim)
            esend.buf[0, at, :] = es[:, piece(ids_ref, 1, width)].astype(BF)
            esend.buf[1, at, :] = es[:, piece(ids_ref, 3, width)].astype(BF)
            esend.flush(slice(None), ds)
            ek0.buf[at, :] = es[:, piece(ids_ref, 0, width)].astype(BF)
            ek0.flush(ds)
            ek2.buf[at, :] = es[:, piece(ids_ref, 2, width)].astype(BF)
            ek2.flush(ds)
        last = pl.ds(count, EXTRA)
        es[0:8, :] = jnp.where(iota((8, dim), 0) == 0, sums, g2_in()[...])
        esend.buf[0, count:, :] = es[0:8, piece(ids_ref, 1, width)].astype(BF)
        esend.buf[1, count:, :] = es[0:8, piece(ids_ref, 3, width)].astype(BF)
        esend.flush(slice(None), last)
        ek0.buf[count:, :] = es[0:8, piece(ids_ref, 0, width)].astype(BF)
        ek0.flush(last)
        ek2.buf[count:, :] = es[0:8, piece(ids_ref, 2, width)].astype(BF)
        ek2.flush(last)

    return call(
        body,
        ids,
        [given(qkv)]
        + a_parts
        + [given(o), (lse, 1), (start_row, 1), given(cos), given(sin), given(w_qkv)]
        + [given(x), (gain, 1), (gg2, 1)],
        [
            ((count, width), BF, blocks),
            ((count, 3 * width), BF, blocks),
            ((count + EXTRA, width), BF, blocks + 1),
            ((count + EXTRA, width), BF, HOLD),
            ((2, count + EXTRA, width), BF, blocks + 1),
        ],
        scratch=[
            pltpu.VMEM((width, count), BF),
            pltpu.VMEM((count, width), F32),
            pltpu.VMEM((count, width), F32),
            pltpu.VMEM((BLK, dim), F32),
        ],
        mib=36,
        name="attention_backward",
    )


def halves(ids_ref, size):
    y = ids_ref[1] & 1
    keep = pl.ds(pl.multiple_of(y * size, size), size)
    send = pl.ds(pl.multiple_of((1 - y) * size, size), size)
    return keep, send


def put_chunks(ids_ref, tmp, full, rel, size, keep_buf, send_buf, at):
    keep, send = halves(ids_ref, size)
    rows_ = slice(at, at + full.shape[0])
    tmp[0 : full.shape[0], :] = full
    low, high = rel & 1, rel >> 1
    keep_buf[low, high, rows_, :] = tmp[0 : full.shape[0], keep].astype(BF)
    send_buf[low, high, rows_, :] = tmp[0 : full.shape[0], send].astype(BF)


def put_low(ids_ref, tmp, full, rel, size, buf, at):
    keep, send = halves(ids_ref, size)
    rows_ = slice(at, at + full.shape[0])
    tmp[0 : full.shape[0], :] = full
    low, high = rel & 1, rel >> 1
    buf[low, 0, high, rows_, :] = tmp[0 : full.shape[0], keep].astype(BF)
    buf[low, 1, high, rows_, :] = tmp[0 : full.shape[0], send].astype(BF)


def mlp_grads(ids, left, first, second, sums, mid, ahead):
    count, dim = left.shape
    chunk = dim // 8
    units = first.shape[1]

    def body(ids_ref, ins, outs, scratch):
        first_in, left_in, second_in = ins[:3]
        send1, keep1, send2, keep2, send_sum, total, mid_out = outs
        mid_out.buf[...] = (ins[-2]()[...].astype(F32) + ins[-1]()[...].astype(F32)).astype(BF)
        tmp, buf = scratch
        z = ids_ref[1] >> 1
        for right, low_first in ((first_in, False), (second_in, True)):
            for half in range(2):
                part = left_in()[:, half * 4 * chunk : (half + 1) * 4 * chunk]
                full = tn(right()[...], part)
                for b in range(2):
                    one = full[:, b * 2 * chunk : (b + 1) * 2 * chunk]
                    rel = z ^ (2 * half + b)
                    if low_first:
                        put_low(ids_ref, tmp, one, rel, chunk, buf, 0)
                    else:
                        put_chunks(ids_ref, tmp, one, rel, chunk, keep1.buf, send1.buf, 0)
            if low_first:
                send2.buf[...] = buf[1]
                send2.flush()
                keep2.buf[...] = buf[0]
                keep2.flush()
            else:
                send1.flush()
                keep1.flush()
        for k in range(len(sums)):
            at = slice(k * size, (k + 1) * size)
            both = ins[3 + 2 * k]()[...] + ins[4 + 2 * k]()[...].astype(F32)
            send_sum.buf[at, :] = both[1].astype(BF)
            total.buf[at, :] = both[0]
        send_sum.flush()
        total.flush()

    shape = (2, 2, units, chunk)
    size = sums[0][0].shape[1]
    added = (size * len(sums), chunk)
    return call(
        body,
        ids,
        [(first, 1), (left, 1), (second, 1)] + [(a, 1) for pair in sums for a in pair] + mid,
        [(shape, BF, HOLD), (shape, BF, 1)] * 2
        + [(added, BF, HOLD), (added, F32, 1), (mid[0][0].shape, BF, HOLD)],
        scratch=[
            pltpu.VMEM((units, 2 * chunk), F32),
            pltpu.VMEM((2, 2, 2, units, chunk), BF),
        ],
        name="grads_mlp",
        ahead=ahead,
    )


def attention_grads(ids, left, right, o_pieces, parts, ahead):
    count, dim = left.shape
    chunk = dim // 8
    three = right.shape[1]
    width = three // 3
    two = 2 * width

    def body(ids_ref, ins, outs, scratch):
        right_in, left_in, o_ins, p_ins = ins[0], ins[1], ins[2:6], ins[6:9]
        send1, keep1, send2, keep2 = outs[:4]
        tmp, buf = scratch
        z = ids_ref[1] >> 1
        for half in range(2):
            part = left_in()[:, half * 4 * chunk : (half + 1) * 4 * chunk]
            full = tn(right_in()[...], part)
            for b in range(2):
                cols = slice(b * 2 * chunk, (b + 1) * 2 * chunk)
                rel = z ^ (2 * half + b)
                put_chunks(ids_ref, tmp, full[:two, cols], rel, chunk, keep1.buf, send1.buf, 0)
                put_low(ids_ref, tmp, full[two:, cols], rel, chunk, buf, 0)
        send1.flush()
        keep1.flush()
        total = p_ins[0]()[...].astype(F32)
        for p in p_ins[1:]:
            total = total + p()[...].astype(F32)
        grad = total.astype(BF)
        for flip, o in enumerate(o_ins):
            put_low(ids_ref, tmp, tn(o()[...], grad), z ^ flip, chunk, buf, width)
        send2.buf[...] = buf[1]
        send2.flush()
        keep2.buf[...] = buf[0]
        keep2.flush()
    shape = (2, 2, two, chunk)
    return call(
        body,
        ids,
        [(right, 1), given(left)] + [given(o) for o in o_pieces] + parts,
        [(shape, BF, HOLD), (shape, BF, 1)] * 2,
        scratch=[
            pltpu.VMEM((two, 2 * chunk), F32),
            pltpu.VMEM((2, 2, 2, two, chunk), BF),
        ],
        name="grads_att",
        ahead=ahead,
    )


def down_grads(ids, hidden, near, far):
    count, units = hidden.shape
    two = near.shape[1]
    width = two // 2
    chunk = width // 2
    half = units // 2

    def body(ids_ref, ins, outs, scratch):
        h_in, a_in, b_in = ins
        send1, keep1, send2, keep2 = outs
        tmp, buf = scratch
        for low, ref in ((0, a_in), (1, b_in)):
            full = tn(h_in()[...], ref()[...])
            for high in range(2):
                one = full[:, high * width : (high + 1) * width]
                rel = ids_ref[0] ^ (ids_ref[1] >> 1) ^ (low + 2 * high)
                put_chunks(ids_ref, tmp, one[:half], rel, chunk, keep1.buf, send1.buf, 0)
                put_low(ids_ref, tmp, one[half:], rel, chunk, buf, 0)
        send1.flush()
        keep1.flush()
        send2.buf[...] = buf[1]
        send2.flush()
        keep2.buf[...] = buf[0]
        keep2.flush()

    shape = (2, 2, half, chunk)
    return call(
        body,
        ids,
        [given(hidden), given(near), given(far)],
        [(shape, BF, HOLD), (shape, BF, 1)] * 2,
        scratch=[pltpu.VMEM((half, width), F32), pltpu.VMEM((2, 2, 2, half, chunk), BF)],
        name="grads_down",
    )


def add_pairs(ids, sums, name, ahead):
    def body(ids_ref, ins, outs, scratch):
        for k in range(len(sums)):
            add_halves(ins[2 * k](), ins[2 * k + 1](), outs[2 * k], outs[2 * k + 1])

    outs, ins = [], []
    for keep, got in sums:
        outs += [(keep.shape[1:], BF, HOLD), (keep.shape[1:], F32, 1)]
        ins += [(keep, 1), given(got)]
    return call(body, ids, ins, outs, name=name, ahead=ahead)


def flip_dp(value, bit):
    n = lax.axis_size("dp")
    return lax.ppermute(value, "dp", [(d, d ^ bit) for d in range(n)])


def flip_tensor(value, bit):
    return lax.ppermute(value, "tensor", [(d, d ^ bit) for d in range(4)])


def tie(values, *others):
    return lax.optimization_barrier((values, others))[0]


def gather_pieces(own, *others):
    two = flip_tensor(own, 2)
    one = flip_tensor(own, 1)
    three = flip_tensor(tie(two, *others) if others else two, 1)
    return (own, one, two, three)


def middle(keep2, got):
    return (keep2.astype(F32) + got[1].astype(F32)).astype(BF)


def pack_grads(ids, slot_row, parts, others, last, n_dp):
    count, width = last.shape
    per = count // n_dp
    k, m = len(parts), len(others)

    def body(ids_ref, ins, outs, scratch):
        (out,) = outs
        total = ins[k + 1]()[...].astype(F32)
        for r in ins[k + 2 : k + m + 1]:
            total = total + r()[...].astype(F32)
        gain = ins[1]()[count:, :].astype(F32)
        total = total + ins[1]()[0:count, :].astype(F32)
        for r in ins[2 : k + 1]:
            total = total + r()[0:count, :].astype(F32)
            gain = gain + r()[count:, :].astype(F32)
        gain = jnp.concatenate([gain.astype(BF)] * 2, axis=1)
        both = jnp.concatenate([total.astype(BF), ins[-1]()[...]], axis=1)
        packed = tn(picks(ins[0]()[...], 0, count), both).astype(BF)
        for d in range(n_dp):
            out.buf[d, 0:per, :] = packed[d * per : (d + 1) * per, :]
            out.buf[d, per:, :] = gain
        out.flush()

    return call(
        body,
        ids,
        [(slot_row, 1)] + parts + others + [given(last)],
        [((n_dp, per + EXTRA, 2 * width), BF, HOLD)],
        name="pack_grads",
    )[0]


def unpack_grads(ids, pos8, back):
    n_dp, padded, two = back.shape
    width = two // 2
    part = width // n_dp
    per = padded - EXTRA
    count = n_dp * per

    def body(ids_ref, ins, outs, scratch):
        a_out, b_out, gain_out = outs
        picked = picks(ins[0]()[0:1, :], 0, count)
        ref = ins[1]()
        both = tn(picked, ref[:, 0:per, :].reshape(count, two)).astype(BF)
        a_out.buf[...] = both[:, :width]
        a_out.flush()
        b_out.buf[...] = both[:, width:]
        b_out.flush()
        total = ref[0, per:, 0:width].astype(F32)
        for d in range(1, n_dp):
            total = total + ref[d, per:, 0:width].astype(F32)
        own = iota((width, part), 1) + ids_ref[1] * part
        pick = jnp.where(iota((width, part), 0) == own, 1.0, 0.0)
        gain_out.buf[...] = lax.dot_general(
            total, pick, (((1,), (0,)), ((), ())),
            precision=lax.Precision.HIGHEST, preferred_element_type=F32,
        )
        gain_out.flush()

    return call(
        body,
        ids,
        [(pos8, 1), given(back)],
        [((count, width), BF, 1), ((count, width), BF, 1), ((EXTRA, part), F32, 1)],
        name="unpack_grads",
    )


def finish_attention(ids, qk_total, vo_total, got, outs_got):
    two, chunk = qk_total.shape[1:]
    width = two // 2

    def body(ids_ref, ins, outs, scratch):
        q_out, k_out, v_out, o_out = outs
        qk, vo, add = ins[0](), ins[1](), ins[2]()
        o_out.buf[...] = ins[3]()[...].astype(F32) + ins[4]()[...].astype(F32)
        o_out.flush()
        for out, ref, at, off in ((q_out, qk, 0, 0), (k_out, qk, width, 0), (v_out, vo, 0, two)):
            total = ref[at : at + width, :] + add[off + at : off + at + width, :].astype(F32)
            out.buf[...] = jnp.transpose(total)
            out.flush()

    return call(
        body,
        ids,
        [(qk_total, 1, 0), (vo_total, 1, 0), given(got)] + [given(o) for o in outs_got],
        [((chunk, width), F32, 1)] * 3 + [((width, chunk), F32, 1)],
        name="finish_attention",
    )


def per_device(
    tokens,
    dealing,
    seq_ids,
    first_values,
    out_grad,
    norm1_gain,
    norm2_gain,
    w_query,
    w_key,
    w_value,
    w_out,
    w_gate,
    w_up,
    w_down,
):
    n_dp = lax.axis_size("dp")
    count, width = tokens.shape
    dim = norm1_gain.shape[0]
    per = count // n_dp
    t = lax.axis_index("tensor")
    d = lax.axis_index("dp")
    ids = jnp.stack([t, d]).astype(jnp.int32)
    gate_t, up_t = w_gate.T, w_up.T

    def exchange(packed):
        return lax.all_to_all(packed, "dp", split_axis=0, concat_axis=0, tiled=True)

    deal_row = dealing.reshape(1, count)
    sent, pos8 = pack_tokens(ids, deal_row, tokens, n_dp)
    arrived = exchange(sent)
    grad_far = flip_tensor(tie(out_grad, sent), 2)
    pos8 = tie(pos8, sent)
    (first_sent,) = sort_rows(ids, pos8, [(first_values, 1)], "pack_rows")
    first_sent = first_sent.reshape(n_dp, per, width)

    start = jnp.sum(seq_ids[None, :] < seq_ids[:, None], axis=1, dtype=jnp.int32)
    offset = (jnp.arange(count, dtype=jnp.int32) - start).astype(F32)
    half = HEAD_DIM // 2
    freqs = THETA ** (-jnp.arange(half, dtype=F32) / half)
    angles = offset[:, None] * jnp.tile(freqs, width // HEAD_DIM)[None, :]
    cos = jnp.cos(angles)
    sin = jnp.sin(angles)
    start_row = start.reshape(1, count)
    gain1 = norm1_gain.reshape(1, dim)
    gain2 = norm2_gain.reshape(1, dim)

    arrived = tie(arrived, first_sent, cos, sin, start_row, grad_far, gain1, gain2)
    slots = (
        arrived[:, per, :per].astype(F32) * 32.0 + arrived[:, per + 1, :per].astype(F32)
    ).astype(jnp.int32)
    slot_row = slots.reshape(1, count)
    grad_near = tie(out_grad, slot_row)
    (grad_sent,) = sort_rows(ids, pos8, [(grad_near, 1), given(grad_far)], "pack_rows")
    grad_sent = grad_sent.reshape(n_dp, per, 2 * width)
    pieces = gather_pieces(arrived, grad_sent)
    firsts = exchange(tie(first_sent, pieces[1]))
    near = exchange(tie(grad_sent, firsts, pieces[2]))
    w_pieces = gather_pieces(tie(w_out, pieces[2]))

    x, normed1, qkv, attended, lse, w_qkv = qkv_attention(
        ids, tie(slot_row, grad_sent), pieces, firsts, cos, sin, gain1, w_query, w_key, w_value,
        start_row,
    )
    near = tie(near, attended).reshape(count, 2 * width)
    near, *early = sort_rows(
        ids, slot_row, [given(near)], "sort_rows", ahead=(gate_t, up_t, w_down, x)
    )
    far = flip_tensor(near, 1)
    o_pieces = gather_pieces(attended, near)
    x1, normed2, fg, fu, hidden, yk0, yk2, ysend = feed_forward(
        ids, early[3], o_pieces, w_pieces, gain2, *early[:3]
    )
    fast = n_dp == 8
    y_got = flip_tensor(ysend, 1)
    early, sums = (), []
    if fast:
        da_send, da_keep, db_send, db_keep = down_grads(ids, hidden, near, far)
        early = (flip_dp(da_send, 1), flip_dp(db_send, 2))
        sums = [(da_keep, early[0]), (db_keep, early[1])]
        yk2 = tie(yk2, da_keep)
    y_mid = middle(yk2, y_got)
    y_far = flip_tensor(y_mid, 2)
    dgate, dup, ak0, ak2, asend, dk0, dk2, dsend, gg2 = feed_backward(
        ids, tie(x1, y_mid), near, far, fg, fu, w_pieces, gain2, gate_t, up_t, w_down
    )
    a_got = flip_tensor(tie(asend, y_far, *early), 1)
    y_sent, *down_sums = return_rows(
        ids,
        slot_row,
        [(tie(yk0, ak0), 1), (y_got, 1, 0), (y_far, 1)],
        "return_rows",
        sums,
    )
    a_mid = middle(tie(ak2, y_sent), a_got)
    a_far = flip_tensor(a_mid, 2)
    y_back = exchange(tie(y_sent, a_mid).reshape(n_dp, per, width)).reshape(count, width)
    d_got = flip_tensor(tie(dsend, a_mid), 1)
    early = ()
    held = (qkv, attended, cos, sin, w_qkv, x)
    if fast:
        da_send, da_total, db_send, db_total = down_sums
        da_got = flip_dp(tie(da_send, a_mid), 2)
        db_got = flip_dp(tie(db_send, a_mid), 1)
        dgate, dup = tie((dgate, dup), a_mid)
        gate_send, gate_keep, up_send, up_keep, down_send, down_sum, d_mid, *held = mlp_grads(
            ids, normed2, dgate, dup, [(da_total, da_got), (db_total, db_got)],
            [given(dk2), given(d_got, 1)], held,
        )
        a_far = tie(a_far, gate_keep)
        gate_got = flip_dp(gate_send, 1)
        up_got = flip_dp(up_send, 2)
        down_got = flip_dp(down_send, 4)
        early = (gate_got, up_got, down_got)
    else:
        d_mid = middle(dk2, d_got)
    a_far = tie(a_far, d_mid)
    d_far = flip_tensor(tie(d_mid, a_far), 2)
    dvp, dqkv, ek0, ek2, esend = attention_backward(
        ids, *held[:2], lse, [(ak0, 1), given(a_got, 0), (a_far, 1)], start_row, *held[2:4],
        held[5], gain1, held[4], gg2,
    )
    e_got = flip_tensor(tie(esend, d_far, y_back, *early), 1)
    if fast:
        gate_send, gate_total, up_send, up_total, *held = add_pairs(
            ids, [(tie(gate_keep, ek2), gate_got), (up_keep, up_got)], "add_pairs",
            (normed1, *o_pieces, dk0, d_far),
        )
        ek2 = tie(ek2, gate_send)
    e_mid = middle(ek2, e_got)
    e_far = flip_tensor(e_mid, 2)
    if fast:
        gate_got = flip_dp(tie(gate_send, e_mid), 2)
        up_got = flip_dp(tie(up_send, e_mid), 1)
        qk_send, qk_keep, vo_send, vo_keep, *held = attention_grads(
            ids, held[0], tie(dqkv, e_mid), held[1:5],
            [given(held[5]), (d_got, 1, 0), given(held[6])], (ek0, dvp, dk0, d_far),
        )
        ek0, dvp, dk0, d_far = held
        qk_got = flip_dp(qk_send, 1)
        vo_got = flip_dp(vo_send, 2)

        def plus(keep, got, *after):
            return keep.astype(F32) + tie(got, *after).astype(F32)

        gate_total = plus(gate_total, gate_got, qk_keep)
        up_total = plus(up_total, up_got, qk_keep)
        mlp_send = jnp.concatenate([gate_total[1], up_total[1]], axis=0).astype(BF)
        mlp_keep = jnp.concatenate([gate_total[0], up_total[0]], axis=0)
        e_far = tie(e_far, mlp_send)
        mlp_got = flip_dp(mlp_send, 4)
    i_sent = pack_grads(
        ids, slot_row, [given(ek0), (e_got, 1, 0), given(e_far)],
        [given(dk0), (d_got, 1, 0), given(d_far)], dvp, n_dp,
    )
    i_back = exchange(i_sent)
    (output,) = restore_rows(ids, pos8, [tie(y_back, i_sent)], "restore_rows")
    input_grad, first_grad, gain_rows = unpack_grads(ids, pos8, i_back)
    if fast:
        units = w_down.shape[0]
        mlp_total = plus(mlp_keep, mlp_got, output)
        qk_total = plus(qk_keep, qk_got, output)
        vo_total = plus(vo_keep, vo_got, output)
        qk_total = plus(qk_total[0], flip_dp(qk_total[1].astype(BF), 2))
        vo_total = plus(vo_total[0], flip_dp(vo_total[1].astype(BF), 1))
        vo_low = vo_total[:, width:].astype(BF)
        outs_got = [
            lax.ppermute(
                vo_low[b],
                ("dp", "tensor"),
                [
                    ((2 * z + y) * 4 + r, (2 * r + y) * 4 + (r ^ z ^ (2 * b)))
                    for z in range(4)
                    for y in range(2)
                    for r in range(4)
                ],
            )
            for b in range(2)
        ]
        att_send = jnp.concatenate([qk_total[1], vo_total[1, :width]], axis=0).astype(BF)
        att_got = flip_dp(att_send, 4)
        gw_q, gw_k, gw_v, gw_out = finish_attention(
            ids, qk_total, vo_total, tie(att_got, input_grad), outs_got
        )
        gw_down = plus(down_sum, down_got, i_sent)
        gw_gate, gw_up = mlp_total[:units].T, mlp_total[units:].T
    else:

        def scattered(left, right, dim_):
            full = jnp.einsum("ta,tb->ab", left, right, preferred_element_type=F32)
            return lax.psum_scatter(full, "dp", scatter_dimension=dim_, tiled=True)

        def natural(parts):
            full = jnp.zeros((count, dim), BF)
            for flip, part in enumerate(parts):
                full = lax.dynamic_update_slice(full, part, (0, (t ^ flip) * width))
            return full

        dy = natural((near[:, :width], far[:, :width], near[:, width:], far[:, width:]))
        dx1 = (dk0 + d_got[0].astype(F32) + d_far.astype(F32)).astype(BF)
        dx1 = lax.all_gather(dx1, "tensor", axis=1, tiled=True)
        gw_gate = scattered(normed2, dgate, 0)
        gw_up = scattered(normed2, dup, 0)
        gw_down = scattered(hidden, dy, 1)
        gw_q, gw_k, gw_v = [scattered(normed1, p, 0) for p in jnp.split(dqkv, 3, axis=1)]
        gw_out = scattered(attended, dx1, 1)

    return (
        output,
        input_grad,
        first_grad,
        gain_rows[0:1],
        gain_rows[1:2],
        gw_q,
        gw_k,
        gw_v,
        gw_out,
        gw_gate,
        gw_up,
        gw_down,
    )


def solution(mesh):
    in_specs = (
        P("dp", "tensor"),
        P("dp"),
        P("dp"),
        P("dp", "tensor"),
        P("dp", "tensor"),
        P(),
        P(),
        P(None, "tensor"),
        P(None, "tensor"),
        P(None, "tensor"),
        P("tensor", None),
        P(None, "tensor"),
        P(None, "tensor"),
        P("tensor", None),
    )
    out_specs = (
        P("dp", "tensor"),
        P("dp", "tensor"),
        P("dp", "tensor"),
        P("tensor", "dp"),
        P("tensor", "dp"),
        P("dp", "tensor"),
        P("dp", "tensor"),
        P("dp", "tensor"),
        P("tensor", "dp"),
        P("dp", "tensor"),
        P("dp", "tensor"),
        P("tensor", "dp"),
    )
    return jax.shard_map(
        per_device, mesh=mesh, in_specs=in_specs, out_specs=out_specs, check_vma=False
    )
```

```python
import functools

import jax
import jax.numpy as jnp
from jax import lax
from jax.experimental import pallas as pl
from jax.experimental.pallas import tpu as pltpu
from jax.sharding import PartitionSpec as P

HEAD_DIM = 64
EPS = 1e-06
THETA = 10000.0
NEG = -1e30
BF = jnp.bfloat16
F32 = jnp.float32
BLK = 256
EXTRA = 8
MIB = 1 << 20


def nn(a, b):
    return lax.dot_general(a, b, (((1,), (0,)), ((), ())), preferred_element_type=F32)


def nt(a, b):
    return lax.dot_general(a, b, (((1,), (1,)), ((), ())), preferred_element_type=F32)


def tn(a, b):
    return lax.dot_general(a, b, (((0,), (0,)), ((), ())), preferred_element_type=F32)


def iota(shape, dim):
    return lax.broadcasted_iota(jnp.int32, shape, dim)


TIMES = {
    "pack_tokens": 3,
    "pack_rows": 3,
    "qkv_attention": 14,
    "feed_forward": 12,
    "sort_rows": 3,
    "grads_down": 5,
    "feed_backward": 15,
    "grads_mlp": 8,
    "return_rows": 3,
    "attention_backward": 17,
    "grads_att": 8,
    "pack_grads": 4,
    "unpack_grads": 4,
    "restore_rows": 3,
    "add_pairs": 3,
    "finish_attention": 2,
}


SCALE_F = 1_150_000_000 // 16
SCALE_B = 3_690_000 // 16


class Fetched:
    def __init__(self, src, buf, sems, base, parts):
        self.buf = buf
        size = src.shape[0] // parts if parts else 0
        self.copies = [
            pltpu.make_async_copy(
                src.at[pl.ds(p * size, size)], buf.at[pl.ds(p * size, size)], sems.at[base + p]
            )
            for p in range(parts)
        ]
        self.waited = [False] * parts

    def __call__(self, part=None):
        one = part is not None and len(self.copies) > 1
        for p in (part,) if one else range(len(self.copies)):
            if not self.waited[p]:
                self.copies[p].wait()
                self.waited[p] = True
        return self.buf


class Stored:
    def __init__(self, dst, buf, sems, base):
        self.dst, self.buf, self.sems, self.at = dst, buf, sems, base
        self.copies = []

    def flush(self, *index):
        if self.sems is None:
            return
        src = self.buf.at[index] if index else self.buf
        dst = self.dst.at[index] if index else self.dst
        c = pltpu.make_async_copy(src, dst, self.sems.at[self.at + len(self.copies)])
        c.start()
        self.copies.append(c)


def call(body, ids, ins, outs, scratch=(), mib=28, name=None, ahead=()):
    ins = [tuple(i) + (None,)[len(i) - 2 :] for i in ins]
    took = TIMES[name]
    n_in, n_out = len(ins), len(outs)
    in_at = [sum(i[1] for i in ins[:k]) for k in range(n_in + 1)]
    out_at = [sum(o[2] for o in outs[:k]) for k in range(n_out + 1)]
    stored = [k for k in range(n_out) if outs[k][2] != HOLD]
    fetched = [k for k in range(n_in) if ins[k][1] != HOLD]
    n_ahead = len(ahead)

    def kernel(ids_ref, *refs):
        srcs, refs = refs[:n_in], refs[n_in:]
        early, refs = refs[:n_ahead], refs[n_ahead:]
        dsts, refs = refs[:n_out], refs[n_out:]
        late, refs = refs[:n_ahead], refs[n_ahead:]
        bufs, refs = refs[: len(fetched)], refs[len(fetched) :]
        obufs, refs = refs[: len(stored)], refs[len(stored) :]
        in_sems, out_sems, refs = refs[0], refs[1], refs[2:]
        srcs = [src if i[2] is None else src.at[i[2]] for src, i in zip(srcs, ins)]
        inputs = [Fetched(None, src, None, 0, 0) for src in srcs]
        for k, buf in zip(fetched, bufs):
            inputs[k] = Fetched(srcs[k], buf, in_sems, in_at[k], ins[k][1])
        outputs = [Stored(None, dst, None, 0) for dst in dsts]
        for k, buf in zip(stored, obufs):
            outputs[k] = Stored(dsts[k], buf, out_sems, out_at[k])
        for p in range(max(i[1] for i in ins)):
            for i in inputs:
                if p < len(i.copies):
                    i.copies[p].start()
        copies = [
            pltpu.make_async_copy(a, b, in_sems.at[in_at[-1] + k])
            for k, (a, b) in enumerate(zip(early, late))
        ]
        for c in copies:
            c.start()
        body(ids_ref, inputs, outputs, refs)
        for i in inputs:
            i()
        for k in stored:
            assert len(outputs[k].copies) == outs[k][2]
            for c in outputs[k].copies:
                c.wait()
        for c in copies:
            c.wait()

    return pl.pallas_call(
        kernel,
        out_shape=tuple(
            (pltpu.HBM if k in stored else pltpu.VMEM)(s, d) for k, (s, d, _) in enumerate(outs)
        )
        + tuple(pltpu.VMEM(a.shape, a.dtype) for a in ahead),
        in_specs=[pl.BlockSpec(memory_space=pltpu.SMEM)]
        + [
            pl.BlockSpec(memory_space=pl.ANY if k in fetched else pltpu.VMEM) for k in range(n_in)
        ]
        + [pl.BlockSpec(memory_space=pl.ANY)] * n_ahead,
        out_specs=tuple(
            pl.BlockSpec(memory_space=pl.ANY if k in stored else pltpu.VMEM) for k in range(n_out)
        )
        + tuple(pl.BlockSpec(memory_space=pltpu.VMEM) for _ in ahead),
        scratch_shapes=[
            pltpu.VMEM(a.shape if index is None else a.shape[1:], a.dtype)
            for a, _, index in (ins[k] for k in fetched)
        ]
        + [pltpu.VMEM(outs[k][0], outs[k][1]) for k in stored]
        + [
            pltpu.SemaphoreType.DMA((max(in_at[-1] + n_ahead, 1),)),
            pltpu.SemaphoreType.DMA((max(out_at[-1], 1),)),
        ]
        + list(scratch),
        compiler_params=pltpu.CompilerParams(vmem_limit_bytes=mib * MIB),
        cost_estimate=pl.CostEstimate(
            flops=took * SCALE_F, transcendentals=0, bytes_accessed=took * SCALE_B
        ),
        name=name,
    )(
        ids,
        *[
            pltpu.with_memory_space_constraint(a, pltpu.VMEM if parts == HOLD else pltpu.HBM)
            for a, parts, _ in ins
        ],
        *[pltpu.with_memory_space_constraint(a, pltpu.HBM) for a in ahead],
    )


HOLD = 0


def given(array, index=None):
    return (array, HOLD, index)


def own_first(pieces, parts=1):
    return [(pieces[0], parts)] + [given(p) for p in pieces[1:]]


def piece(ids_ref, flip, width):
    return pl.ds(pl.multiple_of((ids_ref[0] ^ flip) * width, width), width)


def picks(index, first, size):
    shape = (size, index.shape[1])
    return jnp.where(iota(shape, 0) + first == index, 1.0, 0.0).astype(BF)


def pack_tokens(ids, deal_row, tok, n_dp):
    count, width = tok.shape
    per = count // n_dp
    lanes = 128

    def body(ids_ref, ins, outs, scratch):
        deal_in, tok_in = ins
        out, pos_out = outs
        deal = deal_in()[...]
        dest = deal // count
        slot = deal % count
        oh = jnp.where(iota((n_dp, count), 0) == dest, 1.0, 0.0)
        upto = jnp.where(iota((lanes, lanes), 0) <= iota((lanes, lanes), 1), 1.0, 0.0)
        parts = [oh[:, b * lanes : (b + 1) * lanes] for b in range(count // lanes)]
        inner = nn(jnp.concatenate(parts, axis=0).astype(BF), upto.astype(BF))
        base = (iota((n_dp, 1), 0) * per - 1).astype(F32)
        rows_ = []
        for b, part in enumerate(parts):
            seen = inner[b * n_dp : (b + 1) * n_dp]
            rows_.append(jnp.sum(part * (seen + base), axis=0, keepdims=True))
            base = base + seen[:, lanes - 1 :]
        pos = jnp.concatenate(rows_, axis=1).astype(jnp.int32)
        pos_out.buf[...] = jnp.broadcast_to(pos, (8, count))
        pos_out.flush()
        high = jnp.broadcast_to(slot // 32, (8, count))
        low = jnp.broadcast_to(slot % 32, (8, count))
        hl = jnp.where(iota((8, count), 0) == 0, high, low).astype(F32).astype(BF)
        out.buf[:, per : per + EXTRA, :] = jnp.zeros((n_dp, EXTRA, width), BF)
        size = min(count, 512)
        group = size // per
        for g in range(count // size):
            pick = picks(pos, g * size, size)
            moved = nn(pick, tok_in()[...]).astype(BF)
            marks = nt(hl, pick).astype(BF)
            for e in range(group):
                d = g * group + e
                out.buf[d, 0:per, :] = moved[e * per : (e + 1) * per]
                out.buf[d, per : per + 8, 0:per] = marks[:, e * per : (e + 1) * per]
            out.flush(pl.ds(g * group, group))

    return call(
        body,
        ids,
        [(deal_row, 1), (tok, 1)],
        [
            ((n_dp, per + EXTRA, width), BF, HOLD),
            ((8, count), jnp.int32, 1),
        ],
        name="pack_tokens",
    )


def sort_rows(ids, index, parts, name, ahead=()):
    count, width = parts[0][0].shape
    blocks = 2
    size = count // blocks

    def body(ids_ref, ins, outs, scratch):
        idx = ins[0]()[0:1, :]
        (out,) = outs
        for b in range(blocks):
            at = slice(b * size, (b + 1) * size)
            pick = picks(idx, b * size, size)
            for k, part in enumerate(ins[1:]):
                out.buf[at, k * width : (k + 1) * width] = nn(pick, part()[...]).astype(BF)
            out.flush(pl.ds(b * size, size))

    return call(
        body,
        ids,
        [(index, 1)] + parts,
        [((count, width * len(parts)), BF, HOLD)],
        name=name,
        ahead=ahead,
    )


def add_halves(keep, got, send_out, total_out):
    sums = keep[...].astype(F32) + got[...].astype(F32)
    send_out.buf[...] = sums[1].astype(BF)
    send_out.flush()
    total_out.buf[...] = sums[0]
    total_out.flush()


def return_rows(ids, index, parts, name, sums=()):
    count, width = parts[0][0].shape[-2:]
    m = 1 + len(parts)

    def body(ids_ref, ins, outs, scratch):
        total = ins[1]()[...]
        for r in ins[2:m]:
            total = total.astype(F32) + r()[...].astype(F32)
        outs[0].buf[...] = tn(picks(ins[0]()[0:1, :], 0, count), total.astype(BF)).astype(BF)
        outs[0].flush()
        for k in range(len(sums)):
            at = m + 2 * k
            add_halves(ins[at](), ins[at + 1](), outs[1 + 2 * k], outs[2 + 2 * k])

    outs = [((count, width), BF, HOLD)]
    ins = [(index, 1)] + parts
    for keep, got in sums:
        outs += [(keep.shape[1:], BF, HOLD), (keep.shape[1:], F32, 1)]
        ins += [(keep, 1), given(got)]
    return call(body, ids, ins, outs, name=name)


def restore_rows(ids, index, backs, name):
    count, width = backs[0].shape

    def body(ids_ref, ins, outs, scratch):
        pick = picks(ins[0]()[0:1, :], 0, count)
        both = tn(pick, jnp.concatenate([b()[...] for b in ins[1:]], axis=1)).astype(BF)
        for k, out in enumerate(outs):
            out.buf[...] = both[:, k * width : (k + 1) * width]
            out.flush()

    return call(
        body,
        ids,
        [(index, 1)] + [(b, 1) for b in backs],
        [((count, width), BF, 1)] * len(backs),
        name=name,
    )


def head_mask(shape, head, split):
    lane = iota(shape, 1)
    if split:
        return (lane % (shape[1] // 2)) // (HEAD_DIM // 2) == head
    return lane // HEAD_DIM == head


def split_perm(width):
    half = HEAD_DIM // 2
    src = iota((width, width), 0)
    dst = iota((width, width), 1)
    second = dst // (width // 2)
    rest = dst % (width // 2)
    want = (rest // half) * HEAD_DIM + second * half + rest % half
    return (src == want).astype(F32).astype(BF)


def qkv_attention(ids, slot_row, pieces, firsts, cos, sin, gain, wq, wk, wv, start_row):
    n_dp, padded, width = pieces[0].shape
    per = firsts.shape[1]
    count = n_dp * per
    dim = gain.shape[1]
    heads = width // HEAD_DIM
    blocks = count // BLK
    half = width // 2

    def body(ids_ref, ins, outs, scratch):
        slot_in, x0, x1, x2, x3, fv_in, wq_in, wk_in, wv_in, cos_in, sin_in, gain_in, start_in = ins
        x_out, n_out, qkv_out, o_out, lse_out, w_out = outs
        cat, vt = scratch
        slots = slot_in()[...]
        for flip, ref in enumerate((x0, x1, x2, x3)):
            cat[:, piece(ids_ref, flip, width)] = ref()[:, 0:per, :].reshape(count, width)
        cat[:, dim:] = fv_in()[...].reshape(count, width)
        sp = split_perm(width)
        w_out.buf[:, 0:width] = nn(wq_in()[...], sp).astype(BF)
        w_out.buf[:, width : 2 * width] = nn(wk_in()[...], sp).astype(BF)
        w_out.buf[:, 2 * width :] = wv_in()[...]
        w_out.flush()
        lse_out.buf[...] = jnp.zeros_like(lse_out.buf)

        def rope(v, c, s):
            a, b = v[:, :half], v[:, half:]
            return jnp.concatenate([a * c - b * s, b * c + a * s], axis=1).astype(BF)

        for j in range(blocks):
            at = slice(j * BLK, (j + 1) * BLK)
            ds = pl.ds(j * BLK, BLK)
            moved = nn(picks(slots, j * BLK, BLK), cat[...])
            x = moved[:, :dim]
            x_out.buf[at, :] = x.astype(BF)
            x_out.flush(ds)
            scale = lax.rsqrt(jnp.sum(x * x, axis=1, keepdims=True) / dim + EPS)
            normed = (x * scale * gain_in()[...].astype(F32)).astype(BF)
            n_out.buf[at, :] = normed
            n_out.flush(ds)
            qkv = nn(normed, w_out.buf[...])
            c, s = cos_in(j)[at, :], sin_in(j)[at, :]
            q = rope(qkv[:, 0:width], c, s)
            v = 0.5 * qkv[:, 2 * width :] + 0.5 * moved[:, dim:]
            q = (q.astype(F32) * HEAD_DIM ** (-0.5)).astype(BF)
            qkv_out.buf[at, 0:width] = q
            qkv_out.buf[at, width : 2 * width] = rope(qkv[:, width : 2 * width], c, s)
            qkv_out.buf[at, 2 * width :] = v.astype(BF)
            qkv_out.flush(ds)
            vt[:, at] = jnp.transpose(v).astype(BF)
            start = start_in()[:, at]
            n = (j + 1) * BLK
            keys = qkv_out.buf[0:n, width : 2 * width]
            key = iota((n, BLK), 0)
            valid = (key >= start) & (key <= iota((n, BLK), 1) + j * BLK)
            out = []
            for h in range(heads):
                qh = jnp.where(head_mask((BLK, width), h, True), q, jnp.zeros_like(q))
                sc = jnp.where(valid, nt(keys, qh), NEG)
                top = jnp.max(sc, axis=0, keepdims=True)
                ex = jnp.exp(sc - top)
                total = jnp.sum(ex, axis=0, keepdims=True)
                vals = vt[h * HEAD_DIM : (h + 1) * HEAD_DIM, 0:n]
                out.append(nn(vals, ex.astype(BF)) * (1.0 / total))
                lse_out.buf[h : h + 1, at] = top + jnp.log(total)
            o_out.buf[at, :] = jnp.transpose(jnp.concatenate(out, axis=0)).astype(BF)
            o_out.flush(ds)
        lse_out.flush()

    return call(
        body,
        ids,
        [(slot_row, 1)]
        + [given(p) for p in pieces]
        + [given(firsts)]
        + [(wq, 1), (wk, 1), (wv, 1), (cos, 1), (sin, 1), (gain, 1), (start_row, 1)],
        [
            ((count, dim), BF, blocks),
            ((count, dim), BF, blocks),
            ((count, 3 * width), BF, blocks),
            ((count, width), BF, HOLD),
            ((8, count), F32, 1),
            ((dim, 3 * width), BF, 1),
        ],
        scratch=[pltpu.VMEM((count, dim + width), BF), pltpu.VMEM((width, count), BF)],
        name="qkv_attention",
    )


FEED = 512


def feed_forward(ids, x, o_pieces, w_pieces, gain, w_gate, w_up, w_down):
    count, dim = x.shape
    width = o_pieces[0].shape[1]
    units = w_gate.shape[0]
    size = min(FEED, count)
    blocks = count // size

    def body(ids_ref, ins, outs, scratch):
        w_ins, o_ins = ins[0:4], ins[4:8]
        x_in, gain_in, wg_in, wu_in, wd_in = ins[8:]
        x1_out, n_out, fg_out, fu_out, h_out, yk0, yk2, ysend = outs
        ys, xs, wo = scratch
        for k, w in enumerate(w_ins):
            wo[k * width : (k + 1) * width, :] = w()[...]
        for j in range(blocks):
            at = slice(j * size, (j + 1) * size)
            ds = pl.ds(j * size, size)
            heads = jnp.concatenate([o(j)[at, :] for o in o_ins], axis=1)
            x1 = x_in(j)[at, :].astype(F32) + nn(heads, wo[...])
            xs[...] = x1
            x1_out.buf[at, :] = x1.astype(BF)
            x1_out.flush(ds)
            scale = lax.rsqrt(jnp.sum(x1 * x1, axis=1, keepdims=True) / dim + EPS)
            normed = (x1 * scale * gain_in()[...].astype(F32)).astype(BF)
            n_out.buf[at, :] = normed
            n_out.flush(ds)
            g = nt(normed, wg_in()[...])
            u = nt(normed, wu_in()[...])
            sg = jax.nn.sigmoid(g)
            silu = g * sg
            hid = (silu * u).astype(BF)
            h_out.buf[at, :] = hid
            h_out.flush(ds)
            fu_out.buf[at, :] = silu.astype(BF)
            fu_out.flush(ds)
            fg_out.buf[at, :] = (u * sg * (1.0 + g * (1.0 - sg))).astype(BF)
            fg_out.flush(ds)
            ys[...] = nn(hid, wd_in()[...])
            ysend.buf[0, at, :] = ys[:, piece(ids_ref, 1, width)].astype(BF)
            ysend.buf[1, at, :] = ys[:, piece(ids_ref, 3, width)].astype(BF)
            ysend.flush(slice(None), ds)
            own = piece(ids_ref, 0, width)
            yk0.buf[at, :] = (ys[:, own] + xs[:, own]).astype(BF)
            yk0.flush(ds)
            yk2.buf[at, :] = ys[:, piece(ids_ref, 2, width)].astype(BF)
            yk2.flush(ds)

    return call(
        body,
        ids,
        [(w, 1) for w in w_pieces]
        + own_first(o_pieces)
        + [given(x), (gain, 1), given(w_gate), given(w_up), given(w_down)],
        [
            ((count, dim), BF, blocks),
            ((count, dim), BF, blocks),
            ((count, units), BF, blocks),
            ((count, units), BF, blocks),
            ((count, units), BF, HOLD),
            ((count, width), BF, blocks),
            ((count, width), BF, HOLD),
            ((2, count, width), BF, HOLD),
        ],
        scratch=[
            pltpu.VMEM((size, dim), F32),
            pltpu.VMEM((size, dim), F32),
            pltpu.VMEM((4 * width, dim), BF),
        ],
        mib=44,
        name="feed_forward",
    )


def feed_backward(ids, x1, near, far, fg, fu, w_pieces, gain, w_gate, w_up, w_down):
    count, dim = x1.shape
    width = w_pieces[0].shape[0]
    units = w_gate.shape[0]
    size = min(FEED, count)
    blocks = count // size

    def body(ids_ref, ins, outs, scratch):
        wd_in, fg_in, fu_in, wg_in, wu_in, x1_in, near_in, far_in, gain_in = ins[:9]
        w_ins = ins[9:]
        dg_out, du_out, ak0, ak2, asend, dk0, dk2, dsend, gg_out = outs
        ds_, ys, wo = scratch
        sums = jnp.zeros((1, dim), F32)
        for j in range(blocks):
            at = slice(j * size, (j + 1) * size)
            ds = pl.ds(j * size, size)
            near_, far_ = near_in(j)[at, :], far_in(j)[at, :]
            ys[:, piece(ids_ref, 0, width)] = near_[:, :width]
            ys[:, piece(ids_ref, 2, width)] = near_[:, width:]
            ys[:, piece(ids_ref, 1, width)] = far_[:, :width]
            ys[:, piece(ids_ref, 3, width)] = far_[:, width:]
            dy = ys[...]
            dh = nt(dy, wd_in()[...])
            dg = (dh * fg_in(j)[at, :].astype(F32)).astype(BF)
            du = (dh * fu_in(j)[at, :].astype(F32)).astype(BF)
            dg_out.buf[at, :] = dg
            du_out.buf[at, :] = du
            dg_out.flush(ds)
            du_out.flush(ds)
            dn = nn(dg, wg_in()[...]) + nn(du, wu_in()[...])
            x1 = x1_in(j)[at, :].astype(F32)
            scale = lax.rsqrt(jnp.sum(x1 * x1, axis=1, keepdims=True) / dim + EPS)
            sums = sums + jnp.sum(dn * (x1 * scale), axis=0, keepdims=True)
            z = dn * gain_in()[...].astype(F32)
            dot_row = jnp.sum(z * x1, axis=1, keepdims=True)
            part = scale * z - x1 * (scale * scale * scale * dot_row / dim)
            part = part + 0.25 * dy.astype(F32)
            ds_[...] = part
            if j == 0:
                for k, w in enumerate(w_ins):
                    wo[k * width : (k + 1) * width, :] = w()[...]
            da = nt(part.astype(BF), wo[...])
            asend.buf[0, at, :] = da[:, width : 2 * width].astype(BF)
            asend.buf[1, at, :] = da[:, 3 * width :].astype(BF)
            asend.flush(slice(None), ds)
            ak0.buf[at, :] = da[:, 0:width].astype(BF)
            ak0.flush(ds)
            ak2.buf[at, :] = da[:, 2 * width : 3 * width].astype(BF)
            ak2.flush(ds)
            dsend.buf[0, at, :] = ds_[:, piece(ids_ref, 1, width)].astype(BF)
            dsend.buf[1, at, :] = ds_[:, piece(ids_ref, 3, width)].astype(BF)
            dsend.flush(slice(None), ds)
            dk0.buf[at, :] = ds_[:, piece(ids_ref, 0, width)].astype(BF)
            dk0.flush(ds)
            dk2.buf[at, :] = ds_[:, piece(ids_ref, 2, width)].astype(BF)
            dk2.flush(ds)
        gg_out.buf[...] = jnp.broadcast_to(sums, (8, dim))
        gg_out.flush()

    return call(
        body,
        ids,
        [(w_down, 1), (fg, 1), (fu, 1), (w_gate, 1), (w_up, 1), (x1, 1)]
        + [given(near), given(far), (gain, 1)]
        + [(w, 1) for w in w_pieces],
        [
            ((count, units), BF, blocks),
            ((count, units), BF, blocks),
            ((count, width), BF, blocks),
            ((count, width), BF, HOLD),
            ((2, count, width), BF, HOLD),
            ((count, width), BF, blocks),
            ((count, width), BF, HOLD),
            ((2, count, width), BF, HOLD),
            ((8, dim), F32, 1),
        ],
        scratch=[
            pltpu.VMEM((size, dim), F32),
            pltpu.VMEM((size, dim), BF),
            pltpu.VMEM((4 * width, dim), BF),
        ],
        mib=44,
        name="feed_backward",
    )


def attention_backward(
    ids, qkv, o, lse, a_parts, start_row, cos, sin, x, gain, w_qkv, gg2
):
    count, width = o.shape
    dim = x.shape[1]
    heads = width // HEAD_DIM
    blocks = count // BLK
    half = width // 2
    part = HEAD_DIM // 2

    def body(ids_ref, ins, outs, scratch):
        qkv_in, a0, a1, a2, o_in, lse_in, start_in, cos_in, sin_in, w_in, x_in, gain_in, g2_in = ins
        dv_out, dqkv_out, ek0, ek2, esend = outs
        kt, dk, dv, es = scratch
        qkv_ref = qkv_in()
        for b in range(blocks):
            at = slice(b * BLK, (b + 1) * BLK)
            kt[:, at] = jnp.transpose(qkv_ref[at, width : 2 * width].astype(F32)).astype(BF)
        sums = jnp.zeros((1, dim), F32)
        pick = (iota((8, width), 1) // HEAD_DIM == iota((8, width), 0)).astype(F32)
        sp = split_perm(width)

        def rope_back(g, c, s):
            a, b = g[:, :half], g[:, half:]
            return jnp.concatenate([a * c + b * s, b * c - a * s], axis=1).astype(BF)

        for j in reversed(range(blocks)):
            at = slice(j * BLK, (j + 1) * BLK)
            ds = pl.ds(j * BLK, BLK)
            q = qkv_ref[at, 0:width]
            do = (a0(j)[at, :].astype(F32) + a1(j)[at, :].astype(F32) + a2(j)[at, :].astype(F32)).astype(BF)
            prod = do.astype(F32) * o_in(j)[at, :].astype(F32)
            delta = lax.dot_general(
                pick, prod, (((1,), (1,)), ((), ())),
                precision=lax.Precision.HIGHEST, preferred_element_type=F32,
            )
            start = start_in()[:, at]
            lse = lse_in()[:, at]
            n = (j + 1) * BLK
            keys = qkv_ref[0:n, width : 2 * width]
            vals = qkv_ref[0:n, 2 * width :]
            key = iota((n, BLK), 0)
            valid = (key >= start) & (key <= iota((n, BLK), 1) + j * BLK)
            probs, grads, q_heads, do_heads = [], [], [], []
            first, second = [], []
            for h in range(heads):
                qh = jnp.where(head_mask((BLK, width), h, True), q, jnp.zeros_like(q))
                dh = jnp.where(head_mask((BLK, width), h, False), do, jnp.zeros_like(do))
                sc = jnp.where(valid, nt(keys, qh) - lse[h : h + 1, :], NEG)
                pr = jnp.exp(sc)
                dsc = (pr * (nt(vals, dh) - delta[h : h + 1, :])).astype(BF)
                probs.append(pr.astype(BF))
                grads.append(dsc)
                q_heads.append(qh)
                do_heads.append(dh)
                kh = jnp.concatenate(
                    [
                        kt[h * part : (h + 1) * part, 0:n],
                        kt[half + h * part : half + (h + 1) * part, 0:n],
                    ],
                    axis=0,
                )
                dqh = nn(kh, dsc)
                first.append(dqh[:part])
                second.append(dqh[part:])
            dvn = nn(jnp.concatenate(probs, 1), jnp.concatenate(do_heads, 0))
            dkn = nn(jnp.concatenate(grads, 1), jnp.concatenate(q_heads, 0))
            if j == blocks - 1:
                dv[...] = dvn
                dk[...] = dkn
            else:
                dv[0:n, :] += dvn
                dk[0:n, :] += dkn
            dqj = jnp.transpose(jnp.concatenate(first + second, axis=0)) * HEAD_DIM ** (-0.5)
            c, s = cos_in(j)[at, :], sin_in(j)[at, :]
            dqp = rope_back(dqj, c, s)
            dkp = rope_back(dk[at, :], c, s)
            dvp = (0.5 * dv[at, :].astype(BF).astype(F32)).astype(BF)
            dv_out.buf[at, :] = dvp
            dv_out.flush(ds)
            dqkv_out.buf[at, 0:width] = nt(dqp, sp).astype(BF)
            dqkv_out.buf[at, width : 2 * width] = nt(dkp, sp).astype(BF)
            dqkv_out.buf[at, 2 * width :] = dvp
            dqkv_out.flush(ds)
            dn = nt(jnp.concatenate([dqp, dkp, dvp], axis=1), w_in()[...])
            x = x_in(j)[at, :].astype(F32)
            scale = lax.rsqrt(jnp.sum(x * x, axis=1, keepdims=True) / dim + EPS)
            sums = sums + jnp.sum(dn * (x * scale), axis=0, keepdims=True)
            z = dn * gain_in()[...].astype(F32)
            dot_row = jnp.sum(z * x, axis=1, keepdims=True)
            es[...] = scale * z - x * (scale * scale * scale * dot_row / dim)
            esend.buf[0, at, :] = es[:, piece(ids_ref, 1, width)].astype(BF)
            esend.buf[1, at, :] = es[:, piece(ids_ref, 3, width)].astype(BF)
            esend.flush(slice(None), ds)
            ek0.buf[at, :] = es[:, piece(ids_ref, 0, width)].astype(BF)
            ek0.flush(ds)
            ek2.buf[at, :] = es[:, piece(ids_ref, 2, width)].astype(BF)
            ek2.flush(ds)
        last = pl.ds(count, EXTRA)
        es[0:8, :] = jnp.where(iota((8, dim), 0) == 0, sums, g2_in()[...])
        esend.buf[0, count:, :] = es[0:8, piece(ids_ref, 1, width)].astype(BF)
        esend.buf[1, count:, :] = es[0:8, piece(ids_ref, 3, width)].astype(BF)
        esend.flush(slice(None), last)
        ek0.buf[count:, :] = es[0:8, piece(ids_ref, 0, width)].astype(BF)
        ek0.flush(last)
        ek2.buf[count:, :] = es[0:8, piece(ids_ref, 2, width)].astype(BF)
        ek2.flush(last)

    return call(
        body,
        ids,
        [given(qkv)]
        + a_parts
        + [given(o), (lse, 1), (start_row, 1), given(cos), given(sin), given(w_qkv)]
        + [given(x), (gain, 1), (gg2, 1)],
        [
            ((count, width), BF, blocks),
            ((count, 3 * width), BF, blocks),
            ((count + EXTRA, width), BF, blocks + 1),
            ((count + EXTRA, width), BF, HOLD),
            ((2, count + EXTRA, width), BF, blocks + 1),
        ],
        scratch=[
            pltpu.VMEM((width, count), BF),
            pltpu.VMEM((count, width), F32),
            pltpu.VMEM((count, width), F32),
            pltpu.VMEM((BLK, dim), F32),
        ],
        mib=36,
        name="attention_backward",
    )


def halves(ids_ref, size):
    y = ids_ref[1] & 1
    keep = pl.ds(pl.multiple_of(y * size, size), size)
    send = pl.ds(pl.multiple_of((1 - y) * size, size), size)
    return keep, send


def put_chunks(ids_ref, tmp, full, rel, size, keep_buf, send_buf, at):
    keep, send = halves(ids_ref, size)
    rows_ = slice(at, at + full.shape[0])
    tmp[0 : full.shape[0], :] = full
    low, high = rel & 1, rel >> 1
    keep_buf[low, high, rows_, :] = tmp[0 : full.shape[0], keep].astype(BF)
    send_buf[low, high, rows_, :] = tmp[0 : full.shape[0], send].astype(BF)


def put_low(ids_ref, tmp, full, rel, size, buf, at):
    keep, send = halves(ids_ref, size)
    rows_ = slice(at, at + full.shape[0])
    tmp[0 : full.shape[0], :] = full
    low, high = rel & 1, rel >> 1
    buf[low, 0, high, rows_, :] = tmp[0 : full.shape[0], keep].astype(BF)
    buf[low, 1, high, rows_, :] = tmp[0 : full.shape[0], send].astype(BF)


def mlp_grads(ids, left, first, second, sums, mid, ahead):
    count, dim = left.shape
    chunk = dim // 8
    units = first.shape[1]

    def body(ids_ref, ins, outs, scratch):
        first_in, left_in, second_in = ins[:3]
        send1, keep1, send2, keep2, send_sum, total, mid_out = outs
        mid_out.buf[...] = (ins[-2]()[...].astype(F32) + ins[-1]()[...].astype(F32)).astype(BF)
        tmp, buf = scratch
        z = ids_ref[1] >> 1
        for right, low_first in ((first_in, False), (second_in, True)):
            for half in range(2):
                part = left_in()[:, half * 4 * chunk : (half + 1) * 4 * chunk]
                full = tn(right()[...], part)
                for b in range(2):
                    one = full[:, b * 2 * chunk : (b + 1) * 2 * chunk]
                    rel = z ^ (2 * half + b)
                    if low_first:
                        put_low(ids_ref, tmp, one, rel, chunk, buf, 0)
                    else:
                        put_chunks(ids_ref, tmp, one, rel, chunk, keep1.buf, send1.buf, 0)
            if low_first:
                send2.buf[...] = buf[1]
                send2.flush()
                keep2.buf[...] = buf[0]
                keep2.flush()
            else:
                send1.flush()
                keep1.flush()
        for k in range(len(sums)):
            at = slice(k * size, (k + 1) * size)
            both = ins[3 + 2 * k]()[...] + ins[4 + 2 * k]()[...].astype(F32)
            send_sum.buf[at, :] = both[1].astype(BF)
            total.buf[at, :] = both[0]
        send_sum.flush()
        total.flush()

    shape = (2, 2, units, chunk)
    size = sums[0][0].shape[1]
    added = (size * len(sums), chunk)
    return call(
        body,
        ids,
        [(first, 1), (left, 1), (second, 1)] + [(a, 1) for pair in sums for a in pair] + mid,
        [(shape, BF, HOLD), (shape, BF, 1)] * 2
        + [(added, BF, HOLD), (added, F32, 1), (mid[0][0].shape, BF, HOLD)],
        scratch=[
            pltpu.VMEM((units, 2 * chunk), F32),
            pltpu.VMEM((2, 2, 2, units, chunk), BF),
        ],
        name="grads_mlp",
        ahead=ahead,
    )


def attention_grads(ids, left, right, o_pieces, parts, ahead):
    count, dim = left.shape
    chunk = dim // 8
    three = right.shape[1]
    width = three // 3
    two = 2 * width

    def body(ids_ref, ins, outs, scratch):
        right_in, left_in, o_ins, p_ins = ins[0], ins[1], ins[2:6], ins[6:9]
        send1, keep1, send2, keep2 = outs[:4]
        tmp, buf = scratch
        z = ids_ref[1] >> 1
        for half in range(2):
            part = left_in()[:, half * 4 * chunk : (half + 1) * 4 * chunk]
            full = tn(right_in()[...], part)
            for b in range(2):
                cols = slice(b * 2 * chunk, (b + 1) * 2 * chunk)
                rel = z ^ (2 * half + b)
                put_chunks(ids_ref, tmp, full[:two, cols], rel, chunk, keep1.buf, send1.buf, 0)
                put_low(ids_ref, tmp, full[two:, cols], rel, chunk, buf, 0)
        send1.flush()
        keep1.flush()
        total = p_ins[0]()[...].astype(F32)
        for p in p_ins[1:]:
            total = total + p()[...].astype(F32)
        grad = total.astype(BF)
        for flip, o in enumerate(o_ins):
            put_low(ids_ref, tmp, tn(o()[...], grad), z ^ flip, chunk, buf, width)
        send2.buf[...] = buf[1]
        send2.flush()
        keep2.buf[...] = buf[0]
        keep2.flush()
    shape = (2, 2, two, chunk)
    return call(
        body,
        ids,
        [(right, 1), given(left)] + [given(o) for o in o_pieces] + parts,
        [(shape, BF, HOLD), (shape, BF, 1)] * 2,
        scratch=[
            pltpu.VMEM((two, 2 * chunk), F32),
            pltpu.VMEM((2, 2, 2, two, chunk), BF),
        ],
        name="grads_att",
        ahead=ahead,
    )


def down_grads(ids, hidden, near, far):
    count, units = hidden.shape
    two = near.shape[1]
    width = two // 2
    chunk = width // 2
    half = units // 2

    def body(ids_ref, ins, outs, scratch):
        h_in, a_in, b_in = ins
        send1, keep1, send2, keep2 = outs
        tmp, buf = scratch
        for low, ref in ((0, a_in), (1, b_in)):
            full = tn(h_in()[...], ref()[...])
            for high in range(2):
                one = full[:, high * width : (high + 1) * width]
                rel = ids_ref[0] ^ (ids_ref[1] >> 1) ^ (low + 2 * high)
                put_chunks(ids_ref, tmp, one[:half], rel, chunk, keep1.buf, send1.buf, 0)
                put_low(ids_ref, tmp, one[half:], rel, chunk, buf, 0)
        send1.flush()
        keep1.flush()
        send2.buf[...] = buf[1]
        send2.flush()
        keep2.buf[...] = buf[0]
        keep2.flush()

    shape = (2, 2, half, chunk)
    return call(
        body,
        ids,
        [given(hidden), given(near), given(far)],
        [(shape, BF, HOLD), (shape, BF, 1)] * 2,
        scratch=[pltpu.VMEM((half, width), F32), pltpu.VMEM((2, 2, 2, half, chunk), BF)],
        name="grads_down",
    )


def add_pairs(ids, sums, name, ahead):
    def body(ids_ref, ins, outs, scratch):
        for k in range(len(sums)):
            add_halves(ins[2 * k](), ins[2 * k + 1](), outs[2 * k], outs[2 * k + 1])

    outs, ins = [], []
    for keep, got in sums:
        outs += [(keep.shape[1:], BF, HOLD), (keep.shape[1:], F32, 1)]
        ins += [(keep, 1), given(got)]
    return call(body, ids, ins, outs, name=name, ahead=ahead)


def flip_dp(value, bit):
    n = lax.axis_size("dp")
    return lax.ppermute(value, "dp", [(d, d ^ bit) for d in range(n)])


def flip_tensor(value, bit):
    return lax.ppermute(value, "tensor", [(d, d ^ bit) for d in range(4)])


def tie(values, *others):
    return lax.optimization_barrier((values, others))[0]


def gather_pieces(own, *others):
    two = flip_tensor(own, 2)
    one = flip_tensor(own, 1)
    three = flip_tensor(tie(two, *others) if others else two, 1)
    return (own, one, two, three)


def middle(keep2, got):
    return (keep2.astype(F32) + got[1].astype(F32)).astype(BF)


def pack_grads(ids, slot_row, parts, others, last, n_dp):
    count, width = last.shape
    per = count // n_dp
    k, m = len(parts), len(others)

    def body(ids_ref, ins, outs, scratch):
        (out,) = outs
        total = ins[k + 1]()[...].astype(F32)
        for r in ins[k + 2 : k + m + 1]:
            total = total + r()[...].astype(F32)
        gain = ins[1]()[count:, :].astype(F32)
        total = total + ins[1]()[0:count, :].astype(F32)
        for r in ins[2 : k + 1]:
            total = total + r()[0:count, :].astype(F32)
            gain = gain + r()[count:, :].astype(F32)
        gain = jnp.concatenate([gain.astype(BF)] * 2, axis=1)
        both = jnp.concatenate([total.astype(BF), ins[-1]()[...]], axis=1)
        packed = tn(picks(ins[0]()[...], 0, count), both).astype(BF)
        for d in range(n_dp):
            out.buf[d, 0:per, :] = packed[d * per : (d + 1) * per, :]
            out.buf[d, per:, :] = gain
        out.flush()

    return call(
        body,
        ids,
        [(slot_row, 1)] + parts + others + [given(last)],
        [((n_dp, per + EXTRA, 2 * width), BF, HOLD)],
        name="pack_grads",
    )[0]


def unpack_grads(ids, pos8, back):
    n_dp, padded, two = back.shape
    width = two // 2
    part = width // n_dp
    per = padded - EXTRA
    count = n_dp * per

    def body(ids_ref, ins, outs, scratch):
        a_out, b_out, gain_out = outs
        picked = picks(ins[0]()[0:1, :], 0, count)
        ref = ins[1]()
        both = tn(picked, ref[:, 0:per, :].reshape(count, two)).astype(BF)
        a_out.buf[...] = both[:, :width]
        a_out.flush()
        b_out.buf[...] = both[:, width:]
        b_out.flush()
        total = ref[0, per:, 0:width].astype(F32)
        for d in range(1, n_dp):
            total = total + ref[d, per:, 0:width].astype(F32)
        own = iota((width, part), 1) + ids_ref[1] * part
        pick = jnp.where(iota((width, part), 0) == own, 1.0, 0.0)
        gain_out.buf[...] = lax.dot_general(
            total, pick, (((1,), (0,)), ((), ())),
            precision=lax.Precision.HIGHEST, preferred_element_type=F32,
        )
        gain_out.flush()

    return call(
        body,
        ids,
        [(pos8, 1), given(back)],
        [((count, width), BF, 1), ((count, width), BF, 1), ((EXTRA, part), F32, 1)],
        name="unpack_grads",
    )


def finish_attention(ids, qk_total, vo_total, got, outs_got):
    two, chunk = qk_total.shape[1:]
    width = two // 2

    def body(ids_ref, ins, outs, scratch):
        q_out, k_out, v_out, o_out = outs
        qk, vo, add = ins[0](), ins[1](), ins[2]()
        o_out.buf[...] = ins[3]()[...].astype(F32) + ins[4]()[...].astype(F32)
        o_out.flush()
        for out, ref, at, off in ((q_out, qk, 0, 0), (k_out, qk, width, 0), (v_out, vo, 0, two)):
            total = ref[at : at + width, :] + add[off + at : off + at + width, :].astype(F32)
            out.buf[...] = jnp.transpose(total)
            out.flush()

    return call(
        body,
        ids,
        [(qk_total, 1, 0), (vo_total, 1, 0), given(got)] + [given(o) for o in outs_got],
        [((chunk, width), F32, 1)] * 3 + [((width, chunk), F32, 1)],
        name="finish_attention",
    )


def per_device(
    tokens,
    dealing,
    seq_ids,
    first_values,
    out_grad,
    norm1_gain,
    norm2_gain,
    w_query,
    w_key,
    w_value,
    w_out,
    w_gate,
    w_up,
    w_down,
):
    n_dp = lax.axis_size("dp")
    count, width = tokens.shape
    dim = norm1_gain.shape[0]
    per = count // n_dp
    t = lax.axis_index("tensor")
    d = lax.axis_index("dp")
    ids = jnp.stack([t, d]).astype(jnp.int32)
    gate_t, up_t = w_gate.T, w_up.T

    def exchange(packed):
        return lax.all_to_all(packed, "dp", split_axis=0, concat_axis=0, tiled=True)

    deal_row = dealing.reshape(1, count)
    sent, pos8 = pack_tokens(ids, deal_row, tokens, n_dp)
    arrived = exchange(sent)
    grad_far = flip_tensor(tie(out_grad, sent), 2)
    pos8 = tie(pos8, sent)
    (first_sent,) = sort_rows(ids, pos8, [(first_values, 1)], "pack_rows")
    first_sent = first_sent.reshape(n_dp, per, width)

    start = jnp.sum(seq_ids[None, :] < seq_ids[:, None], axis=1, dtype=jnp.int32)
    offset = (jnp.arange(count, dtype=jnp.int32) - start).astype(F32)
    half = HEAD_DIM // 2
    freqs = THETA ** (-jnp.arange(half, dtype=F32) / half)
    angles = offset[:, None] * jnp.tile(freqs, width // HEAD_DIM)[None, :]
    cos = jnp.cos(angles)
    sin = jnp.sin(angles)
    start_row = start.reshape(1, count)
    gain1 = norm1_gain.reshape(1, dim)
    gain2 = norm2_gain.reshape(1, dim)

    arrived = tie(arrived, first_sent, cos, sin, start_row, grad_far, gain1, gain2)
    slots = (
        arrived[:, per, :per].astype(F32) * 32.0 + arrived[:, per + 1, :per].astype(F32)
    ).astype(jnp.int32)
    slot_row = slots.reshape(1, count)
    grad_near = tie(out_grad, slot_row)
    (grad_sent,) = sort_rows(ids, pos8, [(grad_near, 1), given(grad_far)], "pack_rows")
    grad_sent = grad_sent.reshape(n_dp, per, 2 * width)
    pieces = gather_pieces(arrived, grad_sent)
    firsts = exchange(tie(first_sent, pieces[1]))
    near = exchange(tie(grad_sent, firsts, pieces[2]))
    w_pieces = gather_pieces(tie(w_out, pieces[2]))

    x, normed1, qkv, attended, lse, w_qkv = qkv_attention(
        ids, tie(slot_row, grad_sent), pieces, firsts, cos, sin, gain1, w_query, w_key, w_value,
        start_row,
    )
    near = tie(near, attended).reshape(count, 2 * width)
    near, *early = sort_rows(
        ids, slot_row, [given(near)], "sort_rows", ahead=(gate_t, up_t, w_down, x)
    )
    far = flip_tensor(near, 1)
    o_pieces = gather_pieces(attended, near)
    x1, normed2, fg, fu, hidden, yk0, yk2, ysend = feed_forward(
        ids, early[3], o_pieces, w_pieces, gain2, *early[:3]
    )
    fast = n_dp == 8
    y_got = flip_tensor(ysend, 1)
    early, sums = (), []
    if fast:
        da_send, da_keep, db_send, db_keep = down_grads(ids, hidden, near, far)
        early = (flip_dp(da_send, 1), flip_dp(db_send, 2))
        sums = [(da_keep, early[0]), (db_keep, early[1])]
        yk2 = tie(yk2, da_keep)
    y_mid = middle(yk2, y_got)
    y_far = flip_tensor(y_mid, 2)
    dgate, dup, ak0, ak2, asend, dk0, dk2, dsend, gg2 = feed_backward(
        ids, tie(x1, y_mid), near, far, fg, fu, w_pieces, gain2, gate_t, up_t, w_down
    )
    a_got = flip_tensor(tie(asend, y_far, *early), 1)
    y_sent, *down_sums = return_rows(
        ids,
        slot_row,
        [(tie(yk0, ak0), 1), (y_got, 1, 0), given(y_far)],
        "return_rows",
        sums,
    )
    a_mid = middle(tie(ak2, y_sent), a_got)
    a_far = flip_tensor(a_mid, 2)
    y_back = exchange(tie(y_sent, a_mid).reshape(n_dp, per, width)).reshape(count, width)
    d_got = flip_tensor(tie(dsend, a_mid), 1)
    early = ()
    held = (qkv, attended, cos, sin, w_qkv, x)
    if fast:
        da_send, da_total, db_send, db_total = down_sums
        da_got = flip_dp(tie(da_send, a_mid), 2)
        db_got = flip_dp(tie(db_send, a_mid), 1)
        dgate, dup = tie((dgate, dup), a_mid)
        gate_send, gate_keep, up_send, up_keep, down_send, down_sum, d_mid, *held = mlp_grads(
            ids, normed2, dgate, dup, [(da_total, da_got), (db_total, db_got)],
            [given(dk2), given(d_got, 1)], held,
        )
        a_far = tie(a_far, gate_keep)
        gate_got = flip_dp(gate_send, 1)
        up_got = flip_dp(up_send, 2)
        down_got = flip_dp(down_send, 4)
        early = (gate_got, up_got, down_got)
    else:
        d_mid = middle(dk2, d_got)
    a_far = tie(a_far, d_mid)
    d_far = flip_tensor(tie(d_mid, a_far), 2)
    dvp, dqkv, ek0, ek2, esend = attention_backward(
        ids, *held[:2], lse, [(ak0, 1), given(a_got, 0), (a_far, 1)], start_row, *held[2:4],
        held[5], gain1, held[4], gg2,
    )
    e_got = flip_tensor(tie(esend, d_far, y_back, *early), 1)
    if fast:
        gate_send, gate_total, up_send, up_total, *held = add_pairs(
            ids, [(tie(gate_keep, ek2), gate_got), (up_keep, up_got)], "add_pairs",
            (normed1, *o_pieces, dk0, d_far),
        )
        ek2 = tie(ek2, gate_send)
    e_mid = middle(ek2, e_got)
    e_far = flip_tensor(e_mid, 2)
    if fast:
        gate_got = flip_dp(tie(gate_send, e_mid), 2)
        up_got = flip_dp(tie(up_send, e_mid), 1)
        qk_send, qk_keep, vo_send, vo_keep, *held = attention_grads(
            ids, held[0], tie(dqkv, e_mid), held[1:5],
            [given(held[5]), (d_got, 1, 0), given(held[6])], (ek0, dvp, dk0, d_far),
        )
        ek0, dvp, dk0, d_far = held
        qk_got = flip_dp(qk_send, 1)
        vo_got = flip_dp(vo_send, 2)

        def plus(keep, got, *after):
            return keep.astype(F32) + tie(got, *after).astype(F32)

        gate_total = plus(gate_total, gate_got, qk_keep)
        up_total = plus(up_total, up_got, qk_keep)
        mlp_send = jnp.concatenate([gate_total[1], up_total[1]], axis=0).astype(BF)
        mlp_keep = jnp.concatenate([gate_total[0], up_total[0]], axis=0)
        e_far = tie(e_far, mlp_send)
        mlp_got = flip_dp(mlp_send, 4)
    i_sent = pack_grads(
        ids, slot_row, [given(ek0), (e_got, 1, 0), given(e_far)],
        [given(dk0), (d_got, 1, 0), given(d_far)], dvp, n_dp,
    )
    i_back = exchange(i_sent)
    (output,) = restore_rows(ids, pos8, [tie(y_back, i_sent)], "restore_rows")
    input_grad, first_grad, gain_rows = unpack_grads(ids, pos8, i_back)
    if fast:
        units = w_down.shape[0]
        mlp_total = plus(mlp_keep, mlp_got, output)
        qk_total = plus(qk_keep, qk_got, output)
        vo_total = plus(vo_keep, vo_got, output)
        qk_total = plus(qk_total[0], flip_dp(qk_total[1].astype(BF), 2))
        vo_total = plus(vo_total[0], flip_dp(vo_total[1].astype(BF), 1))
        vo_low = vo_total[:, width:].astype(BF)
        outs_got = [
            lax.ppermute(
                vo_low[b],
                ("dp", "tensor"),
                [
                    ((2 * z + y) * 4 + r, (2 * r + y) * 4 + (r ^ z ^ (2 * b)))
                    for z in range(4)
                    for y in range(2)
                    for r in range(4)
                ],
            )
            for b in range(2)
        ]
        att_send = jnp.concatenate([qk_total[1], vo_total[1, :width]], axis=0).astype(BF)
        att_got = flip_dp(att_send, 4)
        gw_q, gw_k, gw_v, gw_out = finish_attention(
            ids, qk_total, vo_total, tie(att_got, input_grad), outs_got
        )
        gw_down = plus(down_sum, down_got, i_sent)
        gw_gate, gw_up = mlp_total[:units].T, mlp_total[units:].T
    else:

        def scattered(left, right, dim_):
            full = jnp.einsum("ta,tb->ab", left, right, preferred_element_type=F32)
            return lax.psum_scatter(full, "dp", scatter_dimension=dim_, tiled=True)

        def natural(parts):
            full = jnp.zeros((count, dim), BF)
            for flip, part in enumerate(parts):
                full = lax.dynamic_update_slice(full, part, (0, (t ^ flip) * width))
            return full

        dy = natural((near[:, :width], far[:, :width], near[:, width:], far[:, width:]))
        dx1 = (dk0 + d_got[0].astype(F32) + d_far.astype(F32)).astype(BF)
        dx1 = lax.all_gather(dx1, "tensor", axis=1, tiled=True)
        gw_gate = scattered(normed2, dgate, 0)
        gw_up = scattered(normed2, dup, 0)
        gw_down = scattered(hidden, dy, 1)
        gw_q, gw_k, gw_v = [scattered(normed1, p, 0) for p in jnp.split(dqkv, 3, axis=1)]
        gw_out = scattered(attended, dx1, 1)

    return (
        output,
        input_grad,
        first_grad,
        gain_rows[0:1],
        gain_rows[1:2],
        gw_q,
        gw_k,
        gw_v,
        gw_out,
        gw_gate,
        gw_up,
        gw_down,
    )


def solution(mesh):
    in_specs = (
        P("dp", "tensor"),
        P("dp"),
        P("dp"),
        P("dp", "tensor"),
        P("dp", "tensor"),
        P(),
        P(),
        P(None, "tensor"),
        P(None, "tensor"),
        P(None, "tensor"),
        P("tensor", None),
        P(None, "tensor"),
        P(None, "tensor"),
        P("tensor", None),
    )
    out_specs = (
        P("dp", "tensor"),
        P("dp", "tensor"),
        P("dp", "tensor"),
        P("tensor", "dp"),
        P("tensor", "dp"),
        P("dp", "tensor"),
        P("dp", "tensor"),
        P("dp", "tensor"),
        P("tensor", "dp"),
        P("dp", "tensor"),
        P("dp", "tensor"),
        P("tensor", "dp"),
    )
    return jax.shard_map(
        per_device, mesh=mesh, in_specs=in_specs, out_specs=out_specs, check_vma=False
    )
```
